128 devices in a mesh: side: 2 (over core), dev: 64 (over y, z, x).
Axes of the slice: x: 4, y: 4, z: 4, core: 2. Of those that a mesh axis runs over, the one named last changes fastest.
Arguments:
- queries: bfloat16 [1024, 64, 576], P('dev'), may hold values from -18 to 18
- latent_cache: bfloat16 [1024, 768, 576], P('dev', 'side'), may hold values from -18 to 18
- lengths: int32 [1024], P('dev'), may hold values from 64 to 768, as said below
- value_lift: bfloat16 [64, 512, 128], P('side'), may hold values from -0.25 to 0.25
- output_map: bfloat16 [8192, 7168], P('side', 'dev'), may hold values from -0.5 to 0.5
- residual: bfloat16 [1024, 7168], P(('side', 'dev')), may hold values from -6 to 6
- norm_gain: bfloat16 [7168], replicated, may hold values from 0.099609375 to 1.8984375
- expert_ids: int32 [1024, 8], P(('side', 'dev')), may hold values from 0 to 31, all different within a row; in each aligned block of 8 rows (0 to 7, 8 to 15, ...) at most 4 rows name the same one
- gate_values: float32 [1024, 8], P(('side', 'dev')), may hold values from 0.1 to 0.8
- expert_in: bfloat16 [64, 7168, 2, 512], P('dev', None, None, 'side'), may hold values from -0.0625 to 0.0625
- expert_down: bfloat16 [64, 512, 7168], P('dev', 'side'), may hold values from -0.1875 to 0.1875
Outputs:
- layer_out: bfloat16 [1024, 7168], P(('side', 'dev'))
The draws below stay inside these ranges and needn't reach their ends.
Inputs may be any that keep to these rules, and one draw needn't show every extreme that they name: `lengths`: request 0 has all 768 slots live. `expert_ids`: within the rows of one device (aligned blocks of 8 rows) no expert is chosen by more than 4 rows, and some expert is chosen by exactly 4 rows in some blocks.
All inputs are finite; a program needn't handle non-finite values.
Results may differ from the reference program's by a relative error of at most 0.02.
Values may be sent and summed in bfloat16 or wider, within the bound.
A program may use at most 128 MiB of HBM per device.

```python
import math
import jax
import jax.numpy as jnp
import numpy as np
from jax import lax

D = 7168
H = 64
LAT = 512
ROPE = 64
VH = 128
QKD = 192
FFW = 1024
TOP = 8
LEN = 768
REQS = 1024
TOK_DEV = 8
EXPERTS = 32
CAP = 4


def draw_queries(key, part):
    values = jax.random.normal(jax.random.fold_in(key, 1), (REQS, H, LAT + ROPE), jnp.float32)
    return jnp.clip(values, -18.0, 18.0).astype(jnp.bfloat16)


def draw_latent_cache(key, part):
    values = jax.random.normal(jax.random.fold_in(key, 2), (REQS, LEN, LAT + ROPE), jnp.float32)
    return jnp.clip(values, -18.0, 18.0).astype(jnp.bfloat16)


def draw_lengths(key, part):
    lowest = max(6, LEN // 12)
    drawn = jax.random.randint(jax.random.fold_in(key, 3), (REQS,), lowest, LEN + 1, dtype=jnp.int32)
    return drawn.at[0].set(LEN)


def levels(own_key, extent, shards, smallest, largest):
    loudness = 1.0
    for axis_at, shards_of in shards:
        heights = jax.random.uniform(jax.random.fold_in(jax.random.fold_in(own_key, 6), axis_at), (shards_of,), jnp.float32, smallest / len(shards), largest / len(shards))
        loudness = loudness * jnp.repeat(jnp.exp(heights), extent[axis_at] // shards_of).reshape((-1,) + (1,) * (len(extent) - 1 - axis_at))
    return loudness


def assign_block(stream_key, own, number, rows, count, top, reach, lean):
    order = jax.random.permutation(stream_key, count)
    heavy_load, ordinary = shares(count, rows * top, reach, lean, True), shares(count, rows * top, reach, lean, False)
    places = jnp.arange(count)

    def named(tallies, rotation):
        used = int((tallies > 0).sum())
        fixed = max(1, used // 4)
        passed = fixed + (places - fixed + rotation * (used - fixed)) % max(1, count - fixed)
        return jnp.zeros((count,), jnp.int32).at[order[jnp.where(places < fixed, places, passed)]].set(jnp.asarray(tallies, jnp.int32))

    tallies = jnp.where(number % 4 == 0, named(heavy_load, number // 4), named(ordinary, number - number // 4 - 1))
    mixed = jax.random.permutation(jax.random.fold_in(own, 3), count)
    donor, receiver = mixed[0:count // 2 * 2:2], mixed[1:count // 2 * 2:2]
    room = jnp.minimum(tallies[donor] - 1, reach - tallies[receiver]) // 2
    room = jnp.where((donor == order[0]) | (receiver == order[0]) | (tallies[receiver] == 0), 0, jnp.maximum(room, 0))
    passed = jax.random.randint(jax.random.fold_in(own, 4), (count // 2,), 0, 1 << 20) % (room + 1)
    tallies = tallies.at[donor].add(-passed).at[receiver].add(passed)
    labels = jnp.searchsorted(jnp.cumsum(tallies), jnp.arange(rows * top), side="right").astype(jnp.int32)
    table = labels.reshape(top, rows).T
    table = table[jax.random.permutation(jax.random.fold_in(own, 1), rows)]
    rotation = jax.random.randint(jax.random.fold_in(own, 2), (rows, 1), 0, top)
    return jnp.take_along_axis(table, (jnp.arange(top)[None, :] + rotation) % top, axis=1)


def shares(number_of, total, bound, lean, full):
    loads = [(1 << 20) // math.isqrt(grade ** lean) + 1 for grade in range(1, number_of + 1)]
    largest = bound if full else min(bound, max(-(-total // number_of), total * loads[0] // sum(loads)))
    least = 1 if total - largest >= number_of - 1 else 0
    holding, surplus = [largest] + [least] * (number_of - 1), total - largest - least * (number_of - 1)
    while surplus > 0:
        candidates = [i for i in range(1, number_of) if holding[i] < largest] or [i for i in range(1, number_of) if holding[i] < bound]
        whole, left = sum([loads[i] for i in candidates]), surplus
        for i in candidates:
            addition = min(bound - holding[i], max(1, left * loads[i] // whole), surplus)
            holding[i] = holding[i] + addition
            surplus = surplus - addition
    return np.array(holding)


def gaussian(stream_key, dims, spread, reach, cuts=(), kind=jnp.bfloat16):
    factor_of = levels(stream_key, dims, cuts, -0.22, 0.18) if cuts else 1.0
    values = jax.random.normal(stream_key, dims, jnp.float32) * spread * factor_of
    return jnp.minimum(jnp.maximum(values, -reach), reach).astype(kind)


def setup_inputs(seed: int = 0) -> dict:
    splits = jax.random.split(jax.random.key(seed), 12)
    queries = draw_queries(jax.random.fold_in(splits[11], 71), 0)
    latent_cache = draw_latent_cache(jax.random.fold_in(splits[11], 71), 0)
    lengths = draw_lengths(jax.random.fold_in(splits[11], 71), 0)
    value_lift = gaussian(splits[3], (H, LAT, VH), LAT ** -0.5, 0.25, ((0, 2),))
    output_map = gaussian(splits[4], (H * VH, D), (H * 2) ** -0.5, 0.5, ((0, 2), (1, 64)))
    residual = gaussian(splits[5], (REQS, D), 1.0, 6.0, ((0, 128),))
    norm_gain = jnp.clip(1.0 + 0.18 * jax.random.normal(splits[6], (D,), jnp.float32), 0.099609375, 1.8984375).astype(jnp.bfloat16)
    expert_ids_keys = jax.random.split(jax.random.fold_in(splits[7], 1), REQS // TOK_DEV)
    expert_ids_turns = jax.random.permutation(jax.random.fold_in(splits[7], 3), REQS // TOK_DEV)
    expert_ids = jax.vmap(lambda own, number: assign_block(jax.random.fold_in(splits[7], 2), own, number, TOK_DEV, EXPERTS, TOP, CAP, 2))(expert_ids_keys, expert_ids_turns).reshape((REQS, TOP))
    gate_values = jnp.clip(jnp.exp(math.log(0.8) - 2.0794415 * jax.random.uniform(splits[8], (REQS, TOP), jnp.float32) ** levels(splits[8], (REQS, TOP), ((0, 128),), -0.2, 0.2)), 0.1, 0.8)
    expert_in = gaussian(splits[9], (2 * EXPERTS, D, 2, FFW // 2), D ** -0.5, 0.0625, ((0, 64), (3, 2)))
    expert_down = gaussian(splits[10], (2 * EXPERTS, FFW // 2, D), FFW ** -0.5, 0.1875, ((0, 64), (1, 2)))
    return {"queries": queries, "latent_cache": latent_cache, "lengths": lengths, "value_lift": value_lift, "output_map": output_map, "residual": residual, "norm_gain": norm_gain, "expert_ids": expert_ids, "gate_values": gate_values, "expert_in": expert_in, "expert_down": expert_down}


def attend(block):
    query_block, cache_block, length_block = block
    score_scale = QKD ** (-0.5)
    scores = jnp.einsum('rhc,rpc->rhp', query_block.astype(jnp.float32), cache_block.astype(jnp.float32)) * score_scale
    positions = jnp.arange(LEN, dtype=jnp.int32)
    usable = (positions[None, :] < length_block[:, None])[:, None, :]
    masked = jnp.where(usable, scores, -1e+30)
    row_top = lax.optimization_barrier(jnp.max(masked, axis=2, keepdims=True))
    raised = jnp.where(usable, jnp.exp(masked - row_top), 0.0)
    row_total = lax.optimization_barrier(jnp.sum(raised, axis=2))
    probabilities = lax.optimization_barrier(raised.astype(jnp.bfloat16)).astype(jnp.float32)
    latent_sum = jnp.einsum('rhp,rpc->rhc', probabilities, cache_block[:, :, :LAT].astype(jnp.float32))
    return (latent_sum / row_total[:, :, None]).astype(jnp.bfloat16)

def expert_apply(inputs):
    rows_in, gate_up, down_rows = inputs
    wide_rows = rows_in.astype(jnp.float32)
    gate_part = jnp.einsum('rd,jdh->rjh', wide_rows, gate_up[:, :, 0, :].astype(jnp.float32))
    up_part = jnp.einsum('rd,jdh->rjh', wide_rows, gate_up[:, :, 1, :].astype(jnp.float32))
    activated = (jax.nn.silu(gate_part) * up_part).astype(jnp.bfloat16)
    return jnp.einsum('rjh,jhd->rd', activated.astype(jnp.float32), down_rows.astype(jnp.float32)).astype(jnp.bfloat16)

def reference(queries, latent_cache, lengths, value_lift, output_map, residual, norm_gain, expert_ids, gate_values, expert_in, expert_down):
    blocks = REQS // 8
    latent_out = lax.map(attend, (queries.reshape(blocks, 8, H, LAT + ROPE), latent_cache.reshape(blocks, 8, LEN, LAT + ROPE), lengths.reshape(blocks, 8)))
    latent_out = latent_out.reshape(REQS, H, LAT)
    head_values = jnp.einsum('rhc,hcv->rhv', latent_out.astype(jnp.float32), value_lift.astype(jnp.float32))
    head_values = head_values.astype(jnp.bfloat16).reshape(REQS, H * VH)
    attention = jnp.dot(head_values, output_map, preferred_element_type=jnp.float32)
    hidden = (residual.astype(jnp.float32) + attention).astype(jnp.bfloat16)
    hidden_wide = hidden.astype(jnp.float32)
    normed = hidden_wide * lax.rsqrt(lax.optimization_barrier(jnp.mean(hidden_wide * hidden_wide, axis=1, keepdims=True)) + 1e-06)
    normed = (normed * norm_gain.astype(jnp.float32)[None, :]).astype(jnp.bfloat16)
    source_count = REQS // TOK_DEV
    pair_ids = expert_ids.reshape(source_count, TOK_DEV * TOP)
    expert_hits = (pair_ids[:, :, None] == jnp.arange(EXPERTS, dtype=jnp.int32)[None, None, :]).astype(jnp.int32)
    before = jnp.cumsum(expert_hits, axis=1) - expert_hits
    slot_index = lax.optimization_barrier(jnp.sum(before * expert_hits, axis=2)).astype(jnp.int32)
    token_of = jnp.repeat(jnp.arange(TOK_DEV, dtype=jnp.int32), TOP)
    pair_rows = normed.reshape(source_count, TOK_DEV, D)[:, token_of, :]
    source_index = jnp.broadcast_to(jnp.arange(source_count, dtype=jnp.int32)[:, None], pair_ids.shape)
    sectioning = jnp.zeros((EXPERTS, source_count, CAP, D), jnp.bfloat16)
    sectioning = sectioning.at[pair_ids, source_index, slot_index].set(pair_rows)
    expert_out = lax.map(expert_apply, (sectioning.reshape(EXPERTS, source_count * CAP, D), expert_in.reshape(EXPERTS, 2, D, 2, FFW // 2), expert_down.reshape(EXPERTS, 2, FFW // 2, D)))
    expert_out = expert_out.reshape(EXPERTS, source_count, CAP, D)
    pair_out = expert_out[pair_ids, source_index, slot_index].astype(jnp.float32)
    weighted = pair_out * gate_values.reshape(source_count, TOK_DEV * TOP)[:, :, None]
    routed_sum = lax.optimization_barrier(jnp.sum(weighted.reshape(REQS, TOP, D), axis=1))
    return (hidden.astype(jnp.float32) + routed_sum).astype(jnp.bfloat16)
```

```python
import jax
import jax.numpy as jnp
from jax import lax
from jax.sharding import PartitionSpec as P

QKD = 192


def on_device(
    queries,
    latent_cache,
    lengths,
    value_lift,
    output_map,
    residual,
    norm_gain,
    expert_ids,
    gate_values,
    expert_in,
    expert_down,
):
    request_count = queries.shape[0]
    latent_width = value_lift.shape[1]
    half_heads = value_lift.shape[0]
    value_width = value_lift.shape[2]
    half_slots = latent_cache.shape[1]
    model_width = residual.shape[1]
    side_index = lax.axis_index("side")
    score_scale = QKD ** (-0.5)
    scores = (
        jnp.einsum("rhc,rpc->rhp", queries, latent_cache, preferred_element_type=jnp.float32)
        * score_scale
    )
    positions = side_index * half_slots + jnp.arange(half_slots, dtype=jnp.int32)
    usable = (positions[None, :] < lengths[:, None])[:, None, :]
    masked = jnp.where(usable, scores, -1e30)
    row_top = lax.pmax(jnp.max(masked, axis=2), "side")
    raised = jnp.where(usable, jnp.exp(masked - row_top[:, :, None]), 0.0)
    local_total = jnp.sum(raised, axis=2)
    probabilities = raised.astype(jnp.bfloat16)
    local_latent = jnp.einsum(
        "rhp,rpc->rhc",
        probabilities,
        latent_cache[:, :, :latent_width],
        preferred_element_type=jnp.float32,
    )
    swap = [(0, 1), (1, 0)]
    other_index = 1 - side_index
    own_latent = lax.dynamic_slice_in_dim(local_latent, side_index * half_heads, half_heads, 1)
    own_total = lax.dynamic_slice_in_dim(local_total, side_index * half_heads, half_heads, 1)
    sent_latent = lax.dynamic_slice_in_dim(local_latent, other_index * half_heads, half_heads, 1)
    sent_total = lax.dynamic_slice_in_dim(local_total, other_index * half_heads, half_heads, 1)
    got_latent, got_total = lax.ppermute((sent_latent, sent_total), "side", swap)
    row_total = own_total + got_total
    latent_sum = own_latent + got_latent
    own_heads = (latent_sum / row_total[:, :, None]).astype(jnp.bfloat16)
    head_values = jnp.einsum(
        "rhc,hcv->rhv", own_heads, value_lift, preferred_element_type=jnp.float32
    )
    head_values = head_values.astype(jnp.bfloat16).reshape(request_count, half_heads * value_width)
    partial_columns = jnp.dot(
        lax.all_gather(head_values, "dev", axis=0, tiled=True),
        output_map,
        preferred_element_type=jnp.float32,
    )
    summed_columns = lax.psum_scatter(
        partial_columns.astype(jnp.bfloat16), "side", scatter_dimension=0, tiled=True
    ).astype(jnp.float32)
    attention = lax.all_to_all(summed_columns, "dev", split_axis=0, concat_axis=1, tiled=True)
    hidden = (residual.astype(jnp.float32) + attention).astype(jnp.bfloat16)
    hidden_wide = hidden.astype(jnp.float32)
    normed = hidden_wide * lax.rsqrt(
        jnp.mean(hidden_wide * hidden_wide, axis=1, keepdims=True) + 1e-06
    )
    normed = (normed * norm_gain.astype(jnp.float32)[None, :]).astype(jnp.bfloat16)
    token_count = expert_ids.shape[0]
    route_count = expert_ids.shape[1]
    experts = lax.axis_size("dev") // 2
    capacity = max(4, token_count * route_count // experts)
    flat_ids = expert_ids.reshape(-1)
    expert_hits = (flat_ids[:, None] == jnp.arange(experts, dtype=jnp.int32)[None, :]).astype(
        jnp.int32
    )
    before = jnp.cumsum(expert_hits, axis=0) - expert_hits
    slot_index = jnp.sum(before * expert_hits, axis=1).reshape(token_count, route_count)
    slot_code = expert_ids * capacity + slot_index
    slot_table = jnp.arange(experts * capacity, dtype=jnp.int32)
    slot_match = slot_code[None, :, :] == slot_table[:, None, None]
    dispatch_matrix = jnp.any(slot_match, axis=2).astype(jnp.bfloat16)
    combine_matrix = jnp.sum(jnp.where(slot_match, gate_values[None, :, :], 0.0), axis=2).T
    outgoing = jnp.dot(dispatch_matrix, normed, preferred_element_type=jnp.float32).astype(
        jnp.bfloat16
    )
    outgoing = outgoing.reshape(experts, capacity, model_width)
    quarter_width = expert_in.shape[3]
    gate_up_local = expert_in.reshape(model_width, 2 * quarter_width)
    down_local = expert_down[0]
    chips = lax.axis_size("dev")
    spread = jnp.broadcast_to(outgoing[:, None], (experts, chips // experts, capacity, model_width))
    spread = spread.reshape(chips, capacity, model_width)
    arrivals = lax.all_to_all(spread, "dev", split_axis=0, concat_axis=0, tiled=True)
    partner_rows = lax.ppermute(arrivals, "side", swap)
    flat_rows = jnp.concatenate([arrivals, partner_rows], axis=0).reshape(-1, model_width)
    gate_up = jnp.dot(flat_rows, gate_up_local, preferred_element_type=jnp.float32)
    activated = (jax.nn.silu(gate_up[:, :quarter_width]) * gate_up[:, quarter_width:]).astype(
        jnp.bfloat16
    )
    partial_out = jnp.dot(activated, down_local, preferred_element_type=jnp.float32)
    half_rows = chips * capacity
    mine_part = partial_out[:half_rows]
    partner_part = partial_out[half_rows:].astype(jnp.bfloat16)
    got_part = lax.ppermute(partner_part, "side", swap)
    summed = (mine_part + got_part.astype(jnp.float32)).astype(jnp.bfloat16)
    returned = lax.all_to_all(
        summed.reshape(chips, capacity, model_width), "dev", split_axis=0, concat_axis=0, tiled=True
    ).astype(jnp.float32)
    expert_out = jnp.sum(
        returned.reshape(experts, chips // experts, capacity, model_width), axis=1
    ).astype(jnp.bfloat16)
    routed_sum = jnp.dot(
        combine_matrix,
        expert_out.reshape(experts * capacity, model_width).astype(jnp.float32),
        precision=lax.Precision.HIGHEST,
    )
    return (hidden.astype(jnp.float32) + routed_sum).astype(jnp.bfloat16)


def solution(mesh):
    in_specs = (
        P("dev", None, None),
        P("dev", "side", None),
        P("dev"),
        P("side", None, None),
        P("side", "dev"),
        P(("side", "dev"), None),
        P(),
        P(("side", "dev"), None),
        P(("side", "dev"), None),
        P("dev", None, None, "side"),
        P("dev", "side", None),
    )
    out_specs = P(("side", "dev"), None)
    return jax.shard_map(
        on_device, mesh=mesh, in_specs=in_specs, out_specs=out_specs, check_vma=False
    )
```

```python
import jax
import jax.numpy as jnp
from jax import lax
from jax.sharding import PartitionSpec as P

QKD = 192


def on_device(
    queries,
    latent_cache,
    lengths,
    value_lift,
    output_map,
    residual,
    norm_gain,
    expert_ids,
    gate_values,
    expert_in,
    expert_down,
):
    request_count = queries.shape[0]
    latent_width = value_lift.shape[1]
    half_heads = value_lift.shape[0]
    value_width = value_lift.shape[2]
    half_slots = latent_cache.shape[1]
    model_width = residual.shape[1]
    side_index = lax.axis_index("side")
    score_scale = QKD ** (-0.5)
    scores = (
        jnp.einsum("rhc,rpc->rhp", queries, latent_cache, preferred_element_type=jnp.float32)
        * score_scale
    )
    positions = side_index * half_slots + jnp.arange(half_slots, dtype=jnp.int32)
    usable = (positions[None, :] < lengths[:, None])[:, None, :]
    masked = jnp.where(usable, scores, -1e30)
    row_top = lax.pmax(jnp.max(masked, axis=2), "side")
    raised = jnp.where(usable, jnp.exp(masked - row_top[:, :, None]), 0.0)
    local_total = jnp.sum(raised, axis=2)
    probabilities = raised.astype(jnp.bfloat16)
    local_latent = jnp.einsum(
        "rhp,rpc->rhc",
        probabilities,
        latent_cache[:, :, :latent_width],
        preferred_element_type=jnp.float32,
    )
    swap = [(0, 1), (1, 0)]
    other_index = 1 - side_index
    own_latent = lax.dynamic_slice_in_dim(local_latent, side_index * half_heads, half_heads, 1)
    own_total = lax.dynamic_slice_in_dim(local_total, side_index * half_heads, half_heads, 1)
    sent_latent = lax.dynamic_slice_in_dim(local_latent, other_index * half_heads, half_heads, 1)
    sent_total = lax.dynamic_slice_in_dim(local_total, other_index * half_heads, half_heads, 1)
    got_latent, got_total = lax.ppermute((sent_latent, sent_total), "side", swap)
    row_total = own_total + got_total
    latent_sum = own_latent + got_latent
    own_heads = (latent_sum / row_total[:, :, None]).astype(jnp.bfloat16)
    head_values = jnp.einsum(
        "rhc,hcv->rhv", own_heads, value_lift, preferred_element_type=jnp.float32
    )
    head_values = head_values.astype(jnp.bfloat16).reshape(request_count, half_heads * value_width)
    gate_up_local = expert_in.reshape(model_width, -1)
    gathered_values, gate_up_local = lax.optimization_barrier(
        (lax.all_gather(head_values, "dev", axis=0, tiled=True), gate_up_local)
    )
    partial_columns = jnp.dot(
        gathered_values,
        output_map,
        preferred_element_type=jnp.float32,
    )
    summed_columns = lax.psum_scatter(
        partial_columns.astype(jnp.bfloat16), "side", scatter_dimension=0, tiled=True
    ).astype(jnp.float32)
    attention = lax.all_to_all(summed_columns, "dev", split_axis=0, concat_axis=1, tiled=True)
    hidden = (residual.astype(jnp.float32) + attention).astype(jnp.bfloat16)
    hidden_wide = hidden.astype(jnp.float32)
    normed = hidden_wide * lax.rsqrt(
        jnp.mean(hidden_wide * hidden_wide, axis=1, keepdims=True) + 1e-06
    )
    normed = (normed * norm_gain.astype(jnp.float32)[None, :]).astype(jnp.bfloat16)
    token_count = expert_ids.shape[0]
    route_count = expert_ids.shape[1]
    experts = lax.axis_size("dev") // 2
    capacity = max(4, token_count * route_count // experts)
    flat_ids = expert_ids.reshape(-1)
    expert_hits = (flat_ids[:, None] == jnp.arange(experts, dtype=jnp.int32)[None, :]).astype(
        jnp.int32
    )
    before = jnp.cumsum(expert_hits, axis=0) - expert_hits
    slot_index = jnp.sum(before * expert_hits, axis=1).reshape(token_count, route_count)
    slot_code = expert_ids * capacity + slot_index
    slot_table = jnp.arange(experts * capacity, dtype=jnp.int32)
    slot_match = slot_code[None, :, :] == slot_table[:, None, None]
    dispatch_matrix = jnp.any(slot_match, axis=2).astype(jnp.bfloat16)
    combine_matrix = jnp.sum(jnp.where(slot_match, gate_values[None, :, :], 0.0), axis=2).T
    dispatch_cube = dispatch_matrix.reshape(experts, capacity, token_count)
    outgoing = jnp.einsum(
        "sct,td->csd", dispatch_cube, normed, preferred_element_type=jnp.float32
    ).astype(jnp.bfloat16)
    quarter_width = expert_in.shape[3]
    down_local = expert_down[0]
    chips = lax.axis_size("dev")
    spread = jnp.broadcast_to(outgoing[:, :, None], (capacity, experts, chips // experts, model_width))
    spread = spread.reshape(capacity, chips, model_width)
    arrivals = lax.all_to_all(spread, "dev", split_axis=1, concat_axis=1, tiled=True)
    partner_rows = lax.ppermute(arrivals, "side", swap)

    def expert_part(rows):
        flat = rows.reshape(capacity * chips, model_width)
        gate_up = jnp.dot(flat, gate_up_local, preferred_element_type=jnp.float32)
        activated = (
            jax.nn.silu(gate_up[:, :quarter_width]) * gate_up[:, quarter_width:]
        ).astype(jnp.bfloat16)
        out = jnp.dot(activated, down_local, preferred_element_type=jnp.float32)
        return out.reshape(capacity, chips, model_width)

    mine_part = expert_part(arrivals)
    partner_part = expert_part(partner_rows).astype(jnp.bfloat16)
    got_part = lax.ppermute(partner_part, "side", swap)
    summed = (mine_part + got_part.astype(jnp.float32)).astype(jnp.bfloat16)
    returned = lax.all_to_all(summed, "dev", split_axis=1, concat_axis=1, tiled=True)
    expert_out = jnp.sum(
        returned.reshape(capacity, experts, chips // experts, model_width).astype(jnp.float32),
        axis=2,
    ).astype(jnp.bfloat16)
    combine_cube = combine_matrix.reshape(token_count, experts, capacity)
    routed_sum = jnp.einsum(
        "tsc,csd->td",
        combine_cube,
        expert_out.astype(jnp.float32),
        precision=lax.Precision.HIGHEST,
    )
    return (hidden.astype(jnp.float32) + routed_sum).astype(jnp.bfloat16)


def solution(mesh):
    in_specs = (
        P("dev", None, None),
        P("dev", "side", None),
        P("dev"),
        P("side", None, None),
        P("side", "dev"),
        P(("side", "dev"), None),
        P(),
        P(("side", "dev"), None),
        P(("side", "dev"), None),
        P("dev", None, None, "side"),
        P("dev", "side", None),
    )
    out_specs = P(("side", "dev"), None)
    return jax.shard_map(
        on_device, mesh=mesh, in_specs=in_specs, out_specs=out_specs, check_vma=False
    )
```

```python
import jax
import jax.numpy as jnp
from jax import lax
from jax.sharding import PartitionSpec as P

QKD = 192

import functools

from jax.experimental import pallas as pl
from jax.experimental.pallas import tpu as pltpu

MESH_ID = pl.DeviceIdType.MESH
ORDERS = ((2, 0, 1), (0, 1, 2), (1, 2, 0))


def _gather_kernel(sizes, col_cuts, slots, block_ref, out_ref, own_sem, send_sems, recv_sems):
    side = lax.axis_index("side")
    me = lax.axis_index("dev")
    count_y, count_z, count_x = sizes
    mine = (me // (count_z * count_x), (me // count_x) % count_z, me % count_x)

    def chip(coords):
        return (coords[0] * count_z + coords[1]) * count_x + coords[2]

    def shifted(base, axis, offset):
        coords = list(base)
        coords[axis] = (coords[axis] + offset) % sizes[axis]
        return tuple(coords)

    barrier = pltpu.get_barrier_semaphore()
    peers = 0
    for axis in range(3):
        for offset in range(1, sizes[axis]):
            pl.semaphore_signal(
                barrier, 1, device_id=(side, chip(shifted(mine, axis, offset))), device_id_type=MESH_ID
            )
            peers += 1
    pl.semaphore_wait(barrier, peers)

    own = pltpu.make_async_copy(block_ref, out_ref.at[me], own_sem)
    own.start()
    streams = len(col_cuts) - 1
    sent = []

    def sem_at(stream, phase, index):
        return (stream * 3 + phase) * slots + index

    def send(stream, phase, index, block_coords, target):
        cols = pl.ds(col_cuts[stream], col_cuts[stream + 1] - col_cuts[stream])
        at = sem_at(stream, phase, index)
        if phase == 0:
            src = block_ref.at[:, cols]
        else:
            src = out_ref.at[chip(block_coords), :, cols]
        copy = pltpu.make_async_remote_copy(
            src_ref=src,
            dst_ref=out_ref.at[chip(block_coords), :, cols],
            send_sem=send_sems.at[at],
            recv_sem=recv_sems.at[at],
            device_id=(side, chip(target)),
            device_id_type=MESH_ID,
        )
        copy.start()
        sent.append(copy)

    def wait_in(stream, phase, index, block_coords):
        cols = pl.ds(col_cuts[stream], col_cuts[stream + 1] - col_cuts[stream])
        at = sem_at(stream, phase, index)
        pltpu.make_async_remote_copy(
            src_ref=out_ref.at[chip(block_coords), :, cols],
            dst_ref=out_ref.at[chip(block_coords), :, cols],
            send_sem=send_sems.at[at],
            recv_sem=recv_sems.at[at],
            device_id=(side, me),
            device_id_type=MESH_ID,
        ).wait_recv()

    for stream in range(streams):
        a0 = ORDERS[stream][0]
        n0 = sizes[a0]
        for step in range(1, n0):
            send(stream, 0, n0 - step - 1, mine, shifted(mine, a0, step))
    own.wait()
    for stream in range(streams):
        a0, a1, _ = ORDERS[stream]
        n0, n1 = sizes[a0], sizes[a1]
        for d0 in range(1, n0):
            wait_in(stream, 0, d0 - 1, shifted(mine, a0, d0))
        for e0 in range(n0):
            block = shifted(mine, a0, e0)
            for step in range(1, n1):
                send(stream, 1, e0 * (n1 - 1) + (n1 - step) - 1, block, shifted(mine, a1, step))
    for stream in range(streams):
        a0, a1, a2 = ORDERS[stream]
        n0, n1, n2 = sizes[a0], sizes[a1], sizes[a2]
        for e0 in range(n0):
            for d1 in range(1, n1):
                wait_in(stream, 1, e0 * (n1 - 1) + d1 - 1, shifted(shifted(mine, a0, e0), a1, d1))
        for e0 in range(n0):
            for e1 in range(n1):
                block = shifted(shifted(mine, a0, e0), a1, e1)
                for step in range(1, n2):
                    index = (e0 * n1 + e1) * (n2 - 1) + (n2 - step) - 1
                    send(stream, 2, index, block, shifted(mine, a2, step))
    for stream in range(streams):
        a0, a1, a2 = ORDERS[stream]
        n0, n1, n2 = sizes[a0], sizes[a1], sizes[a2]
        for e0 in range(n0):
            for e1 in range(n1):
                for d2 in range(1, n2):
                    block = shifted(shifted(shifted(mine, a0, e0), a1, e1), a2, d2)
                    wait_in(stream, 2, (e0 * n1 + e1) * (n2 - 1) + d2 - 1, block)
    for copy in sent:
        copy.wait_send()


def gather_over_dev(block, chips):
    side_len = round(chips ** (1.0 / 3.0))
    sizes = (side_len, side_len, side_len)
    rows, cols = block.shape
    tiles = cols // 128
    cuts = [0, (tiles + 2) // 3 * 128, (2 * tiles + 2) // 3 * 128, cols]
    slots = side_len * side_len * (side_len - 1)
    gathered = pl.pallas_call(
        functools.partial(_gather_kernel, sizes, cuts, slots),
        out_shape=jax.ShapeDtypeStruct((chips, rows, cols), block.dtype),
        in_specs=[pl.BlockSpec(memory_space=pl.ANY)],
        out_specs=pl.BlockSpec(memory_space=pl.ANY),
        scratch_shapes=[
            pltpu.SemaphoreType.DMA(()),
            pltpu.SemaphoreType.DMA((9 * slots,)),
            pltpu.SemaphoreType.DMA((9 * slots,)),
        ],
        compiler_params=pltpu.CompilerParams(collective_id=0, has_side_effects=True),
    )(block)
    return gathered.reshape(chips * rows, cols)


def on_device(
    queries,
    latent_cache,
    lengths,
    value_lift,
    output_map,
    residual,
    norm_gain,
    expert_ids,
    gate_values,
    expert_in,
    expert_down,
):
    request_count = queries.shape[0]
    latent_width = value_lift.shape[1]
    half_heads = value_lift.shape[0]
    value_width = value_lift.shape[2]
    half_slots = latent_cache.shape[1]
    model_width = residual.shape[1]
    side_index = lax.axis_index("side")
    score_scale = QKD ** (-0.5)
    scores = (
        jnp.einsum("rhc,rpc->rhp", queries, latent_cache, preferred_element_type=jnp.float32)
        * score_scale
    )
    positions = side_index * half_slots + jnp.arange(half_slots, dtype=jnp.int32)
    usable = (positions[None, :] < lengths[:, None])[:, None, :]
    masked = jnp.where(usable, scores, -1e30)
    row_top = lax.pmax(jnp.max(masked, axis=2), "side")
    raised = jnp.where(usable, jnp.exp(masked - row_top[:, :, None]), 0.0)
    local_total = jnp.sum(raised, axis=2)
    probabilities = raised.astype(jnp.bfloat16)
    local_latent = jnp.einsum(
        "rhp,rpc->rhc",
        probabilities,
        latent_cache[:, :, :latent_width],
        preferred_element_type=jnp.float32,
    )
    swap = [(0, 1), (1, 0)]
    other_index = 1 - side_index
    own_latent = lax.dynamic_slice_in_dim(local_latent, side_index * half_heads, half_heads, 1)
    own_total = lax.dynamic_slice_in_dim(local_total, side_index * half_heads, half_heads, 1)
    sent_latent = lax.dynamic_slice_in_dim(local_latent, other_index * half_heads, half_heads, 1)
    sent_total = lax.dynamic_slice_in_dim(local_total, other_index * half_heads, half_heads, 1)
    got_latent, got_total = lax.ppermute((sent_latent, sent_total), "side", swap)
    row_total = own_total + got_total
    latent_sum = own_latent + got_latent
    own_heads = (latent_sum / row_total[:, :, None]).astype(jnp.bfloat16)
    head_values = jnp.einsum(
        "rhc,hcv->rhv", own_heads, value_lift, preferred_element_type=jnp.float32
    )
    head_values = head_values.astype(jnp.bfloat16).reshape(request_count, half_heads * value_width)
    gathered_values = gather_over_dev(head_values, lax.axis_size("dev"))
    partial_columns = jnp.dot(
        gathered_values,
        output_map,
        preferred_element_type=jnp.float32,
    )
    summed_columns = lax.psum_scatter(
        partial_columns.astype(jnp.bfloat16), "side", scatter_dimension=0, tiled=True
    ).astype(jnp.float32)
    attention = lax.all_to_all(summed_columns, "dev", split_axis=0, concat_axis=1, tiled=True)
    gate_up_local = expert_in.reshape(model_width, -1)
    attention, gate_up_local = lax.optimization_barrier((attention, gate_up_local))
    hidden = (residual.astype(jnp.float32) + attention).astype(jnp.bfloat16)
    hidden_wide = hidden.astype(jnp.float32)
    normed = hidden_wide * lax.rsqrt(
        jnp.mean(hidden_wide * hidden_wide, axis=1, keepdims=True) + 1e-06
    )
    normed = (normed * norm_gain.astype(jnp.float32)[None, :]).astype(jnp.bfloat16)
    token_count = expert_ids.shape[0]
    route_count = expert_ids.shape[1]
    experts = lax.axis_size("dev") // 2
    capacity = max(4, token_count * route_count // experts)
    flat_ids = expert_ids.reshape(-1)
    expert_hits = (flat_ids[:, None] == jnp.arange(experts, dtype=jnp.int32)[None, :]).astype(
        jnp.int32
    )
    before = jnp.cumsum(expert_hits, axis=0) - expert_hits
    slot_index = jnp.sum(before * expert_hits, axis=1).reshape(token_count, route_count)
    slot_code = expert_ids * capacity + slot_index
    slot_table = jnp.arange(experts * capacity, dtype=jnp.int32)
    slot_match = slot_code[None, :, :] == slot_table[:, None, None]
    dispatch_matrix = jnp.any(slot_match, axis=2).astype(jnp.bfloat16)
    combine_matrix = jnp.sum(jnp.where(slot_match, gate_values[None, :, :], 0.0), axis=2).T
    dispatch_cube = dispatch_matrix.reshape(experts, capacity, token_count)
    outgoing = jnp.einsum(
        "sct,td->csd", dispatch_cube, normed, preferred_element_type=jnp.float32
    ).astype(jnp.bfloat16)
    quarter_width = expert_in.shape[3]
    down_local = expert_down[0]
    chips = lax.axis_size("dev")
    spread = jnp.broadcast_to(outgoing[:, :, None], (capacity, experts, chips // experts, model_width))
    spread = spread.reshape(capacity, chips, model_width)
    arrivals = lax.all_to_all(spread, "dev", split_axis=1, concat_axis=1, tiled=True)
    partner_rows = lax.ppermute(arrivals, "side", swap)

    def expert_part(rows):
        flat = rows.reshape(capacity * chips, model_width)
        gate_up = jnp.dot(flat, gate_up_local, preferred_element_type=jnp.float32)
        activated = (
            jax.nn.silu(gate_up[:, :quarter_width]) * gate_up[:, quarter_width:]
        ).astype(jnp.bfloat16)
        out = jnp.dot(activated, down_local, preferred_element_type=jnp.float32)
        return out.reshape(capacity, chips, model_width)

    mine_part = expert_part(arrivals)
    partner_part = expert_part(partner_rows).astype(jnp.bfloat16)
    got_part = lax.ppermute(partner_part, "side", swap)
    summed = (mine_part + got_part.astype(jnp.float32)).astype(jnp.bfloat16)
    returned = lax.all_to_all(summed, "dev", split_axis=1, concat_axis=1, tiled=True)
    expert_out = jnp.sum(
        returned.reshape(capacity, experts, chips // experts, model_width).astype(jnp.float32),
        axis=2,
    ).astype(jnp.bfloat16)
    combine_cube = combine_matrix.reshape(token_count, experts, capacity)
    routed_sum = jnp.einsum(
        "tsc,csd->td",
        combine_cube,
        expert_out.astype(jnp.float32),
        precision=lax.Precision.HIGHEST,
    )
    return (hidden.astype(jnp.float32) + routed_sum).astype(jnp.bfloat16)


def solution(mesh):
    in_specs = (
        P("dev", None, None),
        P("dev", "side", None),
        P("dev"),
        P("side", None, None),
        P("side", "dev"),
        P(("side", "dev"), None),
        P(),
        P(("side", "dev"), None),
        P(("side", "dev"), None),
        P("dev", None, None, "side"),
        P("dev", "side", None),
    )
    out_specs = P(("side", "dev"), None)
    return jax.shard_map(
        on_device, mesh=mesh, in_specs=in_specs, out_specs=out_specs, check_vma=False
    )
```

```python
import jax
import jax.numpy as jnp
from jax import lax
from jax.sharding import PartitionSpec as P

QKD = 192

import functools

from jax.experimental import pallas as pl
from jax.experimental.pallas import tpu as pltpu

MESH_ID = pl.DeviceIdType.MESH
ORDERS = ((2, 0, 1), (0, 1, 2), (1, 2, 0))


def _gather_kernel(sizes, col_cuts, slots, block_ref, out_ref, own_sem, send_sems, recv_sems):
    side = lax.axis_index("side")
    me = lax.axis_index("dev")
    count_y, count_z, count_x = sizes
    mine = (me // (count_z * count_x), (me // count_x) % count_z, me % count_x)

    def chip(coords):
        return (coords[0] * count_z + coords[1]) * count_x + coords[2]

    def shifted(base, axis, offset):
        coords = list(base)
        coords[axis] = (coords[axis] + offset) % sizes[axis]
        return tuple(coords)

    barrier = pltpu.get_barrier_semaphore()
    peers = 0
    for axis in range(3):
        for offset in range(1, sizes[axis]):
            pl.semaphore_signal(
                barrier, 1, device_id=(side, chip(shifted(mine, axis, offset))), device_id_type=MESH_ID
            )
            peers += 1
    pl.semaphore_wait(barrier, peers)

    own = pltpu.make_async_copy(block_ref, out_ref.at[me], own_sem)
    own.start()
    streams = len(col_cuts) - 1
    sent = []

    def sem_at(stream, phase, index):
        return (stream * 3 + phase) * slots + index

    def remote(stream, phase, index, block_coords, target):
        cols = pl.ds(col_cuts[stream], col_cuts[stream + 1] - col_cuts[stream])
        at = sem_at(stream, phase, index)
        if phase == 0:
            src = block_ref.at[:, cols]
        else:
            src = out_ref.at[chip(block_coords), :, cols]
        return pltpu.make_async_remote_copy(
            src_ref=src,
            dst_ref=out_ref.at[chip(block_coords), :, cols],
            send_sem=send_sems.at[at],
            recv_sem=recv_sems.at[at],
            device_id=(side, chip(target)),
            device_id_type=MESH_ID,
        )

    def send(stream, phase, index, block_coords, target):
        copy = remote(stream, phase, index, block_coords, target)
        copy.start()
        sent.append(copy)

    def wait_in(stream, phase, index, block_coords):
        remote(stream, phase, index, block_coords, mine).wait_recv()

    for stream in range(streams):
        a0 = ORDERS[stream][0]
        n0 = sizes[a0]
        for step in range(1, n0):
            send(stream, 0, n0 - step - 1, mine, shifted(mine, a0, step))
    own.wait()
    def phase_one_copy(stream, e0, step):
        a0, a1, _ = ORDERS[stream]
        n1 = sizes[a1]
        index = e0 * (n1 - 1) + (n1 - step) - 1
        return remote(stream, 1, index, shifted(mine, a0, e0), shifted(mine, a1, step))

    for stream in range(streams):
        a0, a1, _ = ORDERS[stream]
        n0, n1 = sizes[a0], sizes[a1]
        for d0 in range(1, n0):
            wait_in(stream, 0, d0 - 1, shifted(mine, a0, d0))

        def start_line(e0, carry, stream=stream, n1=n1):
            for step in range(1, n1):
                phase_one_copy(stream, e0, step).start()
            return carry

        lax.fori_loop(0, n0, start_line, 0)

    def plane_block(stream, flat):
        a0, a1, _ = ORDERS[stream]
        n1 = sizes[a1]
        return shifted(shifted(mine, a0, flat // n1), a1, flat % n1)

    def phase_two_copy(stream, flat, step):
        a2 = ORDERS[stream][2]
        n2 = sizes[a2]
        index = flat * (n2 - 1) + (n2 - step) - 1
        return remote(stream, 2, index, plane_block(stream, flat), shifted(mine, a2, step))

    for stream in range(streams):
        a0, a1, a2 = ORDERS[stream]
        n0, n1, n2 = sizes[a0], sizes[a1], sizes[a2]
        for e0 in range(n0):
            for d1 in range(1, n1):
                wait_in(stream, 1, e0 * (n1 - 1) + d1 - 1, shifted(shifted(mine, a0, e0), a1, d1))

        def start_plane(flat, carry, stream=stream, n2=n2):
            for step in range(1, n2):
                phase_two_copy(stream, flat, step).start()
            return carry

        lax.fori_loop(0, n0 * n1, start_plane, 0)
    for stream in range(streams):
        a0, a1, a2 = ORDERS[stream]
        n0, n1, n2 = sizes[a0], sizes[a1], sizes[a2]

        def wait_plane(flat, carry, stream=stream, a2=a2, n2=n2):
            for d2 in range(1, n2):
                index = flat * (n2 - 1) + d2 - 1
                block = shifted(plane_block(stream, flat), a2, d2)
                wait_in(stream, 2, index, block)
            return carry

        lax.fori_loop(0, n0 * n1, wait_plane, 0)
    for copy in sent:
        copy.wait_send()
    for stream in range(streams):
        a0, a1, _ = ORDERS[stream]
        n0, n1 = sizes[a0], sizes[a1]

        def drain_line(e0, carry, stream=stream, n1=n1):
            for step in range(1, n1):
                phase_one_copy(stream, e0, step).wait_send()
            return carry

        lax.fori_loop(0, n0, drain_line, 0)
    for stream in range(streams):
        a0, a1, a2 = ORDERS[stream]
        n0, n1, n2 = sizes[a0], sizes[a1], sizes[a2]

        def drain_plane(flat, carry, stream=stream, n2=n2):
            for step in range(1, n2):
                phase_two_copy(stream, flat, step).wait_send()
            return carry

        lax.fori_loop(0, n0 * n1, drain_plane, 0)


def gather_over_dev(block, chips):
    side_len = round(chips ** (1.0 / 3.0))
    sizes = (side_len, side_len, side_len)
    rows, cols = block.shape
    tiles = cols // 128
    cuts = [0, (tiles + 2) // 3 * 128, (2 * tiles + 2) // 3 * 128, cols]
    slots = side_len * side_len * (side_len - 1)
    gathered = pl.pallas_call(
        functools.partial(_gather_kernel, sizes, cuts, slots),
        out_shape=jax.ShapeDtypeStruct((chips, rows, cols), block.dtype),
        in_specs=[pl.BlockSpec(memory_space=pl.ANY)],
        out_specs=pl.BlockSpec(memory_space=pl.ANY),
        scratch_shapes=[
            pltpu.SemaphoreType.DMA(()),
            pltpu.SemaphoreType.DMA((9 * slots,)),
            pltpu.SemaphoreType.DMA((9 * slots,)),
        ],
        compiler_params=pltpu.CompilerParams(collective_id=0, has_side_effects=True),
    )(block)
    return gathered.reshape(chips * rows, cols)


def on_device(
    queries,
    latent_cache,
    lengths,
    value_lift,
    output_map,
    residual,
    norm_gain,
    expert_ids,
    gate_values,
    expert_in,
    expert_down,
):
    request_count = queries.shape[0]
    latent_width = value_lift.shape[1]
    half_heads = value_lift.shape[0]
    value_width = value_lift.shape[2]
    half_slots = latent_cache.shape[1]
    model_width = residual.shape[1]
    side_index = lax.axis_index("side")
    score_scale = QKD ** (-0.5)
    scores = (
        jnp.einsum("rhc,rpc->rhp", queries, latent_cache, preferred_element_type=jnp.float32)
        * score_scale
    )
    positions = side_index * half_slots + jnp.arange(half_slots, dtype=jnp.int32)
    usable = (positions[None, :] < lengths[:, None])[:, None, :]
    masked = jnp.where(usable, scores, -1e30)
    swap = [(0, 1), (1, 0)]
    local_top = jnp.max(masked, axis=2)
    row_top = jnp.maximum(local_top, lax.ppermute(local_top, "side", swap))
    raised = jnp.where(usable, jnp.exp(masked - row_top[:, :, None]), 0.0)
    local_total = jnp.sum(raised, axis=2)
    probabilities = raised.astype(jnp.bfloat16)
    local_latent = jnp.einsum(
        "rhp,rpc->rhc",
        probabilities,
        latent_cache[:, :, :latent_width],
        preferred_element_type=jnp.float32,
    )
    other_index = 1 - side_index
    own_latent = lax.dynamic_slice_in_dim(local_latent, side_index * half_heads, half_heads, 1)
    own_total = lax.dynamic_slice_in_dim(local_total, side_index * half_heads, half_heads, 1)
    sent_latent = lax.dynamic_slice_in_dim(local_latent, other_index * half_heads, half_heads, 1)
    sent_total = lax.dynamic_slice_in_dim(local_total, other_index * half_heads, half_heads, 1)
    got_latent, got_total = lax.ppermute((sent_latent, sent_total), "side", swap)
    row_total = own_total + got_total
    latent_sum = own_latent + got_latent
    own_heads = (latent_sum / row_total[:, :, None]).astype(jnp.bfloat16)
    head_values = jnp.einsum(
        "rhc,hcv->rhv", own_heads, value_lift, preferred_element_type=jnp.float32
    )
    head_values = head_values.astype(jnp.bfloat16).reshape(request_count, half_heads * value_width)
    gathered_values = gather_over_dev(head_values, lax.axis_size("dev"))
    partial_columns = jnp.dot(
        gathered_values,
        output_map,
        preferred_element_type=jnp.float32,
    )
    half_requests = partial_columns.shape[0] // 2
    kept_columns = lax.dynamic_slice_in_dim(partial_columns, side_index * half_requests, half_requests, 0)
    sent_columns = lax.dynamic_slice_in_dim(partial_columns, other_index * half_requests, half_requests, 0)
    got_columns = lax.ppermute(sent_columns.astype(jnp.bfloat16), "side", swap)
    summed_columns = kept_columns + got_columns.astype(jnp.float32)
    attention = lax.all_to_all(summed_columns, "dev", split_axis=0, concat_axis=1, tiled=True)
    gate_up_local = expert_in.reshape(model_width, -1)
    attention, gate_up_local = lax.optimization_barrier((attention, gate_up_local))
    hidden = (residual.astype(jnp.float32) + attention).astype(jnp.bfloat16)
    hidden_wide = hidden.astype(jnp.float32)
    normed = hidden_wide * lax.rsqrt(
        jnp.mean(hidden_wide * hidden_wide, axis=1, keepdims=True) + 1e-06
    )
    normed = (normed * norm_gain.astype(jnp.float32)[None, :]).astype(jnp.bfloat16)
    token_count = expert_ids.shape[0]
    route_count = expert_ids.shape[1]
    experts = lax.axis_size("dev") // 2
    capacity = max(4, token_count * route_count // experts)
    flat_ids = expert_ids.reshape(-1)
    expert_hits = (flat_ids[:, None] == jnp.arange(experts, dtype=jnp.int32)[None, :]).astype(
        jnp.int32
    )
    before = jnp.cumsum(expert_hits, axis=0) - expert_hits
    slot_index = jnp.sum(before * expert_hits, axis=1).reshape(token_count, route_count)
    slot_code = expert_ids * capacity + slot_index
    slot_table = jnp.arange(experts * capacity, dtype=jnp.int32)
    slot_match = slot_code[None, :, :] == slot_table[:, None, None]
    dispatch_matrix = jnp.any(slot_match, axis=2).astype(jnp.bfloat16)
    combine_matrix = jnp.sum(jnp.where(slot_match, gate_values[None, :, :], 0.0), axis=2).T
    dispatch_cube = dispatch_matrix.reshape(experts, capacity, token_count)
    outgoing = jnp.einsum(
        "sct,td->csd", dispatch_cube, normed, preferred_element_type=jnp.float32
    ).astype(jnp.bfloat16)
    quarter_width = expert_in.shape[3]
    down_local = expert_down[0]
    chips = lax.axis_size("dev")
    spread = jnp.broadcast_to(outgoing[:, :, None], (capacity, experts, chips // experts, model_width))
    spread = spread.reshape(capacity, chips, model_width)
    arrivals = lax.all_to_all(spread, "dev", split_axis=1, concat_axis=1, tiled=True)
    partner_rows = lax.ppermute(arrivals, "side", swap)

    def expert_part(rows):
        flat = rows.reshape(capacity * chips, model_width)
        gate_up = jnp.dot(flat, gate_up_local, preferred_element_type=jnp.float32)
        activated = (
            jax.nn.silu(gate_up[:, :quarter_width]) * gate_up[:, quarter_width:]
        ).astype(jnp.bfloat16)
        out = jnp.dot(activated, down_local, preferred_element_type=jnp.float32)
        return out.reshape(capacity, chips, model_width)

    mine_part = expert_part(arrivals)
    partner_part = expert_part(partner_rows).astype(jnp.bfloat16)
    got_part = lax.ppermute(partner_part, "side", swap)
    summed = (mine_part + got_part.astype(jnp.float32)).astype(jnp.bfloat16)
    returned = lax.all_to_all(summed, "dev", split_axis=1, concat_axis=1, tiled=True)
    expert_out = jnp.sum(
        returned.reshape(capacity, experts, chips // experts, model_width).astype(jnp.float32),
        axis=2,
    ).astype(jnp.bfloat16)
    combine_cube = combine_matrix.reshape(token_count, experts, capacity)
    routed_sum = jnp.einsum(
        "tsc,csd->td",
        combine_cube,
        expert_out.astype(jnp.float32),
        precision=lax.Precision.HIGHEST,
    )
    return (hidden.astype(jnp.float32) + routed_sum).astype(jnp.bfloat16)


def solution(mesh):
    in_specs = (
        P("dev", None, None),
        P("dev", "side", None),
        P("dev"),
        P("side", None, None),
        P("side", "dev"),
        P(("side", "dev"), None),
        P(),
        P(("side", "dev"), None),
        P(("side", "dev"), None),
        P("dev", None, None, "side"),
        P("dev", "side", None),
    )
    out_specs = P(("side", "dev"), None)
    return jax.shard_map(
        on_device, mesh=mesh, in_specs=in_specs, out_specs=out_specs, check_vma=False
    )
```

```python
import jax
import jax.numpy as jnp
from jax import lax
from jax.sharding import PartitionSpec as P

QKD = 192

import functools

from jax.experimental import pallas as pl
from jax.experimental.pallas import tpu as pltpu

MESH_ID = pl.DeviceIdType.MESH
ORDERS = ((2, 0, 1), (0, 1, 2), (1, 2, 0))


def _gather_kernel(sizes, col_cuts, slots, block_ref, out_ref, own_sem, send_sems, recv_sems):
    side = lax.axis_index("side")
    me = lax.axis_index("dev")
    count_y, count_z, count_x = sizes
    mine = (me // (count_z * count_x), (me // count_x) % count_z, me % count_x)

    def chip(coords):
        return (coords[0] * count_z + coords[1]) * count_x + coords[2]

    def shifted(base, axis, offset):
        coords = list(base)
        coords[axis] = (coords[axis] + offset) % sizes[axis]
        return tuple(coords)

    barrier = pltpu.get_barrier_semaphore()
    peers = 0
    for axis in range(3):
        for offset in range(1, sizes[axis]):
            pl.semaphore_signal(
                barrier, 1, device_id=(side, chip(shifted(mine, axis, offset))), device_id_type=MESH_ID
            )
            peers += 1
    pl.semaphore_wait(barrier, peers)

    own = pltpu.make_async_copy(block_ref, out_ref.at[me], own_sem)
    own.start()
    streams = len(col_cuts) - 1
    sent = []

    def sem_at(stream, phase, index):
        return (stream * 3 + phase) * slots + index

    def remote(stream, phase, index, block_coords, target):
        cols = pl.ds(col_cuts[stream], col_cuts[stream + 1] - col_cuts[stream])
        at = sem_at(stream, phase, index)
        if phase == 0:
            src = block_ref.at[:, cols]
        else:
            src = out_ref.at[chip(block_coords), :, cols]
        return pltpu.make_async_remote_copy(
            src_ref=src,
            dst_ref=out_ref.at[chip(block_coords), :, cols],
            send_sem=send_sems.at[at],
            recv_sem=recv_sems.at[at],
            device_id=(side, chip(target)),
            device_id_type=MESH_ID,
        )

    def send(stream, phase, index, block_coords, target):
        copy = remote(stream, phase, index, block_coords, target)
        copy.start()
        sent.append(copy)

    def wait_in(stream, phase, index, block_coords):
        remote(stream, phase, index, block_coords, mine).wait_recv()

    for stream in range(streams):
        a0 = ORDERS[stream][0]
        n0 = sizes[a0]
        for step in range(1, n0):
            send(stream, 0, n0 - step - 1, mine, shifted(mine, a0, step))
    own.wait()
    def phase_one_copy(stream, e0, step):
        a0, a1, _ = ORDERS[stream]
        n1 = sizes[a1]
        index = e0 * (n1 - 1) + (n1 - step) - 1
        return remote(stream, 1, index, shifted(mine, a0, e0), shifted(mine, a1, step))

    for stream in range(streams):
        a0, a1, _ = ORDERS[stream]
        n0, n1 = sizes[a0], sizes[a1]
        for d0 in range(1, n0):
            wait_in(stream, 0, d0 - 1, shifted(mine, a0, d0))

        def start_line(e0, carry, stream=stream, n1=n1):
            for step in range(1, n1):
                phase_one_copy(stream, e0, step).start()
            return carry

        lax.fori_loop(0, n0, start_line, 0)

    def plane_block(stream, flat):
        a0, a1, _ = ORDERS[stream]
        n1 = sizes[a1]
        return shifted(shifted(mine, a0, flat // n1), a1, flat % n1)

    def phase_two_copy(stream, flat, step):
        a2 = ORDERS[stream][2]
        n2 = sizes[a2]
        index = flat * (n2 - 1) + (n2 - step) - 1
        return remote(stream, 2, index, plane_block(stream, flat), shifted(mine, a2, step))

    for stream in range(streams):
        a0, a1, a2 = ORDERS[stream]
        n0, n1, n2 = sizes[a0], sizes[a1], sizes[a2]
        for e0 in range(n0):
            for d1 in range(1, n1):
                wait_in(stream, 1, e0 * (n1 - 1) + d1 - 1, shifted(shifted(mine, a0, e0), a1, d1))

        def start_plane(flat, carry, stream=stream, n2=n2):
            for step in range(1, n2):
                phase_two_copy(stream, flat, step).start()
            return carry

        lax.fori_loop(0, n0 * n1, start_plane, 0)
    for stream in range(streams):
        a0, a1, a2 = ORDERS[stream]
        n0, n1, n2 = sizes[a0], sizes[a1], sizes[a2]

        def wait_plane(flat, carry, stream=stream, a2=a2, n2=n2):
            for d2 in range(1, n2):
                index = flat * (n2 - 1) + d2 - 1
                block = shifted(plane_block(stream, flat), a2, d2)
                wait_in(stream, 2, index, block)
            return carry

        lax.fori_loop(0, n0 * n1, wait_plane, 0)
    for copy in sent:
        copy.wait_send()
    for stream in range(streams):
        a0, a1, _ = ORDERS[stream]
        n0, n1 = sizes[a0], sizes[a1]

        def drain_line(e0, carry, stream=stream, n1=n1):
            for step in range(1, n1):
                phase_one_copy(stream, e0, step).wait_send()
            return carry

        lax.fori_loop(0, n0, drain_line, 0)
    for stream in range(streams):
        a0, a1, a2 = ORDERS[stream]
        n0, n1, n2 = sizes[a0], sizes[a1], sizes[a2]

        def drain_plane(flat, carry, stream=stream, n2=n2):
            for step in range(1, n2):
                phase_two_copy(stream, flat, step).wait_send()
            return carry

        lax.fori_loop(0, n0 * n1, drain_plane, 0)


def gather_over_dev(block, chips):
    side_len = round(chips ** (1.0 / 3.0))
    sizes = (side_len, side_len, side_len)
    rows, cols = block.shape
    tiles = cols // 128
    cuts = [0, (tiles + 2) // 3 * 128, (2 * tiles + 2) // 3 * 128, cols]
    slots = side_len * side_len * (side_len - 1)
    gathered = pl.pallas_call(
        functools.partial(_gather_kernel, sizes, cuts, slots),
        out_shape=jax.ShapeDtypeStruct((chips, rows, cols), block.dtype),
        in_specs=[pl.BlockSpec(memory_space=pl.ANY)],
        out_specs=pl.BlockSpec(memory_space=pl.ANY),
        scratch_shapes=[
            pltpu.SemaphoreType.DMA(()),
            pltpu.SemaphoreType.DMA((9 * slots,)),
            pltpu.SemaphoreType.DMA((9 * slots,)),
        ],
        compiler_params=pltpu.CompilerParams(collective_id=0, has_side_effects=True),
    )(block)
    return gathered.reshape(chips * rows, cols)


def on_device(
    queries,
    latent_cache,
    lengths,
    value_lift,
    output_map,
    residual,
    norm_gain,
    expert_ids,
    gate_values,
    expert_in,
    expert_down,
):
    request_count = queries.shape[0]
    latent_width = value_lift.shape[1]
    half_heads = value_lift.shape[0]
    value_width = value_lift.shape[2]
    half_slots = latent_cache.shape[1]
    model_width = residual.shape[1]
    side_index = lax.axis_index("side")
    score_scale = QKD ** (-0.5)
    scores = (
        jnp.einsum("rhc,rpc->rhp", queries, latent_cache, preferred_element_type=jnp.float32)
        * score_scale
    )
    positions = side_index * half_slots + jnp.arange(half_slots, dtype=jnp.int32)
    usable = (positions[None, :] < lengths[:, None])[:, None, :]
    masked = jnp.where(usable, scores, -1e30)
    swap = [(0, 1), (1, 0)]
    local_top = jnp.max(masked, axis=2)
    row_top = jnp.maximum(local_top, lax.ppermute(local_top, "side", swap))
    raised = jnp.where(usable, jnp.exp(masked - row_top[:, :, None]), 0.0)
    local_total = jnp.sum(raised, axis=2)
    probabilities = raised.astype(jnp.bfloat16)
    local_latent = jnp.einsum(
        "rhp,rpc->rhc",
        probabilities,
        latent_cache[:, :, :latent_width],
        preferred_element_type=jnp.float32,
    )
    other_index = 1 - side_index
    own_latent = lax.dynamic_slice_in_dim(local_latent, side_index * half_heads, half_heads, 1)
    own_total = lax.dynamic_slice_in_dim(local_total, side_index * half_heads, half_heads, 1)
    sent_latent = lax.dynamic_slice_in_dim(local_latent, other_index * half_heads, half_heads, 1)
    sent_total = lax.dynamic_slice_in_dim(local_total, other_index * half_heads, half_heads, 1)
    got_latent, got_total = lax.ppermute((sent_latent, sent_total), "side", swap)
    row_total = own_total + got_total
    latent_sum = own_latent + got_latent
    own_heads = (latent_sum / row_total[:, :, None]).astype(jnp.bfloat16)
    head_values = jnp.einsum(
        "rhc,hcv->rhv", own_heads, value_lift, preferred_element_type=jnp.float32
    )
    head_values = head_values.astype(jnp.bfloat16).reshape(request_count, half_heads * value_width)
    gathered_values = gather_over_dev(head_values, lax.axis_size("dev"))
    partial_columns = jnp.dot(
        gathered_values,
        output_map,
        preferred_element_type=jnp.float32,
    )
    half_requests = partial_columns.shape[0] // 2
    kept_columns = lax.dynamic_slice_in_dim(partial_columns, side_index * half_requests, half_requests, 0)
    sent_columns = lax.dynamic_slice_in_dim(partial_columns, other_index * half_requests, half_requests, 0)
    got_columns = lax.ppermute(sent_columns.astype(jnp.bfloat16), "side", swap)
    summed_columns = kept_columns + got_columns.astype(jnp.float32)
    attention = lax.all_to_all(summed_columns, "dev", split_axis=0, concat_axis=1, tiled=True)
    gate_up_local = expert_in.reshape(model_width, -1)
    attention, gate_up_local = lax.optimization_barrier((attention, gate_up_local))
    hidden = (residual.astype(jnp.float32) + attention).astype(jnp.bfloat16)
    hidden_wide = hidden.astype(jnp.float32)
    normed = hidden_wide * lax.rsqrt(
        jnp.mean(hidden_wide * hidden_wide, axis=1, keepdims=True) + 1e-06
    )
    normed = (normed * norm_gain.astype(jnp.float32)[None, :]).astype(jnp.bfloat16)
    token_count = expert_ids.shape[0]
    route_count = expert_ids.shape[1]
    experts = lax.axis_size("dev") // 2
    capacity = max(4, token_count * route_count // experts)
    flat_ids = expert_ids.reshape(-1)
    expert_hits = (flat_ids[:, None] == jnp.arange(experts, dtype=jnp.int32)[None, :]).astype(
        jnp.int32
    )
    before = jnp.cumsum(expert_hits, axis=0) - expert_hits
    slot_index = jnp.sum(before * expert_hits, axis=1).reshape(token_count, route_count)
    slot_code = expert_ids * capacity + slot_index
    slot_table = jnp.arange(experts * capacity, dtype=jnp.int32)
    slot_match = slot_code[None, :, :] == slot_table[:, None, None]
    dispatch_matrix = jnp.any(slot_match, axis=2).astype(jnp.bfloat16)
    combine_matrix = jnp.sum(jnp.where(slot_match, gate_values[None, :, :], 0.0), axis=2).T
    dispatch_cube = dispatch_matrix.reshape(experts, capacity, token_count)
    outgoing = jnp.einsum(
        "sct,td->csd", dispatch_cube, normed, preferred_element_type=jnp.float32
    ).astype(jnp.bfloat16)
    quarter_width = expert_in.shape[3]
    down_local = expert_down[0]
    chips = lax.axis_size("dev")
    spread = jnp.broadcast_to(outgoing[:, :, None], (capacity, experts, chips // experts, model_width))
    spread = spread.reshape(capacity, chips, model_width)

    def expert_part(rows):
        flat = rows.reshape(-1, model_width)
        gate_up = jnp.dot(flat, gate_up_local, preferred_element_type=jnp.float32)
        activated = (
            jax.nn.silu(gate_up[:, :quarter_width]) * gate_up[:, quarter_width:]
        ).astype(jnp.bfloat16)
        out = jnp.dot(activated, down_local, preferred_element_type=jnp.float32)
        return out.reshape(rows.shape)

    pieces = 2
    piece = capacity // pieces
    returned_pieces = []
    for index in range(pieces):
        part = spread[index * piece:(index + 1) * piece]
        arrivals = lax.all_to_all(part, "dev", split_axis=1, concat_axis=1, tiled=True)
        partner_rows = lax.ppermute(arrivals, "side", swap)
        mine_part = expert_part(arrivals)
        partner_part = expert_part(partner_rows).astype(jnp.bfloat16)
        got_part = lax.ppermute(partner_part, "side", swap)
        summed = (mine_part + got_part.astype(jnp.float32)).astype(jnp.bfloat16)
        returned_pieces.append(
            lax.all_to_all(summed, "dev", split_axis=1, concat_axis=1, tiled=True)
        )
    returned = jnp.concatenate(returned_pieces, axis=0)
    expert_out = jnp.sum(
        returned.reshape(capacity, experts, chips // experts, model_width).astype(jnp.float32),
        axis=2,
    ).astype(jnp.bfloat16)
    combine_cube = combine_matrix.reshape(token_count, experts, capacity)
    routed_sum = jnp.einsum(
        "tsc,csd->td",
        combine_cube,
        expert_out.astype(jnp.float32),
        precision=lax.Precision.HIGHEST,
    )
    return (hidden.astype(jnp.float32) + routed_sum).astype(jnp.bfloat16)


def solution(mesh):
    in_specs = (
        P("dev", None, None),
        P("dev", "side", None),
        P("dev"),
        P("side", None, None),
        P("side", "dev"),
        P(("side", "dev"), None),
        P(),
        P(("side", "dev"), None),
        P(("side", "dev"), None),
        P("dev", None, None, "side"),
        P("dev", "side", None),
    )
    out_specs = P(("side", "dev"), None)
    return jax.shard_map(
        on_device, mesh=mesh, in_specs=in_specs, out_specs=out_specs, check_vma=False
    )
```

```python
import jax
import jax.numpy as jnp
from jax import lax
from jax.sharding import PartitionSpec as P

QKD = 192

import functools

from jax.experimental import pallas as pl
from jax.experimental.pallas import tpu as pltpu

MESH_ID = pl.DeviceIdType.MESH
ORDERS = ((2, 0, 1), (0, 1, 2), (1, 2, 0))


def _gather_kernel(sizes, col_cuts, slots, block_ref, out_ref, own_sem, send_sems, recv_sems):
    side = lax.axis_index("side")
    me = lax.axis_index("dev")
    count_y, count_z, count_x = sizes
    mine = (me // (count_z * count_x), (me // count_x) % count_z, me % count_x)

    def chip(coords):
        return (coords[0] * count_z + coords[1]) * count_x + coords[2]

    def shifted(base, axis, offset):
        coords = list(base)
        coords[axis] = (coords[axis] + offset) % sizes[axis]
        return tuple(coords)

    barrier = pltpu.get_barrier_semaphore()
    peers = 0
    for axis in range(3):
        for offset in range(1, sizes[axis]):
            pl.semaphore_signal(
                barrier, 1, device_id=(side, chip(shifted(mine, axis, offset))), device_id_type=MESH_ID
            )
            peers += 1
    pl.semaphore_wait(barrier, peers)

    own = pltpu.make_async_copy(block_ref, out_ref.at[me], own_sem)
    own.start()
    streams = len(col_cuts) - 1
    sent = []

    def sem_at(stream, phase, index):
        return (stream * 3 + phase) * slots + index

    def remote(stream, phase, index, block_coords, target):
        cols = pl.ds(col_cuts[stream], col_cuts[stream + 1] - col_cuts[stream])
        at = sem_at(stream, phase, index)
        if phase == 0:
            src = block_ref.at[:, cols]
        else:
            src = out_ref.at[chip(block_coords), :, cols]
        return pltpu.make_async_remote_copy(
            src_ref=src,
            dst_ref=out_ref.at[chip(block_coords), :, cols],
            send_sem=send_sems.at[at],
            recv_sem=recv_sems.at[at],
            device_id=(side, chip(target)),
            device_id_type=MESH_ID,
        )

    def send(stream, phase, index, block_coords, target):
        copy = remote(stream, phase, index, block_coords, target)
        copy.start()
        sent.append(copy)

    def wait_in(stream, phase, index, block_coords):
        remote(stream, phase, index, block_coords, mine).wait_recv()

    for stream in range(streams):
        a0 = ORDERS[stream][0]
        n0 = sizes[a0]
        for step in range(1, n0):
            send(stream, 0, n0 - step - 1, mine, shifted(mine, a0, step))
    own.wait()
    def phase_one_copy(stream, e0, step):
        a0, a1, _ = ORDERS[stream]
        n1 = sizes[a1]
        index = e0 * (n1 - 1) + (n1 - step) - 1
        return remote(stream, 1, index, shifted(mine, a0, e0), shifted(mine, a1, step))

    for stream in range(streams):
        a0, a1, _ = ORDERS[stream]
        n0, n1 = sizes[a0], sizes[a1]
        for d0 in range(1, n0):
            wait_in(stream, 0, d0 - 1, shifted(mine, a0, d0))

        def start_line(e0, carry, stream=stream, n1=n1):
            for step in range(1, n1):
                phase_one_copy(stream, e0, step).start()
            return carry

        lax.fori_loop(0, n0, start_line, 0)

    def plane_block(stream, flat):
        a0, a1, _ = ORDERS[stream]
        n1 = sizes[a1]
        return shifted(shifted(mine, a0, flat // n1), a1, flat % n1)

    def phase_two_copy(stream, flat, step):
        a2 = ORDERS[stream][2]
        n2 = sizes[a2]
        index = flat * (n2 - 1) + (n2 - step) - 1
        return remote(stream, 2, index, plane_block(stream, flat), shifted(mine, a2, step))

    for stream in range(streams):
        a0, a1, a2 = ORDERS[stream]
        n0, n1, n2 = sizes[a0], sizes[a1], sizes[a2]
        for e0 in range(n0):
            for d1 in range(1, n1):
                wait_in(stream, 1, e0 * (n1 - 1) + d1 - 1, shifted(shifted(mine, a0, e0), a1, d1))

        def start_plane(flat, carry, stream=stream, n2=n2):
            for step in range(1, n2):
                phase_two_copy(stream, flat, step).start()
            return carry

        lax.fori_loop(0, n0 * n1, start_plane, 0)
    for stream in range(streams):
        a0, a1, a2 = ORDERS[stream]
        n0, n1, n2 = sizes[a0], sizes[a1], sizes[a2]

        def wait_plane(flat, carry, stream=stream, a2=a2, n2=n2):
            for d2 in range(1, n2):
                index = flat * (n2 - 1) + d2 - 1
                block = shifted(plane_block(stream, flat), a2, d2)
                wait_in(stream, 2, index, block)
            return carry

        lax.fori_loop(0, n0 * n1, wait_plane, 0)
    for copy in sent:
        copy.wait_send()
    for stream in range(streams):
        a0, a1, _ = ORDERS[stream]
        n0, n1 = sizes[a0], sizes[a1]

        def drain_line(e0, carry, stream=stream, n1=n1):
            for step in range(1, n1):
                phase_one_copy(stream, e0, step).wait_send()
            return carry

        lax.fori_loop(0, n0, drain_line, 0)
    for stream in range(streams):
        a0, a1, a2 = ORDERS[stream]
        n0, n1, n2 = sizes[a0], sizes[a1], sizes[a2]

        def drain_plane(flat, carry, stream=stream, n2=n2):
            for step in range(1, n2):
                phase_two_copy(stream, flat, step).wait_send()
            return carry

        lax.fori_loop(0, n0 * n1, drain_plane, 0)


def gather_over_dev(block, chips):
    side_len = round(chips ** (1.0 / 3.0))
    sizes = (side_len, side_len, side_len)
    rows, cols = block.shape
    tiles = cols // 128
    cuts = [0, (tiles + 2) // 3 * 128, (2 * tiles + 2) // 3 * 128, cols]
    slots = side_len * side_len * (side_len - 1)
    gathered = pl.pallas_call(
        functools.partial(_gather_kernel, sizes, cuts, slots),
        out_shape=jax.ShapeDtypeStruct((chips, rows, cols), block.dtype),
        in_specs=[pl.BlockSpec(memory_space=pl.ANY)],
        out_specs=pl.BlockSpec(memory_space=pl.ANY),
        scratch_shapes=[
            pltpu.SemaphoreType.DMA(()),
            pltpu.SemaphoreType.DMA((9 * slots,)),
            pltpu.SemaphoreType.DMA((9 * slots,)),
        ],
        compiler_params=pltpu.CompilerParams(collective_id=0, has_side_effects=True),
    )(block)
    return gathered.reshape(chips * rows, cols)


def _attend_kernel(limits_ref, query_ref, cache_ref, top_ref, total_ref, latent_ref, *, scale, latent_width):
    request = pl.program_id(0)
    query = query_ref[0]
    cache = cache_ref[0]
    scores = lax.dot_general(
        query, cache, (((1,), (1,)), ((), ())), preferred_element_type=jnp.float32
    ) * scale
    positions = lax.broadcasted_iota(jnp.int32, scores.shape, 1)
    usable = positions < limits_ref[request]
    masked = jnp.where(usable, scores, -1e30)
    top = jnp.max(masked, axis=1, keepdims=True)
    raised = jnp.where(usable, jnp.exp(masked - top), 0.0)
    top_ref[0] = top.reshape(1, -1)
    total_ref[0] = jnp.sum(raised, axis=1).reshape(1, -1)
    latent_ref[0] = jnp.dot(
        raised.astype(jnp.bfloat16), cache[:, :latent_width], preferred_element_type=jnp.float32
    )


def attend_local(limits, queries, cache, latent_width, scale):
    requests, heads, width = queries.shape
    slots = cache.shape[1]
    grid_spec = pltpu.PrefetchScalarGridSpec(
        num_scalar_prefetch=1,
        grid=(requests,),
        in_specs=[
            pl.BlockSpec((1, heads, width), lambda r, lim: (r, 0, 0)),
            pl.BlockSpec((1, slots, width), lambda r, lim: (r, 0, 0)),
        ],
        out_specs=[
            pl.BlockSpec((1, 1, heads), lambda r, lim: (r, 0, 0)),
            pl.BlockSpec((1, 1, heads), lambda r, lim: (r, 0, 0)),
            pl.BlockSpec((1, heads, latent_width), lambda r, lim: (r, 0, 0)),
        ],
    )
    top, total, latent = pl.pallas_call(
        functools.partial(_attend_kernel, scale=scale, latent_width=latent_width),
        grid_spec=grid_spec,
        out_shape=[
            jax.ShapeDtypeStruct((requests, 1, heads), jnp.float32),
            jax.ShapeDtypeStruct((requests, 1, heads), jnp.float32),
            jax.ShapeDtypeStruct((requests, heads, latent_width), jnp.float32),
        ],
    )(limits, queries, cache)
    return top.reshape(requests, heads), total.reshape(requests, heads), latent


def on_device(
    queries,
    latent_cache,
    lengths,
    value_lift,
    output_map,
    residual,
    norm_gain,
    expert_ids,
    gate_values,
    expert_in,
    expert_down,
):
    request_count = queries.shape[0]
    latent_width = value_lift.shape[1]
    half_heads = value_lift.shape[0]
    value_width = value_lift.shape[2]
    half_slots = latent_cache.shape[1]
    model_width = residual.shape[1]
    side_index = lax.axis_index("side")
    score_scale = QKD ** (-0.5)
    limits = lengths - side_index * half_slots
    local_top, local_total, local_latent = attend_local(
        limits, queries, latent_cache, latent_width, score_scale
    )
    swap = [(0, 1), (1, 0)]
    other_index = 1 - side_index

    def own_part(values):
        return lax.dynamic_slice_in_dim(values, side_index * half_heads, half_heads, 1)

    def sent_part(values):
        return lax.dynamic_slice_in_dim(values, other_index * half_heads, half_heads, 1)

    got_top, got_total, got_latent = lax.ppermute(
        (sent_part(local_top), sent_part(local_total), sent_part(local_latent)), "side", swap
    )
    own_top = own_part(local_top)
    row_top = jnp.maximum(own_top, got_top)
    own_weight = jnp.exp(own_top - row_top)
    got_weight = jnp.exp(got_top - row_top)
    row_total = own_weight * own_part(local_total) + got_weight * got_total
    latent_sum = (
        own_weight[:, :, None] * own_part(local_latent) + got_weight[:, :, None] * got_latent
    )
    own_heads = (latent_sum / row_total[:, :, None]).astype(jnp.bfloat16)
    head_values = jnp.einsum(
        "rhc,hcv->rhv", own_heads, value_lift, preferred_element_type=jnp.float32
    )
    head_values = head_values.astype(jnp.bfloat16).reshape(request_count, half_heads * value_width)
    gathered_values = gather_over_dev(head_values, lax.axis_size("dev"))
    partial_columns = jnp.dot(
        gathered_values,
        output_map,
        preferred_element_type=jnp.float32,
    )
    half_requests = partial_columns.shape[0] // 2
    kept_columns = lax.dynamic_slice_in_dim(partial_columns, side_index * half_requests, half_requests, 0)
    sent_columns = lax.dynamic_slice_in_dim(partial_columns, other_index * half_requests, half_requests, 0)
    got_columns = lax.ppermute(sent_columns.astype(jnp.bfloat16), "side", swap)
    summed_columns = kept_columns + got_columns.astype(jnp.float32)
    attention = lax.all_to_all(summed_columns, "dev", split_axis=0, concat_axis=1, tiled=True)
    gate_up_local = expert_in.reshape(model_width, -1)
    attention, gate_up_local = lax.optimization_barrier((attention, gate_up_local))
    hidden = (residual.astype(jnp.float32) + attention).astype(jnp.bfloat16)
    hidden_wide = hidden.astype(jnp.float32)
    normed = hidden_wide * lax.rsqrt(
        jnp.mean(hidden_wide * hidden_wide, axis=1, keepdims=True) + 1e-06
    )
    normed = (normed * norm_gain.astype(jnp.float32)[None, :]).astype(jnp.bfloat16)
    token_count = expert_ids.shape[0]
    route_count = expert_ids.shape[1]
    experts = lax.axis_size("dev") // 2
    capacity = max(4, token_count * route_count // experts)
    flat_ids = expert_ids.reshape(-1)
    expert_hits = (flat_ids[:, None] == jnp.arange(experts, dtype=jnp.int32)[None, :]).astype(
        jnp.int32
    )
    before = jnp.cumsum(expert_hits, axis=0) - expert_hits
    slot_index = jnp.sum(before * expert_hits, axis=1).reshape(token_count, route_count)
    slot_code = expert_ids * capacity + slot_index
    slot_table = jnp.arange(experts * capacity, dtype=jnp.int32)
    slot_match = slot_code[None, :, :] == slot_table[:, None, None]
    dispatch_matrix = jnp.any(slot_match, axis=2).astype(jnp.bfloat16)
    combine_matrix = jnp.sum(jnp.where(slot_match, gate_values[None, :, :], 0.0), axis=2).T
    dispatch_cube = dispatch_matrix.reshape(experts, capacity, token_count)
    outgoing = jnp.einsum(
        "sct,td->csd", dispatch_cube, normed, preferred_element_type=jnp.float32
    ).astype(jnp.bfloat16)
    quarter_width = expert_in.shape[3]
    down_local = expert_down[0]
    chips = lax.axis_size("dev")
    spread = jnp.broadcast_to(outgoing[:, :, None], (capacity, experts, chips // experts, model_width))
    spread = spread.reshape(capacity, chips, model_width)
    arrivals = lax.all_to_all(spread, "dev", split_axis=1, concat_axis=1, tiled=True)
    partner_rows = lax.ppermute(arrivals, "side", swap)

    def expert_part(rows):
        flat = rows.reshape(capacity * chips, model_width)
        gate_up = jnp.dot(flat, gate_up_local, preferred_element_type=jnp.float32)
        activated = (
            jax.nn.silu(gate_up[:, :quarter_width]) * gate_up[:, quarter_width:]
        ).astype(jnp.bfloat16)
        out = jnp.dot(activated, down_local, preferred_element_type=jnp.float32)
        return out.reshape(capacity, chips, model_width)

    mine_part = expert_part(arrivals)
    partner_part = expert_part(partner_rows).astype(jnp.bfloat16)
    got_part = lax.ppermute(partner_part, "side", swap)
    summed = (mine_part + got_part.astype(jnp.float32)).astype(jnp.bfloat16)
    returned = lax.all_to_all(summed, "dev", split_axis=1, concat_axis=1, tiled=True)
    halves = chips // experts
    combine_cube = jnp.broadcast_to(
        combine_matrix.reshape(token_count, experts, 1, capacity),
        (token_count, experts, halves, capacity),
    )
    routed_sum = jnp.einsum(
        "tsjc,csjd->td",
        combine_cube,
        returned.reshape(capacity, experts, halves, model_width).astype(jnp.float32),
        precision=lax.Precision.HIGHEST,
    )
    return (hidden.astype(jnp.float32) + routed_sum).astype(jnp.bfloat16)


def solution(mesh):
    in_specs = (
        P("dev", None, None),
        P("dev", "side", None),
        P("dev"),
        P("side", None, None),
        P("side", "dev"),
        P(("side", "dev"), None),
        P(),
        P(("side", "dev"), None),
        P(("side", "dev"), None),
        P("dev", None, None, "side"),
        P("dev", "side", None),
    )
    out_specs = P(("side", "dev"), None)
    return jax.shard_map(
        on_device, mesh=mesh, in_specs=in_specs, out_specs=out_specs, check_vma=False
    )
```

```python
import jax
import jax.numpy as jnp
from jax import lax
from jax.sharding import PartitionSpec as P

QKD = 192

import functools

from jax.experimental import pallas as pl
from jax.experimental.pallas import tpu as pltpu

MESH_ID = pl.DeviceIdType.MESH
ORDERS = ((2, 0, 1), (0, 1, 2), (1, 2, 0))


def _gather_kernel(
    sizes, col_cuts, slots, block_ref, weight_ref, result_ref, out_ref, own_sem, send_sems, recv_sems
):
    side = lax.axis_index("side")
    me = lax.axis_index("dev")
    count_y, count_z, count_x = sizes
    mine = (me // (count_z * count_x), (me // count_x) % count_z, me % count_x)

    def chip(coords):
        return (coords[0] * count_z + coords[1]) * count_x + coords[2]

    def shifted(base, axis, offset):
        coords = list(base)
        coords[axis] = (coords[axis] + offset) % sizes[axis]
        return tuple(coords)

    barrier = pltpu.get_barrier_semaphore()
    peers = 0
    for axis in range(3):
        for offset in range(1, sizes[axis]):
            pl.semaphore_signal(
                barrier, 1, device_id=(side, chip(shifted(mine, axis, offset))), device_id_type=MESH_ID
            )
            peers += 1
    pl.semaphore_wait(barrier, peers)

    own = pltpu.make_async_copy(block_ref, out_ref.at[me], own_sem)
    own.start()
    streams = len(col_cuts) - 1
    sent = []

    def sem_at(stream, phase, index):
        return (stream * 3 + phase) * slots + index

    def remote(stream, phase, index, block_coords, target):
        cols = pl.ds(col_cuts[stream], col_cuts[stream + 1] - col_cuts[stream])
        at = sem_at(stream, phase, index)
        if phase == 0:
            src = block_ref.at[:, cols]
        else:
            src = out_ref.at[chip(block_coords), :, cols]
        return pltpu.make_async_remote_copy(
            src_ref=src,
            dst_ref=out_ref.at[chip(block_coords), :, cols],
            send_sem=send_sems.at[at],
            recv_sem=recv_sems.at[at],
            device_id=(side, chip(target)),
            device_id_type=MESH_ID,
        )

    def send(stream, phase, index, block_coords, target):
        copy = remote(stream, phase, index, block_coords, target)
        copy.start()
        sent.append(copy)

    def wait_in(stream, phase, index, block_coords):
        remote(stream, phase, index, block_coords, mine).wait_recv()

    for stream in range(streams):
        a0 = ORDERS[stream][0]
        n0 = sizes[a0]
        for step in range(1, n0):
            send(stream, 0, n0 - step - 1, mine, shifted(mine, a0, step))
    own.wait()
    def phase_one_copy(stream, e0, step):
        a0, a1, _ = ORDERS[stream]
        n1 = sizes[a1]
        index = e0 * (n1 - 1) + (n1 - step) - 1
        return remote(stream, 1, index, shifted(mine, a0, e0), shifted(mine, a1, step))

    for stream in range(streams):
        a0, a1, _ = ORDERS[stream]
        n0, n1 = sizes[a0], sizes[a1]
        for d0 in range(1, n0):
            wait_in(stream, 0, d0 - 1, shifted(mine, a0, d0))

        def start_line(e0, carry, stream=stream, n1=n1):
            for step in range(1, n1):
                phase_one_copy(stream, e0, step).start()
            return carry

        lax.fori_loop(0, n0, start_line, 0)

    def plane_block(stream, flat):
        a0, a1, _ = ORDERS[stream]
        n1 = sizes[a1]
        return shifted(shifted(mine, a0, flat // n1), a1, flat % n1)

    def phase_two_copy(stream, flat, step):
        a2 = ORDERS[stream][2]
        n2 = sizes[a2]
        index = flat * (n2 - 1) + (n2 - step) - 1
        return remote(stream, 2, index, plane_block(stream, flat), shifted(mine, a2, step))

    for stream in range(streams):
        a0, a1, a2 = ORDERS[stream]
        n0, n1, n2 = sizes[a0], sizes[a1], sizes[a2]
        for e0 in range(n0):
            for d1 in range(1, n1):
                wait_in(stream, 1, e0 * (n1 - 1) + d1 - 1, shifted(shifted(mine, a0, e0), a1, d1))

        def start_plane(flat, carry, stream=stream, n2=n2):
            for step in range(1, n2):
                phase_two_copy(stream, flat, step).start()
            return carry

        lax.fori_loop(0, n0 * n1, start_plane, 0)
    for stream in range(streams):
        a0, a1, a2 = ORDERS[stream]
        n0, n1, n2 = sizes[a0], sizes[a1], sizes[a2]

        def wait_plane(flat, carry, stream=stream, a2=a2, n2=n2):
            for d2 in range(1, n2):
                index = flat * (n2 - 1) + d2 - 1
                block = shifted(plane_block(stream, flat), a2, d2)
                wait_in(stream, 2, index, block)
            return carry

        lax.fori_loop(0, n0 * n1, wait_plane, 0)
    for copy in sent:
        copy.wait_send()
    for stream in range(streams):
        a0, a1, _ = ORDERS[stream]
        n0, n1 = sizes[a0], sizes[a1]

        def drain_line(e0, carry, stream=stream, n1=n1):
            for step in range(1, n1):
                phase_one_copy(stream, e0, step).wait_send()
            return carry

        lax.fori_loop(0, n0, drain_line, 0)
    for stream in range(streams):
        a0, a1, a2 = ORDERS[stream]
        n0, n1, n2 = sizes[a0], sizes[a1], sizes[a2]

        def drain_plane(flat, carry, stream=stream, n2=n2):
            for step in range(1, n2):
                phase_two_copy(stream, flat, step).wait_send()
            return carry

        lax.fori_loop(0, n0 * n1, drain_plane, 0)

    chips, rows, width = out_ref.shape
    group = max(1, 128 // rows)

    def project(index, carry):
        held = out_ref[pl.ds(index * group, group)].reshape(group * rows, width)
        result_ref[pl.ds(index * group * rows, group * rows), :] = jnp.dot(
            held, weight_ref[...], preferred_element_type=jnp.float32
        )
        return carry

    lax.fori_loop(0, chips // group, project, 0)


def gather_and_project(block, weight, chips):
    side_len = round(chips ** (1.0 / 3.0))
    sizes = (side_len, side_len, side_len)
    rows, cols = block.shape
    tiles = cols // 128
    cuts = [0, (tiles + 2) // 3 * 128, (2 * tiles + 2) // 3 * 128, cols]
    slots = side_len * side_len * (side_len - 1)
    return pl.pallas_call(
        functools.partial(_gather_kernel, sizes, cuts, slots),
        out_shape=jax.ShapeDtypeStruct((chips * rows, weight.shape[1]), jnp.float32),
        in_specs=[pl.BlockSpec(memory_space=pltpu.VMEM), pl.BlockSpec(memory_space=pltpu.VMEM)],
        out_specs=pl.BlockSpec(memory_space=pltpu.VMEM),
        scratch_shapes=[
            pltpu.VMEM((chips, rows, cols), block.dtype),
            pltpu.SemaphoreType.DMA(()),
            pltpu.SemaphoreType.DMA((9 * slots,)),
            pltpu.SemaphoreType.DMA((9 * slots,)),
        ],
        compiler_params=pltpu.CompilerParams(
            collective_id=0, has_side_effects=True, vmem_limit_bytes=48 * 1024 * 1024
        ),
    )(block, weight)

def on_device(
    queries,
    latent_cache,
    lengths,
    value_lift,
    output_map,
    residual,
    norm_gain,
    expert_ids,
    gate_values,
    expert_in,
    expert_down,
):
    request_count = queries.shape[0]
    latent_width = value_lift.shape[1]
    half_heads = value_lift.shape[0]
    value_width = value_lift.shape[2]
    half_slots = latent_cache.shape[1]
    model_width = residual.shape[1]
    side_index = lax.axis_index("side")
    score_scale = QKD ** (-0.5)
    scores = (
        jnp.einsum("rhc,rpc->rhp", queries, latent_cache, preferred_element_type=jnp.float32)
        * score_scale
    )
    positions = side_index * half_slots + jnp.arange(half_slots, dtype=jnp.int32)
    usable = (positions[None, :] < lengths[:, None])[:, None, :]
    masked = jnp.where(usable, scores, -1e30)
    swap = [(0, 1), (1, 0)]
    local_top = jnp.max(masked, axis=2)
    row_top = jnp.maximum(local_top, lax.ppermute(local_top, "side", swap))
    raised = jnp.where(usable, jnp.exp(masked - row_top[:, :, None]), 0.0)
    local_total = jnp.sum(raised, axis=2)
    probabilities = raised.astype(jnp.bfloat16)
    local_latent = jnp.einsum(
        "rhp,rpc->rhc",
        probabilities,
        latent_cache[:, :, :latent_width],
        preferred_element_type=jnp.float32,
    )
    other_index = 1 - side_index
    own_latent = lax.dynamic_slice_in_dim(local_latent, side_index * half_heads, half_heads, 1)
    own_total = lax.dynamic_slice_in_dim(local_total, side_index * half_heads, half_heads, 1)
    sent_latent = lax.dynamic_slice_in_dim(local_latent, other_index * half_heads, half_heads, 1)
    sent_total = lax.dynamic_slice_in_dim(local_total, other_index * half_heads, half_heads, 1)
    got_latent, got_total = lax.ppermute((sent_latent, sent_total), "side", swap)
    row_total = own_total + got_total
    latent_sum = own_latent + got_latent
    own_heads = (latent_sum / row_total[:, :, None]).astype(jnp.bfloat16)
    head_values = jnp.einsum(
        "rhc,hcv->rhv", own_heads, value_lift, preferred_element_type=jnp.float32
    )
    head_values = head_values.astype(jnp.bfloat16).reshape(request_count, half_heads * value_width)
    partial_columns = gather_and_project(head_values, output_map, lax.axis_size("dev"))
    half_requests = partial_columns.shape[0] // 2
    kept_columns = lax.dynamic_slice_in_dim(partial_columns, side_index * half_requests, half_requests, 0)
    sent_columns = lax.dynamic_slice_in_dim(partial_columns, other_index * half_requests, half_requests, 0)
    got_columns = lax.ppermute(sent_columns.astype(jnp.bfloat16), "side", swap)
    summed_columns = kept_columns + got_columns.astype(jnp.float32)
    attention = lax.all_to_all(summed_columns, "dev", split_axis=0, concat_axis=1, tiled=True)
    gate_up_local = expert_in.reshape(model_width, -1)
    attention, gate_up_local = lax.optimization_barrier((attention, gate_up_local))
    hidden = (residual.astype(jnp.float32) + attention).astype(jnp.bfloat16)
    hidden_wide = hidden.astype(jnp.float32)
    normed = hidden_wide * lax.rsqrt(
        jnp.mean(hidden_wide * hidden_wide, axis=1, keepdims=True) + 1e-06
    )
    normed = (normed * norm_gain.astype(jnp.float32)[None, :]).astype(jnp.bfloat16)
    token_count = expert_ids.shape[0]
    route_count = expert_ids.shape[1]
    experts = lax.axis_size("dev") // 2
    capacity = max(4, token_count * route_count // experts)
    flat_ids = expert_ids.reshape(-1)
    expert_hits = (flat_ids[:, None] == jnp.arange(experts, dtype=jnp.int32)[None, :]).astype(
        jnp.int32
    )
    before = jnp.cumsum(expert_hits, axis=0) - expert_hits
    slot_index = jnp.sum(before * expert_hits, axis=1).reshape(token_count, route_count)
    slot_code = expert_ids * capacity + slot_index
    slot_table = jnp.arange(experts * capacity, dtype=jnp.int32)
    slot_match = slot_code[None, :, :] == slot_table[:, None, None]
    dispatch_matrix = jnp.any(slot_match, axis=2).astype(jnp.bfloat16)
    combine_matrix = jnp.sum(jnp.where(slot_match, gate_values[None, :, :], 0.0), axis=2).T
    dispatch_cube = dispatch_matrix.reshape(experts, capacity, token_count)
    outgoing = jnp.einsum(
        "sct,td->csd", dispatch_cube, normed, preferred_element_type=jnp.float32
    ).astype(jnp.bfloat16)
    quarter_width = expert_in.shape[3]
    down_local = expert_down[0]
    chips = lax.axis_size("dev")
    spread = jnp.broadcast_to(outgoing[:, :, None], (capacity, experts, chips // experts, model_width))
    spread = spread.reshape(capacity, chips, model_width)
    arrivals = lax.all_to_all(spread, "dev", split_axis=1, concat_axis=1, tiled=True)
    partner_rows = lax.ppermute(arrivals, "side", swap)

    def expert_part(rows):
        flat = rows.reshape(capacity * chips, model_width)
        gate_up = jnp.dot(flat, gate_up_local, preferred_element_type=jnp.float32)
        activated = (
            jax.nn.silu(gate_up[:, :quarter_width]) * gate_up[:, quarter_width:]
        ).astype(jnp.bfloat16)
        out = jnp.dot(activated, down_local, preferred_element_type=jnp.float32)
        return out.reshape(capacity, chips, model_width)

    mine_part = expert_part(arrivals)
    partner_part = expert_part(partner_rows).astype(jnp.bfloat16)
    got_part = lax.ppermute(partner_part, "side", swap)
    summed = (mine_part + got_part.astype(jnp.float32)).astype(jnp.bfloat16)
    returned = lax.all_to_all(summed, "dev", split_axis=1, concat_axis=1, tiled=True)
    expert_out = jnp.sum(
        returned.reshape(capacity, experts, chips // experts, model_width).astype(jnp.float32),
        axis=2,
    ).astype(jnp.bfloat16)
    combine_cube = combine_matrix.reshape(token_count, experts, capacity)
    routed_sum = jnp.einsum(
        "tsc,csd->td",
        combine_cube,
        expert_out.astype(jnp.float32),
        precision=lax.Precision.HIGHEST,
    )
    return (hidden.astype(jnp.float32) + routed_sum).astype(jnp.bfloat16)


def solution(mesh):
    in_specs = (
        P("dev", None, None),
        P("dev", "side", None),
        P("dev"),
        P("side", None, None),
        P("side", "dev"),
        P(("side", "dev"), None),
        P(),
        P(("side", "dev"), None),
        P(("side", "dev"), None),
        P("dev", None, None, "side"),
        P("dev", "side", None),
    )
    out_specs = P(("side", "dev"), None)
    return jax.shard_map(
        on_device, mesh=mesh, in_specs=in_specs, out_specs=out_specs, check_vma=False
    )
```

```python
import jax
import jax.numpy as jnp
from jax import lax
from jax.sharding import PartitionSpec as P

QKD = 192

import functools

from jax.experimental import pallas as pl
from jax.experimental.pallas import tpu as pltpu

MESH_ID = pl.DeviceIdType.MESH
ORDERS = ((2, 0, 1), (0, 1, 2), (1, 2, 0))


def _gather_kernel(
    sizes, col_cuts, slots, block_ref, weight_ref, result_ref, out_ref, own_sem, send_sems, recv_sems
):
    side = lax.axis_index("side")
    me = lax.axis_index("dev")
    count_y, count_z, count_x = sizes
    mine = (me // (count_z * count_x), (me // count_x) % count_z, me % count_x)

    def chip(coords):
        return (coords[0] * count_z + coords[1]) * count_x + coords[2]

    def shifted(base, axis, offset):
        coords = list(base)
        coords[axis] = (coords[axis] + offset) % sizes[axis]
        return tuple(coords)

    barrier = pltpu.get_barrier_semaphore()
    peers = 0
    for axis in range(3):
        for offset in range(1, sizes[axis]):
            pl.semaphore_signal(
                barrier, 1, device_id=(side, chip(shifted(mine, axis, offset))), device_id_type=MESH_ID
            )
            peers += 1
    pl.semaphore_wait(barrier, peers)

    own = pltpu.make_async_copy(block_ref, out_ref.at[me], own_sem)
    own.start()
    streams = len(col_cuts) - 1
    sent = []

    def sem_at(stream, phase, index):
        return (stream * 3 + phase) * slots + index

    def remote(stream, phase, index, block_coords, target, from_input=False):
        cols = pl.ds(col_cuts[stream], col_cuts[stream + 1] - col_cuts[stream])
        at = sem_at(stream, phase, index)
        if from_input:
            src = block_ref.at[:, cols]
        else:
            src = out_ref.at[chip(block_coords), :, cols]
        return pltpu.make_async_remote_copy(
            src_ref=src,
            dst_ref=out_ref.at[chip(block_coords), :, cols],
            send_sem=send_sems.at[at],
            recv_sem=recv_sems.at[at],
            device_id=(side, chip(target)),
            device_id_type=MESH_ID,
        )

    def wait_in(stream, phase, index, block_coords):
        remote(stream, phase, index, block_coords, mine).wait_recv()

    def phase_one_copy(stream, e0, from_input=False):
        a0, a1, _ = ORDERS[stream]
        n1 = sizes[a1]
        for step in range(1, n1):
            index = e0 * (n1 - 1) + (n1 - step) - 1
            yield remote(stream, 1, index, shifted(mine, a0, e0), shifted(mine, a1, step), from_input)

    def phase_two_copy(stream, e0, e1, from_input=False):
        a0, a1, a2 = ORDERS[stream]
        n1, n2 = sizes[a1], sizes[a2]
        block = shifted(shifted(mine, a0, e0), a1, e1)
        for step in range(1, n2):
            index = (e0 * n1 + e1) * (n2 - 1) + (n2 - step) - 1
            yield remote(stream, 2, index, block, shifted(mine, a2, step), from_input)

    def start_all(copies):
        for copy in copies:
            copy.start()
            sent.append(copy)

    for stream in range(streams):
        a0 = ORDERS[stream][0]
        n0 = sizes[a0]
        for step in range(1, n0):
            copy = remote(stream, 0, n0 - step - 1, mine, shifted(mine, a0, step), True)
            copy.start()
            sent.append(copy)
        start_all(phase_one_copy(stream, 0, True))
        start_all(phase_two_copy(stream, 0, 0, True))
    own.wait()
    for stream in range(streams):
        a0 = ORDERS[stream][0]
        for d0 in range(1, sizes[a0]):
            wait_in(stream, 0, d0 - 1, shifted(mine, a0, d0))
            start_all(phase_one_copy(stream, d0))
            start_all(phase_two_copy(stream, d0, 0))
    for stream in range(streams):
        a0, a1, _ = ORDERS[stream]
        n0, n1 = sizes[a0], sizes[a1]

        def forward(flat, carry, stream=stream, a0=a0, a1=a1, n1=n1):
            e0 = flat // (n1 - 1)
            d1 = flat % (n1 - 1) + 1
            wait_in(stream, 1, flat, shifted(shifted(mine, a0, e0), a1, d1))
            for copy in phase_two_copy(stream, e0, d1):
                copy.start()
            return carry

        lax.fori_loop(0, n0 * (n1 - 1), forward, 0)
    for stream in range(streams):
        a0, a1, a2 = ORDERS[stream]
        n0, n1, n2 = sizes[a0], sizes[a1], sizes[a2]

        def wait_plane(flat, carry, stream=stream, a0=a0, a1=a1, a2=a2, n1=n1, n2=n2):
            block = shifted(shifted(mine, a0, flat // n1), a1, flat % n1)
            for d2 in range(1, n2):
                wait_in(stream, 2, flat * (n2 - 1) + d2 - 1, shifted(block, a2, d2))
            return carry

        lax.fori_loop(0, n0 * n1, wait_plane, 0)
    for copy in sent:
        copy.wait_send()
    for stream in range(streams):
        a0, a1, _ = ORDERS[stream]
        n0, n1 = sizes[a0], sizes[a1]

        def drain(flat, carry, stream=stream, n1=n1):
            for copy in phase_two_copy(stream, flat // (n1 - 1), flat % (n1 - 1) + 1):
                copy.wait_send()
            return carry

        lax.fori_loop(0, n0 * (n1 - 1), drain, 0)

    chips, rows, width = out_ref.shape
    group = max(1, 128 // rows)

    def project(index, carry):
        held = out_ref[pl.ds(index * group, group)].reshape(group * rows, width)
        result_ref[pl.ds(index * group * rows, group * rows), :] = jnp.dot(
            held, weight_ref[...], preferred_element_type=jnp.float32
        )
        return carry

    lax.fori_loop(0, chips // group, project, 0)


def gather_and_project(block, weight, chips):
    side_len = round(chips ** (1.0 / 3.0))
    sizes = (side_len, side_len, side_len)
    rows, cols = block.shape
    tiles = cols // 128
    cuts = [0, (tiles + 2) // 3 * 128, (2 * tiles + 2) // 3 * 128, cols]
    slots = side_len * side_len * (side_len - 1)
    return pl.pallas_call(
        functools.partial(_gather_kernel, sizes, cuts, slots),
        out_shape=jax.ShapeDtypeStruct((chips * rows, weight.shape[1]), jnp.float32),
        in_specs=[pl.BlockSpec(memory_space=pltpu.VMEM), pl.BlockSpec(memory_space=pltpu.VMEM)],
        out_specs=pl.BlockSpec(memory_space=pltpu.VMEM),
        scratch_shapes=[
            pltpu.VMEM((chips, rows, cols), block.dtype),
            pltpu.SemaphoreType.DMA(()),
            pltpu.SemaphoreType.DMA((9 * slots,)),
            pltpu.SemaphoreType.DMA((9 * slots,)),
        ],
        compiler_params=pltpu.CompilerParams(
            collective_id=0, has_side_effects=True, vmem_limit_bytes=48 * 1024 * 1024
        ),
    )(block, weight)

def on_device(
    queries,
    latent_cache,
    lengths,
    value_lift,
    output_map,
    residual,
    norm_gain,
    expert_ids,
    gate_values,
    expert_in,
    expert_down,
):
    request_count = queries.shape[0]
    latent_width = value_lift.shape[1]
    half_heads = value_lift.shape[0]
    value_width = value_lift.shape[2]
    half_slots = latent_cache.shape[1]
    model_width = residual.shape[1]
    side_index = lax.axis_index("side")
    score_scale = QKD ** (-0.5)
    scores = (
        jnp.einsum("rhc,rpc->rhp", queries, latent_cache, preferred_element_type=jnp.float32)
        * score_scale
    )
    positions = side_index * half_slots + jnp.arange(half_slots, dtype=jnp.int32)
    usable = (positions[None, :] < lengths[:, None])[:, None, :]
    masked = jnp.where(usable, scores, -1e30)
    swap = [(0, 1), (1, 0)]
    local_top = jnp.max(masked, axis=2)
    row_top = jnp.maximum(local_top, lax.ppermute(local_top, "side", swap))
    raised = jnp.where(usable, jnp.exp(masked - row_top[:, :, None]), 0.0)
    local_total = jnp.sum(raised, axis=2)
    probabilities = raised.astype(jnp.bfloat16)
    local_latent = jnp.einsum(
        "rhp,rpc->rhc",
        probabilities,
        latent_cache[:, :, :latent_width],
        preferred_element_type=jnp.float32,
    )
    other_index = 1 - side_index
    own_latent = lax.dynamic_slice_in_dim(local_latent, side_index * half_heads, half_heads, 1)
    own_total = lax.dynamic_slice_in_dim(local_total, side_index * half_heads, half_heads, 1)
    sent_latent = lax.dynamic_slice_in_dim(local_latent, other_index * half_heads, half_heads, 1)
    sent_total = lax.dynamic_slice_in_dim(local_total, other_index * half_heads, half_heads, 1)
    got_latent, got_total = lax.ppermute((sent_latent, sent_total), "side", swap)
    row_total = own_total + got_total
    latent_sum = own_latent + got_latent
    own_heads = (latent_sum / row_total[:, :, None]).astype(jnp.bfloat16)
    head_values = jnp.einsum(
        "rhc,hcv->rhv", own_heads, value_lift, preferred_element_type=jnp.float32
    )
    head_values = head_values.astype(jnp.bfloat16).reshape(request_count, half_heads * value_width)
    partial_columns = gather_and_project(head_values, output_map, lax.axis_size("dev"))
    half_requests = partial_columns.shape[0] // 2
    kept_columns = lax.dynamic_slice_in_dim(partial_columns, side_index * half_requests, half_requests, 0)
    sent_columns = lax.dynamic_slice_in_dim(partial_columns, other_index * half_requests, half_requests, 0)
    got_columns = lax.ppermute(sent_columns.astype(jnp.bfloat16), "side", swap)
    summed_columns = kept_columns + got_columns.astype(jnp.float32)
    attention = lax.all_to_all(summed_columns, "dev", split_axis=0, concat_axis=1, tiled=True)
    gate_up_local = expert_in.reshape(model_width, -1)
    attention, gate_up_local = lax.optimization_barrier((attention, gate_up_local))
    hidden = (residual.astype(jnp.float32) + attention).astype(jnp.bfloat16)
    hidden_wide = hidden.astype(jnp.float32)
    normed = hidden_wide * lax.rsqrt(
        jnp.mean(hidden_wide * hidden_wide, axis=1, keepdims=True) + 1e-06
    )
    normed = (normed * norm_gain.astype(jnp.float32)[None, :]).astype(jnp.bfloat16)
    token_count = expert_ids.shape[0]
    route_count = expert_ids.shape[1]
    experts = lax.axis_size("dev") // 2
    capacity = max(4, token_count * route_count // experts)
    flat_ids = expert_ids.reshape(-1)
    expert_hits = (flat_ids[:, None] == jnp.arange(experts, dtype=jnp.int32)[None, :]).astype(
        jnp.int32
    )
    before = jnp.cumsum(expert_hits, axis=0) - expert_hits
    slot_index = jnp.sum(before * expert_hits, axis=1).reshape(token_count, route_count)
    slot_code = expert_ids * capacity + slot_index
    slot_table = jnp.arange(experts * capacity, dtype=jnp.int32)
    slot_match = slot_code[None, :, :] == slot_table[:, None, None]
    dispatch_matrix = jnp.any(slot_match, axis=2).astype(jnp.bfloat16)
    combine_matrix = jnp.sum(jnp.where(slot_match, gate_values[None, :, :], 0.0), axis=2).T
    dispatch_cube = dispatch_matrix.reshape(experts, capacity, token_count)
    outgoing = jnp.einsum(
        "sct,td->csd", dispatch_cube, normed, preferred_element_type=jnp.float32
    ).astype(jnp.bfloat16)
    quarter_width = expert_in.shape[3]
    down_local = expert_down[0]
    chips = lax.axis_size("dev")
    spread = jnp.broadcast_to(outgoing[:, :, None], (capacity, experts, chips // experts, model_width))
    spread = spread.reshape(capacity, chips, model_width)
    arrivals = lax.all_to_all(spread, "dev", split_axis=1, concat_axis=1, tiled=True)
    partner_rows = lax.ppermute(arrivals, "side", swap)

    def expert_part(rows):
        flat = rows.reshape(capacity * chips, model_width)
        gate_up = jnp.dot(flat, gate_up_local, preferred_element_type=jnp.float32)
        activated = (
            jax.nn.silu(gate_up[:, :quarter_width]) * gate_up[:, quarter_width:]
        ).astype(jnp.bfloat16)
        out = jnp.dot(activated, down_local, preferred_element_type=jnp.float32)
        return out.reshape(capacity, chips, model_width)

    mine_part = expert_part(arrivals)
    partner_part = expert_part(partner_rows).astype(jnp.bfloat16)
    got_part = lax.ppermute(partner_part, "side", swap)
    summed = (mine_part + got_part.astype(jnp.float32)).astype(jnp.bfloat16)
    returned = lax.all_to_all(summed, "dev", split_axis=1, concat_axis=1, tiled=True)
    expert_out = jnp.sum(
        returned.reshape(capacity, experts, chips // experts, model_width).astype(jnp.float32),
        axis=2,
    ).astype(jnp.bfloat16)
    combine_cube = combine_matrix.reshape(token_count, experts, capacity)
    routed_sum = jnp.einsum(
        "tsc,csd->td",
        combine_cube,
        expert_out.astype(jnp.float32),
        precision=lax.Precision.HIGHEST,
    )
    return (hidden.astype(jnp.float32) + routed_sum).astype(jnp.bfloat16)


def solution(mesh):
    in_specs = (
        P("dev", None, None),
        P("dev", "side", None),
        P("dev"),
        P("side", None, None),
        P("side", "dev"),
        P(("side", "dev"), None),
        P(),
        P(("side", "dev"), None),
        P(("side", "dev"), None),
        P("dev", None, None, "side"),
        P("dev", "side", None),
    )
    out_specs = P(("side", "dev"), None)
    return jax.shard_map(
        on_device, mesh=mesh, in_specs=in_specs, out_specs=out_specs, check_vma=False
    )
```

```python
import jax
import jax.numpy as jnp
from jax import lax
from jax.sharding import PartitionSpec as P

QKD = 192

import functools

from jax.experimental import pallas as pl
from jax.experimental.pallas import tpu as pltpu

MESH_ID = pl.DeviceIdType.MESH
ORDERS = ((2, 0, 1), (0, 1, 2), (1, 2, 0))


def _gather_kernel(
    sizes, col_cuts, slots, block_ref, weight_ref, result_ref, out_ref, own_sem, send_sems, recv_sems
):
    side = lax.axis_index("side")
    me = lax.axis_index("dev")
    count_y, count_z, count_x = sizes
    mine = (me // (count_z * count_x), (me // count_x) % count_z, me % count_x)

    def chip(coords):
        return (coords[0] * count_z + coords[1]) * count_x + coords[2]

    def shifted(base, axis, offset):
        coords = list(base)
        coords[axis] = (coords[axis] + offset) % sizes[axis]
        return tuple(coords)

    barrier = pltpu.get_barrier_semaphore()
    peers = 0
    for axis in range(3):
        for offset in range(1, sizes[axis]):
            pl.semaphore_signal(
                barrier, 1, device_id=(side, chip(shifted(mine, axis, offset))), device_id_type=MESH_ID
            )
            peers += 1
    pl.semaphore_wait(barrier, peers)

    own = pltpu.make_async_copy(block_ref, out_ref.at[me], own_sem)
    own.start()
    streams = len(col_cuts) - 1
    sent = []

    def sem_at(stream, phase, index):
        return (stream * 3 + phase) * slots + index

    def remote(stream, phase, index, block_coords, target, from_input=False):
        cols = pl.ds(col_cuts[stream], col_cuts[stream + 1] - col_cuts[stream])
        at = sem_at(stream, phase, index)
        if from_input:
            src = block_ref.at[:, cols]
        else:
            src = out_ref.at[chip(block_coords), :, cols]
        return pltpu.make_async_remote_copy(
            src_ref=src,
            dst_ref=out_ref.at[chip(block_coords), :, cols],
            send_sem=send_sems.at[at],
            recv_sem=recv_sems.at[at],
            device_id=(side, chip(target)),
            device_id_type=MESH_ID,
        )

    def wait_in(stream, phase, index, block_coords):
        remote(stream, phase, index, block_coords, mine).wait_recv()

    def phase_one_copy(stream, e0, from_input=False):
        a0, a1, _ = ORDERS[stream]
        n1 = sizes[a1]
        for step in range(1, n1):
            index = e0 * (n1 - 1) + (n1 - step) - 1
            yield remote(stream, 1, index, shifted(mine, a0, e0), shifted(mine, a1, step), from_input)

    def phase_two_copy(stream, e0, e1, from_input=False):
        a0, a1, a2 = ORDERS[stream]
        n1, n2 = sizes[a1], sizes[a2]
        block = shifted(shifted(mine, a0, e0), a1, e1)
        for step in range(1, n2):
            index = (e0 * n1 + e1) * (n2 - 1) + (n2 - step) - 1
            yield remote(stream, 2, index, block, shifted(mine, a2, step), from_input)

    def start_all(copies):
        for copy in copies:
            copy.start()
            sent.append(copy)

    for stream in range(streams):
        a0 = ORDERS[stream][0]
        n0 = sizes[a0]
        for step in range(1, n0):
            copy = remote(stream, 0, n0 - step - 1, mine, shifted(mine, a0, step), True)
            copy.start()
            sent.append(copy)
        start_all(phase_one_copy(stream, 0, True))
        start_all(phase_two_copy(stream, 0, 0, True))
    own.wait()
    for stream in range(streams):
        a0 = ORDERS[stream][0]
        for d0 in range(1, sizes[a0]):
            wait_in(stream, 0, d0 - 1, shifted(mine, a0, d0))
            start_all(phase_one_copy(stream, d0))
            start_all(phase_two_copy(stream, d0, 0))
    for stream in range(streams):
        a0, a1, _ = ORDERS[stream]
        n0, n1 = sizes[a0], sizes[a1]

        def forward(flat, carry, stream=stream, a0=a0, a1=a1, n1=n1):
            e0 = flat // (n1 - 1)
            d1 = flat % (n1 - 1) + 1
            wait_in(stream, 1, flat, shifted(shifted(mine, a0, e0), a1, d1))
            for copy in phase_two_copy(stream, e0, d1):
                copy.start()
            return carry

        lax.fori_loop(0, n0 * (n1 - 1), forward, 0)
    for stream in range(streams):
        a0, a1, a2 = ORDERS[stream]
        n0, n1, n2 = sizes[a0], sizes[a1], sizes[a2]

        def wait_plane(flat, carry, stream=stream, a0=a0, a1=a1, a2=a2, n1=n1, n2=n2):
            block = shifted(shifted(mine, a0, flat // n1), a1, flat % n1)
            for d2 in range(1, n2):
                wait_in(stream, 2, flat * (n2 - 1) + d2 - 1, shifted(block, a2, d2))
            return carry

        lax.fori_loop(0, n0 * n1, wait_plane, 0)
    for copy in sent:
        copy.wait_send()
    for stream in range(streams):
        a0, a1, _ = ORDERS[stream]
        n0, n1 = sizes[a0], sizes[a1]

        def drain(flat, carry, stream=stream, n1=n1):
            for copy in phase_two_copy(stream, flat // (n1 - 1), flat % (n1 - 1) + 1):
                copy.wait_send()
            return carry

        lax.fori_loop(0, n0 * (n1 - 1), drain, 0)

    chips, rows, width = out_ref.shape
    group = max(1, 128 // rows)

    def project(index, carry):
        held = out_ref[pl.ds(index * group, group)].reshape(group * rows, width)
        result_ref[pl.ds(index * group * rows, group * rows), :] = jnp.dot(
            held, weight_ref[...], preferred_element_type=jnp.float32
        )
        return carry

    lax.fori_loop(0, chips // group, project, 0)


def gather_and_project(block, weight, chips):
    side_len = round(chips ** (1.0 / 3.0))
    sizes = (side_len, side_len, side_len)
    rows, cols = block.shape
    tiles = cols // 128
    cuts = [0, (tiles + 2) // 3 * 128, (2 * tiles + 2) // 3 * 128, cols]
    slots = side_len * side_len * (side_len - 1)
    return pl.pallas_call(
        functools.partial(_gather_kernel, sizes, cuts, slots),
        out_shape=jax.ShapeDtypeStruct((chips * rows, weight.shape[1]), jnp.float32),
        in_specs=[pl.BlockSpec(memory_space=pltpu.VMEM), pl.BlockSpec(memory_space=pltpu.VMEM)],
        out_specs=pl.BlockSpec(memory_space=pltpu.VMEM),
        scratch_shapes=[
            pltpu.VMEM((chips, rows, cols), block.dtype),
            pltpu.SemaphoreType.DMA(()),
            pltpu.SemaphoreType.DMA((9 * slots,)),
            pltpu.SemaphoreType.DMA((9 * slots,)),
        ],
        compiler_params=pltpu.CompilerParams(
            collective_id=0, has_side_effects=True, vmem_limit_bytes=48 * 1024 * 1024
        ),
    )(block, weight)

def on_device(
    queries,
    latent_cache,
    lengths,
    value_lift,
    output_map,
    residual,
    norm_gain,
    expert_ids,
    gate_values,
    expert_in,
    expert_down,
):
    request_count = queries.shape[0]
    latent_width = value_lift.shape[1]
    half_heads = value_lift.shape[0]
    value_width = value_lift.shape[2]
    half_slots = latent_cache.shape[1]
    model_width = residual.shape[1]
    side_index = lax.axis_index("side")
    swap = [(0, 1), (1, 0)]
    partner_in, partner_down = lax.ppermute((expert_in, expert_down), "side", swap)
    score_scale = QKD ** (-0.5)
    scores = (
        jnp.einsum("rhc,rpc->rhp", queries, latent_cache, preferred_element_type=jnp.float32)
        * score_scale
    )
    positions = side_index * half_slots + jnp.arange(half_slots, dtype=jnp.int32)
    usable = (positions[None, :] < lengths[:, None])[:, None, :]
    masked = jnp.where(usable, scores, -1e30)
    swap = [(0, 1), (1, 0)]
    local_top = jnp.max(masked, axis=2)
    row_top = jnp.maximum(local_top, lax.ppermute(local_top, "side", swap))
    raised = jnp.where(usable, jnp.exp(masked - row_top[:, :, None]), 0.0)
    local_total = jnp.sum(raised, axis=2)
    probabilities = raised.astype(jnp.bfloat16)
    local_latent = jnp.einsum(
        "rhp,rpc->rhc",
        probabilities,
        latent_cache[:, :, :latent_width],
        preferred_element_type=jnp.float32,
    )
    other_index = 1 - side_index
    own_latent = lax.dynamic_slice_in_dim(local_latent, side_index * half_heads, half_heads, 1)
    own_total = lax.dynamic_slice_in_dim(local_total, side_index * half_heads, half_heads, 1)
    sent_latent = lax.dynamic_slice_in_dim(local_latent, other_index * half_heads, half_heads, 1)
    sent_total = lax.dynamic_slice_in_dim(local_total, other_index * half_heads, half_heads, 1)
    got_latent, got_total = lax.ppermute((sent_latent, sent_total), "side", swap)
    row_total = own_total + got_total
    latent_sum = own_latent + got_latent
    own_heads = (latent_sum / row_total[:, :, None]).astype(jnp.bfloat16)
    head_values = jnp.einsum(
        "rhc,hcv->rhv", own_heads, value_lift, preferred_element_type=jnp.float32
    )
    head_values = head_values.astype(jnp.bfloat16).reshape(request_count, half_heads * value_width)
    partial_columns = gather_and_project(head_values, output_map, lax.axis_size("dev"))
    partial_columns, partner_in, partner_down = lax.optimization_barrier(
        (partial_columns, partner_in, partner_down)
    )
    half_requests = partial_columns.shape[0] // 2
    kept_columns = lax.dynamic_slice_in_dim(partial_columns, side_index * half_requests, half_requests, 0)
    sent_columns = lax.dynamic_slice_in_dim(partial_columns, other_index * half_requests, half_requests, 0)
    got_columns = lax.ppermute(sent_columns.astype(jnp.bfloat16), "side", swap)
    summed_columns = kept_columns + got_columns.astype(jnp.float32)
    attention = lax.all_to_all(summed_columns, "dev", split_axis=0, concat_axis=1, tiled=True)
    gate_up_local = expert_in.reshape(model_width, -1)
    gate_up_partner = partner_in.reshape(model_width, -1)
    attention, gate_up_local, gate_up_partner = lax.optimization_barrier(
        (attention, gate_up_local, gate_up_partner)
    )
    hidden = (residual.astype(jnp.float32) + attention).astype(jnp.bfloat16)
    hidden_wide = hidden.astype(jnp.float32)
    normed = hidden_wide * lax.rsqrt(
        jnp.mean(hidden_wide * hidden_wide, axis=1, keepdims=True) + 1e-06
    )
    normed = (normed * norm_gain.astype(jnp.float32)[None, :]).astype(jnp.bfloat16)
    token_count = expert_ids.shape[0]
    route_count = expert_ids.shape[1]
    experts = lax.axis_size("dev") // 2
    capacity = max(4, token_count * route_count // experts)
    flat_ids = expert_ids.reshape(-1)
    expert_hits = (flat_ids[:, None] == jnp.arange(experts, dtype=jnp.int32)[None, :]).astype(
        jnp.int32
    )
    before = jnp.cumsum(expert_hits, axis=0) - expert_hits
    slot_index = jnp.sum(before * expert_hits, axis=1).reshape(token_count, route_count)
    slot_code = expert_ids * capacity + slot_index
    slot_table = jnp.arange(experts * capacity, dtype=jnp.int32)
    slot_match = slot_code[None, :, :] == slot_table[:, None, None]
    dispatch_matrix = jnp.any(slot_match, axis=2).astype(jnp.bfloat16)
    combine_matrix = jnp.sum(jnp.where(slot_match, gate_values[None, :, :], 0.0), axis=2).T
    dispatch_cube = dispatch_matrix.reshape(experts, capacity, token_count)
    outgoing = jnp.einsum(
        "sct,td->csd", dispatch_cube, normed, preferred_element_type=jnp.float32
    ).astype(jnp.bfloat16)
    quarter_width = expert_in.shape[3]
    down_local = expert_down[0]
    chips = lax.axis_size("dev")
    spread = jnp.broadcast_to(outgoing[:, :, None], (capacity, experts, chips // experts, model_width))
    spread = spread.reshape(capacity, chips, model_width)
    arrivals = lax.all_to_all(spread, "dev", split_axis=1, concat_axis=1, tiled=True)
    flat_rows = arrivals.reshape(capacity * chips, model_width)

    def expert_part(gate_up_weights, down_weights):
        gate_up = jnp.dot(flat_rows, gate_up_weights, preferred_element_type=jnp.float32)
        activated = (
            jax.nn.silu(gate_up[:, :quarter_width]) * gate_up[:, quarter_width:]
        ).astype(jnp.bfloat16)
        return jnp.dot(activated, down_weights, preferred_element_type=jnp.float32)

    summed = (
        expert_part(gate_up_local, down_local) + expert_part(gate_up_partner, partner_down[0])
    ).astype(jnp.bfloat16).reshape(capacity, chips, model_width)
    returned = lax.all_to_all(summed, "dev", split_axis=1, concat_axis=1, tiled=True)
    expert_out = jnp.sum(
        returned.reshape(capacity, experts, chips // experts, model_width).astype(jnp.float32),
        axis=2,
    ).astype(jnp.bfloat16)
    combine_cube = combine_matrix.reshape(token_count, experts, capacity)
    routed_sum = jnp.einsum(
        "tsc,csd->td",
        combine_cube,
        expert_out.astype(jnp.float32),
        precision=lax.Precision.HIGHEST,
    )
    return (hidden.astype(jnp.float32) + routed_sum).astype(jnp.bfloat16)


def solution(mesh):
    in_specs = (
        P("dev", None, None),
        P("dev", "side", None),
        P("dev"),
        P("side", None, None),
        P("side", "dev"),
        P(("side", "dev"), None),
        P(),
        P(("side", "dev"), None),
        P(("side", "dev"), None),
        P("dev", None, None, "side"),
        P("dev", "side", None),
    )
    out_specs = P(("side", "dev"), None)
    return jax.shard_map(
        on_device, mesh=mesh, in_specs=in_specs, out_specs=out_specs, check_vma=False
    )
```

```python
import jax
import jax.numpy as jnp
from jax import lax
from jax.sharding import PartitionSpec as P

QKD = 192

import functools

from jax.experimental import pallas as pl
from jax.experimental.pallas import tpu as pltpu

MESH_ID = pl.DeviceIdType.MESH
ORDERS = ((2, 0, 1), (0, 1, 2), (1, 2, 0))


def _gather_kernel(
    sizes, col_cuts, slots, block_ref, weight_ref, result_ref, out_ref, own_sem, send_sems, recv_sems
):
    side = lax.axis_index("side")
    me = lax.axis_index("dev")
    count_y, count_z, count_x = sizes
    mine = (me // (count_z * count_x), (me // count_x) % count_z, me % count_x)

    def chip(coords):
        return (coords[0] * count_z + coords[1]) * count_x + coords[2]

    def shifted(base, axis, offset):
        coords = list(base)
        coords[axis] = (coords[axis] + offset) % sizes[axis]
        return tuple(coords)

    barrier = pltpu.get_barrier_semaphore()
    peers = 0
    for axis in range(3):
        for offset in range(1, sizes[axis]):
            pl.semaphore_signal(
                barrier, 1, device_id=(side, chip(shifted(mine, axis, offset))), device_id_type=MESH_ID
            )
            peers += 1
    pl.semaphore_wait(barrier, peers)

    own = pltpu.make_async_copy(block_ref, out_ref.at[me], own_sem)
    own.start()
    streams = len(col_cuts) - 1
    sent = []

    def sem_at(stream, phase, index):
        return (stream * 3 + phase) * slots + index

    def remote(stream, phase, index, block_coords, target, from_input=False):
        cols = pl.ds(col_cuts[stream], col_cuts[stream + 1] - col_cuts[stream])
        at = sem_at(stream, phase, index)
        if from_input:
            src = block_ref.at[:, cols]
        else:
            src = out_ref.at[chip(block_coords), :, cols]
        return pltpu.make_async_remote_copy(
            src_ref=src,
            dst_ref=out_ref.at[chip(block_coords), :, cols],
            send_sem=send_sems.at[at],
            recv_sem=recv_sems.at[at],
            device_id=(side, chip(target)),
            device_id_type=MESH_ID,
        )

    def wait_in(stream, phase, index, block_coords):
        remote(stream, phase, index, block_coords, mine).wait_recv()

    def phase_one_copy(stream, e0, from_input=False):
        a0, a1, _ = ORDERS[stream]
        n1 = sizes[a1]
        for step in range(1, n1):
            index = e0 * (n1 - 1) + (n1 - step) - 1
            yield remote(stream, 1, index, shifted(mine, a0, e0), shifted(mine, a1, step), from_input)

    def phase_two_copy(stream, e0, e1, from_input=False):
        a0, a1, a2 = ORDERS[stream]
        n1, n2 = sizes[a1], sizes[a2]
        block = shifted(shifted(mine, a0, e0), a1, e1)
        for step in range(1, n2):
            index = (e0 * n1 + e1) * (n2 - 1) + (n2 - step) - 1
            yield remote(stream, 2, index, block, shifted(mine, a2, step), from_input)

    def start_all(copies):
        for copy in copies:
            copy.start()
            sent.append(copy)

    for stream in range(streams):
        a0 = ORDERS[stream][0]
        n0 = sizes[a0]
        for step in range(1, n0):
            copy = remote(stream, 0, n0 - step - 1, mine, shifted(mine, a0, step), True)
            copy.start()
            sent.append(copy)
        start_all(phase_one_copy(stream, 0, True))
        start_all(phase_two_copy(stream, 0, 0, True))
    own.wait()
    for stream in range(streams):
        a0 = ORDERS[stream][0]
        for d0 in range(1, sizes[a0]):
            wait_in(stream, 0, d0 - 1, shifted(mine, a0, d0))
            start_all(phase_one_copy(stream, d0))
            start_all(phase_two_copy(stream, d0, 0))
    for stream in range(streams):
        a0, a1, _ = ORDERS[stream]
        n0, n1 = sizes[a0], sizes[a1]

        def forward(flat, carry, stream=stream, a0=a0, a1=a1, n1=n1):
            e0 = flat // (n1 - 1)
            d1 = flat % (n1 - 1) + 1
            wait_in(stream, 1, flat, shifted(shifted(mine, a0, e0), a1, d1))
            for copy in phase_two_copy(stream, e0, d1):
                copy.start()
            return carry

        lax.fori_loop(0, n0 * (n1 - 1), forward, 0)
    for stream in range(streams):
        a0, a1, a2 = ORDERS[stream]
        n0, n1, n2 = sizes[a0], sizes[a1], sizes[a2]

        def wait_plane(flat, carry, stream=stream, a0=a0, a1=a1, a2=a2, n1=n1, n2=n2):
            block = shifted(shifted(mine, a0, flat // n1), a1, flat % n1)
            for d2 in range(1, n2):
                wait_in(stream, 2, flat * (n2 - 1) + d2 - 1, shifted(block, a2, d2))
            return carry

        lax.fori_loop(0, n0 * n1, wait_plane, 0)
    for copy in sent:
        copy.wait_send()
    for stream in range(streams):
        a0, a1, _ = ORDERS[stream]
        n0, n1 = sizes[a0], sizes[a1]

        def drain(flat, carry, stream=stream, n1=n1):
            for copy in phase_two_copy(stream, flat // (n1 - 1), flat % (n1 - 1) + 1):
                copy.wait_send()
            return carry

        lax.fori_loop(0, n0 * (n1 - 1), drain, 0)

    chips, rows, width = out_ref.shape
    group = max(1, 128 // rows)

    def project(index, carry):
        held = out_ref[pl.ds(index * group, group)].reshape(group * rows, width)
        result_ref[pl.ds(index * group * rows, group * rows), :] = jnp.dot(
            held, weight_ref[...], preferred_element_type=jnp.float32
        )
        return carry

    lax.fori_loop(0, chips // group, project, 0)


def gather_and_project(block, weight, chips):
    side_len = round(chips ** (1.0 / 3.0))
    sizes = (side_len, side_len, side_len)
    rows, cols = block.shape
    tiles = cols // 128
    cuts = [0, (tiles + 2) // 3 * 128, (2 * tiles + 2) // 3 * 128, cols]
    slots = side_len * side_len * (side_len - 1)
    return pl.pallas_call(
        functools.partial(_gather_kernel, sizes, cuts, slots),
        out_shape=jax.ShapeDtypeStruct((chips * rows, weight.shape[1]), jnp.float32),
        in_specs=[pl.BlockSpec(memory_space=pltpu.VMEM), pl.BlockSpec(memory_space=pltpu.VMEM)],
        out_specs=pl.BlockSpec(memory_space=pltpu.VMEM),
        scratch_shapes=[
            pltpu.VMEM((chips, rows, cols), block.dtype),
            pltpu.SemaphoreType.DMA(()),
            pltpu.SemaphoreType.DMA((9 * slots,)),
            pltpu.SemaphoreType.DMA((9 * slots,)),
        ],
        compiler_params=pltpu.CompilerParams(
            collective_id=0, has_side_effects=True, vmem_limit_bytes=48 * 1024 * 1024
        ),
    )(block, weight)

def on_device(
    queries,
    latent_cache,
    lengths,
    value_lift,
    output_map,
    residual,
    norm_gain,
    expert_ids,
    gate_values,
    expert_in,
    expert_down,
):
    request_count = queries.shape[0]
    latent_width = value_lift.shape[1]
    half_heads = value_lift.shape[0]
    value_width = value_lift.shape[2]
    half_slots = latent_cache.shape[1]
    model_width = residual.shape[1]
    side_index = lax.axis_index("side")
    swap = [(0, 1), (1, 0)]
    score_scale = QKD ** (-0.5)
    scores = (
        jnp.einsum("rhc,rpc->rhp", queries, latent_cache, preferred_element_type=jnp.float32)
        * score_scale
    )
    positions = side_index * half_slots + jnp.arange(half_slots, dtype=jnp.int32)
    usable = (positions[None, :] < lengths[:, None])[:, None, :]
    masked = jnp.where(usable, scores, -1e30)
    swap = [(0, 1), (1, 0)]
    local_top = jnp.max(masked, axis=2)
    row_top = jnp.maximum(local_top, lax.ppermute(local_top, "side", swap))
    raised = jnp.where(usable, jnp.exp(masked - row_top[:, :, None]), 0.0)
    local_total = jnp.sum(raised, axis=2)
    probabilities = raised.astype(jnp.bfloat16)
    local_latent = jnp.einsum(
        "rhp,rpc->rhc",
        probabilities,
        latent_cache[:, :, :latent_width],
        preferred_element_type=jnp.float32,
    )
    other_index = 1 - side_index
    own_latent = lax.dynamic_slice_in_dim(local_latent, side_index * half_heads, half_heads, 1)
    own_total = lax.dynamic_slice_in_dim(local_total, side_index * half_heads, half_heads, 1)
    sent_latent = lax.dynamic_slice_in_dim(local_latent, other_index * half_heads, half_heads, 1)
    sent_total = lax.dynamic_slice_in_dim(local_total, other_index * half_heads, half_heads, 1)
    got_latent, got_total = lax.ppermute((sent_latent, sent_total), "side", swap)
    row_total = own_total + got_total
    latent_sum = own_latent + got_latent
    own_heads = (latent_sum / row_total[:, :, None]).astype(jnp.bfloat16)
    head_values = jnp.einsum(
        "rhc,hcv->rhv", own_heads, value_lift, preferred_element_type=jnp.float32
    )
    head_values = head_values.astype(jnp.bfloat16).reshape(request_count, half_heads * value_width)
    held_in, held_down, head_values = lax.optimization_barrier((expert_in, expert_down, head_values))
    partner_in, partner_down = lax.ppermute((held_in, held_down), "side", swap)
    partial_columns = gather_and_project(head_values, output_map, lax.axis_size("dev"))
    partial_columns, partner_in, partner_down = lax.optimization_barrier(
        (partial_columns, partner_in, partner_down)
    )
    half_requests = partial_columns.shape[0] // 2
    kept_columns = lax.dynamic_slice_in_dim(partial_columns, side_index * half_requests, half_requests, 0)
    sent_columns = lax.dynamic_slice_in_dim(partial_columns, other_index * half_requests, half_requests, 0)
    got_columns = lax.ppermute(sent_columns.astype(jnp.bfloat16), "side", swap)
    summed_columns = kept_columns + got_columns.astype(jnp.float32)
    attention = lax.all_to_all(summed_columns, "dev", split_axis=0, concat_axis=1, tiled=True)
    gate_up_local = expert_in.reshape(model_width, -1)
    attention, gate_up_local = lax.optimization_barrier((attention, gate_up_local))
    gate_up_partner = partner_in.reshape(model_width, -1)
    hidden = (residual.astype(jnp.float32) + attention).astype(jnp.bfloat16)
    hidden_wide = hidden.astype(jnp.float32)
    normed = hidden_wide * lax.rsqrt(
        jnp.mean(hidden_wide * hidden_wide, axis=1, keepdims=True) + 1e-06
    )
    normed = (normed * norm_gain.astype(jnp.float32)[None, :]).astype(jnp.bfloat16)
    token_count = expert_ids.shape[0]
    route_count = expert_ids.shape[1]
    experts = lax.axis_size("dev") // 2
    capacity = max(4, token_count * route_count // experts)
    flat_ids = expert_ids.reshape(-1)
    expert_hits = (flat_ids[:, None] == jnp.arange(experts, dtype=jnp.int32)[None, :]).astype(
        jnp.int32
    )
    before = jnp.cumsum(expert_hits, axis=0) - expert_hits
    slot_index = jnp.sum(before * expert_hits, axis=1).reshape(token_count, route_count)
    slot_code = expert_ids * capacity + slot_index
    slot_table = jnp.arange(experts * capacity, dtype=jnp.int32)
    slot_match = slot_code[None, :, :] == slot_table[:, None, None]
    dispatch_matrix = jnp.any(slot_match, axis=2).astype(jnp.bfloat16)
    combine_matrix = jnp.sum(jnp.where(slot_match, gate_values[None, :, :], 0.0), axis=2).T
    dispatch_cube = dispatch_matrix.reshape(experts, capacity, token_count)
    outgoing = jnp.einsum(
        "sct,td->csd", dispatch_cube, normed, preferred_element_type=jnp.float32
    ).astype(jnp.bfloat16)
    quarter_width = expert_in.shape[3]
    down_local = expert_down[0]
    chips = lax.axis_size("dev")
    spread = jnp.broadcast_to(outgoing[:, :, None], (capacity, experts, chips // experts, model_width))
    spread = spread.reshape(capacity, chips, model_width)
    arrivals = lax.all_to_all(spread, "dev", split_axis=1, concat_axis=1, tiled=True)
    flat_rows = arrivals.reshape(capacity * chips, model_width)

    def expert_part(gate_up_weights, down_weights):
        gate_up = jnp.dot(flat_rows, gate_up_weights, preferred_element_type=jnp.float32)
        activated = (
            jax.nn.silu(gate_up[:, :quarter_width]) * gate_up[:, quarter_width:]
        ).astype(jnp.bfloat16)
        return jnp.dot(activated, down_weights, preferred_element_type=jnp.float32)

    summed = (
        expert_part(gate_up_local, down_local) + expert_part(gate_up_partner, partner_down[0])
    ).astype(jnp.bfloat16).reshape(capacity, chips, model_width)
    returned = lax.all_to_all(summed, "dev", split_axis=1, concat_axis=1, tiled=True)
    expert_out = jnp.sum(
        returned.reshape(capacity, experts, chips // experts, model_width).astype(jnp.float32),
        axis=2,
    ).astype(jnp.bfloat16)
    combine_cube = combine_matrix.reshape(token_count, experts, capacity)
    routed_sum = jnp.einsum(
        "tsc,csd->td",
        combine_cube,
        expert_out.astype(jnp.float32),
        precision=lax.Precision.HIGHEST,
    )
    return (hidden.astype(jnp.float32) + routed_sum).astype(jnp.bfloat16)


def solution(mesh):
    in_specs = (
        P("dev", None, None),
        P("dev", "side", None),
        P("dev"),
        P("side", None, None),
        P("side", "dev"),
        P(("side", "dev"), None),
        P(),
        P(("side", "dev"), None),
        P(("side", "dev"), None),
        P("dev", None, None, "side"),
        P("dev", "side", None),
    )
    out_specs = P(("side", "dev"), None)
    return jax.shard_map(
        on_device, mesh=mesh, in_specs=in_specs, out_specs=out_specs, check_vma=False
    )
```

```python
import jax
import jax.numpy as jnp
from jax import lax
from jax.sharding import PartitionSpec as P

QKD = 192

import functools

from jax.experimental import pallas as pl
from jax.experimental.pallas import tpu as pltpu

MESH_ID = pl.DeviceIdType.MESH
ORDERS = ((2, 0, 1), (0, 1, 2), (1, 2, 0))


def _gather_kernel(
    sizes, col_cuts, slots, block_ref, weight_ref, result_ref, out_ref, own_sem, send_sems, recv_sems
):
    side = lax.axis_index("side")
    me = lax.axis_index("dev")
    count_y, count_z, count_x = sizes
    mine = (me // (count_z * count_x), (me // count_x) % count_z, me % count_x)

    def chip(coords):
        return (coords[0] * count_z + coords[1]) * count_x + coords[2]

    def shifted(base, axis, offset):
        coords = list(base)
        coords[axis] = (coords[axis] + offset) % sizes[axis]
        return tuple(coords)

    barrier = pltpu.get_barrier_semaphore()
    peers = 0
    for axis in range(3):
        for offset in range(1, sizes[axis]):
            pl.semaphore_signal(
                barrier, 1, device_id=(side, chip(shifted(mine, axis, offset))), device_id_type=MESH_ID
            )
            peers += 1
    pl.semaphore_wait(barrier, peers)

    own = pltpu.make_async_copy(block_ref, out_ref.at[me], own_sem)
    own.start()
    streams = len(col_cuts) - 1
    sent = []

    def sem_at(stream, phase, index):
        return (stream * 3 + phase) * slots + index

    def remote(stream, phase, index, block_coords, target, from_input=False):
        cols = pl.ds(col_cuts[stream], col_cuts[stream + 1] - col_cuts[stream])
        at = sem_at(stream, phase, index)
        if from_input:
            src = block_ref.at[:, cols]
        else:
            src = out_ref.at[chip(block_coords), :, cols]
        return pltpu.make_async_remote_copy(
            src_ref=src,
            dst_ref=out_ref.at[chip(block_coords), :, cols],
            send_sem=send_sems.at[at],
            recv_sem=recv_sems.at[at],
            device_id=(side, chip(target)),
            device_id_type=MESH_ID,
        )

    def wait_in(stream, phase, index, block_coords):
        remote(stream, phase, index, block_coords, mine).wait_recv()

    def phase_one_copy(stream, e0, from_input=False):
        a0, a1, _ = ORDERS[stream]
        n1 = sizes[a1]
        for step in range(1, n1):
            index = e0 * (n1 - 1) + (n1 - step) - 1
            yield remote(stream, 1, index, shifted(mine, a0, e0), shifted(mine, a1, step), from_input)

    def phase_two_copy(stream, e0, e1, from_input=False):
        a0, a1, a2 = ORDERS[stream]
        n1, n2 = sizes[a1], sizes[a2]
        block = shifted(shifted(mine, a0, e0), a1, e1)
        for step in range(1, n2):
            index = (e0 * n1 + e1) * (n2 - 1) + (n2 - step) - 1
            yield remote(stream, 2, index, block, shifted(mine, a2, step), from_input)

    def start_all(copies):
        for copy in copies:
            copy.start()
            sent.append(copy)

    for stream in range(streams):
        a0 = ORDERS[stream][0]
        n0 = sizes[a0]
        for step in range(1, n0):
            copy = remote(stream, 0, n0 - step - 1, mine, shifted(mine, a0, step), True)
            copy.start()
            sent.append(copy)
        start_all(phase_one_copy(stream, 0, True))
        start_all(phase_two_copy(stream, 0, 0, True))
    own.wait()
    for stream in range(streams):
        a0 = ORDERS[stream][0]
        for d0 in range(1, sizes[a0]):
            wait_in(stream, 0, d0 - 1, shifted(mine, a0, d0))
            start_all(phase_one_copy(stream, d0))
            start_all(phase_two_copy(stream, d0, 0))
    for stream in range(streams):
        a0, a1, _ = ORDERS[stream]
        n0, n1 = sizes[a0], sizes[a1]

        def forward(flat, carry, stream=stream, a0=a0, a1=a1, n1=n1):
            e0 = flat // (n1 - 1)
            d1 = flat % (n1 - 1) + 1
            wait_in(stream, 1, flat, shifted(shifted(mine, a0, e0), a1, d1))
            for copy in phase_two_copy(stream, e0, d1):
                copy.start()
            return carry

        lax.fori_loop(0, n0 * (n1 - 1), forward, 0)
    for stream in range(streams):
        a0, a1, a2 = ORDERS[stream]
        n0, n1, n2 = sizes[a0], sizes[a1], sizes[a2]

        def wait_plane(flat, carry, stream=stream, a0=a0, a1=a1, a2=a2, n1=n1, n2=n2):
            block = shifted(shifted(mine, a0, flat // n1), a1, flat % n1)
            for d2 in range(1, n2):
                wait_in(stream, 2, flat * (n2 - 1) + d2 - 1, shifted(block, a2, d2))
            return carry

        lax.fori_loop(0, n0 * n1, wait_plane, 0)
    for copy in sent:
        copy.wait_send()
    for stream in range(streams):
        a0, a1, _ = ORDERS[stream]
        n0, n1 = sizes[a0], sizes[a1]

        def drain(flat, carry, stream=stream, n1=n1):
            for copy in phase_two_copy(stream, flat // (n1 - 1), flat % (n1 - 1) + 1):
                copy.wait_send()
            return carry

        lax.fori_loop(0, n0 * (n1 - 1), drain, 0)

    chips, rows, width = out_ref.shape
    group = max(1, 128 // rows)

    def project(index, carry):
        held = out_ref[pl.ds(index * group, group)].reshape(group * rows, width)
        result_ref[pl.ds(index * group * rows, group * rows), :] = jnp.dot(
            held, weight_ref[...], preferred_element_type=jnp.float32
        )
        return carry

    lax.fori_loop(0, chips // group, project, 0)


def gather_and_project(block, weight, chips):
    side_len = round(chips ** (1.0 / 3.0))
    sizes = (side_len, side_len, side_len)
    rows, cols = block.shape
    tiles = cols // 128
    cuts = [0, (tiles + 2) // 3 * 128, (2 * tiles + 2) // 3 * 128, cols]
    slots = side_len * side_len * (side_len - 1)
    return pl.pallas_call(
        functools.partial(_gather_kernel, sizes, cuts, slots),
        out_shape=jax.ShapeDtypeStruct((chips * rows, weight.shape[1]), jnp.float32),
        in_specs=[pl.BlockSpec(memory_space=pltpu.VMEM), pl.BlockSpec(memory_space=pltpu.VMEM)],
        out_specs=pl.BlockSpec(memory_space=pltpu.VMEM),
        scratch_shapes=[
            pltpu.VMEM((chips, rows, cols), block.dtype),
            pltpu.SemaphoreType.DMA(()),
            pltpu.SemaphoreType.DMA((9 * slots,)),
            pltpu.SemaphoreType.DMA((9 * slots,)),
        ],
        compiler_params=pltpu.CompilerParams(
            collective_id=0, has_side_effects=True, vmem_limit_bytes=48 * 1024 * 1024
        ),
    )(block, weight)

def on_device(
    queries,
    latent_cache,
    lengths,
    value_lift,
    output_map,
    residual,
    norm_gain,
    expert_ids,
    gate_values,
    expert_in,
    expert_down,
):
    request_count = queries.shape[0]
    latent_width = value_lift.shape[1]
    half_heads = value_lift.shape[0]
    value_width = value_lift.shape[2]
    half_slots = latent_cache.shape[1]
    model_width = residual.shape[1]
    side_index = lax.axis_index("side")
    swap = [(0, 1), (1, 0)]
    score_scale = QKD ** (-0.5)
    scores = (
        jnp.einsum("rhc,rpc->rhp", queries, latent_cache, preferred_element_type=jnp.float32)
        * score_scale
    )
    positions = side_index * half_slots + jnp.arange(half_slots, dtype=jnp.int32)
    usable = (positions[None, :] < lengths[:, None])[:, None, :]
    masked = jnp.where(usable, scores, -1e30)
    swap = [(0, 1), (1, 0)]
    local_top = jnp.max(masked, axis=2)
    row_top = jnp.maximum(local_top, lax.ppermute(local_top, "side", swap))
    raised = jnp.where(usable, jnp.exp(masked - row_top[:, :, None]), 0.0)
    local_total = jnp.sum(raised, axis=2)
    probabilities = raised.astype(jnp.bfloat16)
    local_latent = jnp.einsum(
        "rhp,rpc->rhc",
        probabilities,
        latent_cache[:, :, :latent_width],
        preferred_element_type=jnp.float32,
    )
    other_index = 1 - side_index
    own_latent = lax.dynamic_slice_in_dim(local_latent, side_index * half_heads, half_heads, 1)
    own_total = lax.dynamic_slice_in_dim(local_total, side_index * half_heads, half_heads, 1)
    sent_latent = lax.dynamic_slice_in_dim(local_latent, other_index * half_heads, half_heads, 1)
    sent_total = lax.dynamic_slice_in_dim(local_total, other_index * half_heads, half_heads, 1)
    got_latent, got_total = lax.ppermute((sent_latent, sent_total), "side", swap)
    row_total = own_total + got_total
    latent_sum = own_latent + got_latent
    own_heads = (latent_sum / row_total[:, :, None]).astype(jnp.bfloat16)
    head_values = jnp.einsum(
        "rhc,hcv->rhv", own_heads, value_lift, preferred_element_type=jnp.float32
    )
    head_values = head_values.astype(jnp.bfloat16).reshape(request_count, half_heads * value_width)
    held_in, held_down, head_values = lax.optimization_barrier((expert_in, expert_down, head_values))
    partner_in, partner_down = lax.ppermute((held_in, held_down), "side", swap)
    partial_columns = gather_and_project(head_values, output_map, lax.axis_size("dev"))
    partial_columns, partner_in, partner_down = lax.optimization_barrier(
        (partial_columns, partner_in, partner_down)
    )
    half_requests = partial_columns.shape[0] // 2
    kept_columns = lax.dynamic_slice_in_dim(partial_columns, side_index * half_requests, half_requests, 0)
    sent_columns = lax.dynamic_slice_in_dim(partial_columns, other_index * half_requests, half_requests, 0)
    got_columns = lax.ppermute(sent_columns.astype(jnp.bfloat16), "side", swap)
    summed_columns = kept_columns + got_columns.astype(jnp.float32)
    attention = lax.all_to_all(summed_columns, "dev", split_axis=0, concat_axis=1, tiled=True)
    gate_up_local = expert_in.reshape(model_width, -1)
    attention, gate_up_local = lax.optimization_barrier((attention, gate_up_local))
    gate_up_partner = partner_in.reshape(model_width, -1)
    hidden = (residual.astype(jnp.float32) + attention).astype(jnp.bfloat16)
    hidden_wide = hidden.astype(jnp.float32)
    normed = hidden_wide * lax.rsqrt(
        jnp.mean(hidden_wide * hidden_wide, axis=1, keepdims=True) + 1e-06
    )
    normed = (normed * norm_gain.astype(jnp.float32)[None, :]).astype(jnp.bfloat16)
    token_count = expert_ids.shape[0]
    route_count = expert_ids.shape[1]
    experts = lax.axis_size("dev") // 2
    capacity = max(4, token_count * route_count // experts)
    flat_ids = expert_ids.reshape(-1)
    expert_hits = (flat_ids[:, None] == jnp.arange(experts, dtype=jnp.int32)[None, :]).astype(
        jnp.int32
    )
    before = jnp.cumsum(expert_hits, axis=0) - expert_hits
    slot_index = jnp.sum(before * expert_hits, axis=1).reshape(token_count, route_count)
    slot_code = expert_ids * capacity + slot_index
    slot_table = jnp.arange(experts * capacity, dtype=jnp.int32)
    slot_match = slot_code[None, :, :] == slot_table[:, None, None]
    dispatch_matrix = jnp.any(slot_match, axis=2).astype(jnp.bfloat16)
    combine_matrix = jnp.sum(jnp.where(slot_match, gate_values[None, :, :], 0.0), axis=2).T
    dispatch_cube = dispatch_matrix.reshape(experts, capacity, token_count)
    outgoing = jnp.einsum(
        "sct,td->csd", dispatch_cube, normed, preferred_element_type=jnp.float32
    ).astype(jnp.bfloat16)
    quarter_width = expert_in.shape[3]
    down_local = expert_down[0]
    chips = lax.axis_size("dev")
    spread = jnp.broadcast_to(outgoing[:, :, None], (capacity, experts, chips // experts, model_width))
    spread = spread.reshape(capacity, chips, model_width)
    arrivals = lax.all_to_all(spread, "dev", split_axis=1, concat_axis=1, tiled=True)
    flat_rows = arrivals.reshape(capacity * chips, model_width)

    def expert_part(gate_up_weights, down_weights):
        gate_up = jnp.dot(flat_rows, gate_up_weights, preferred_element_type=jnp.float32)
        activated = (
            jax.nn.silu(gate_up[:, :quarter_width]) * gate_up[:, quarter_width:]
        ).astype(jnp.bfloat16)
        return jnp.dot(activated, down_weights, preferred_element_type=jnp.float32)

    summed = (
        expert_part(gate_up_local, down_local) + expert_part(gate_up_partner, partner_down[0])
    ).astype(jnp.bfloat16).reshape(capacity, chips, model_width)
    returned = lax.all_to_all(summed, "dev", split_axis=1, concat_axis=1, tiled=True)
    halves = chips // experts
    combine_cube = jnp.broadcast_to(
        combine_matrix.reshape(token_count, 1, experts, 1, capacity),
        (token_count, capacity, experts, halves, capacity),
    )
    slot_eye = jnp.eye(capacity, dtype=jnp.float32)[None, :, None, None, :]
    combine_full = jnp.sum(combine_cube * slot_eye, axis=4).reshape(token_count, capacity, chips)
    routed_sum = jnp.einsum(
        "tcs,csd->td",
        combine_full.astype(jnp.bfloat16),
        returned,
        preferred_element_type=jnp.float32,
    )
    return (hidden.astype(jnp.float32) + routed_sum).astype(jnp.bfloat16)


def solution(mesh):
    in_specs = (
        P("dev", None, None),
        P("dev", "side", None),
        P("dev"),
        P("side", None, None),
        P("side", "dev"),
        P(("side", "dev"), None),
        P(),
        P(("side", "dev"), None),
        P(("side", "dev"), None),
        P("dev", None, None, "side"),
        P("dev", "side", None),
    )
    out_specs = P(("side", "dev"), None)
    return jax.shard_map(
        on_device, mesh=mesh, in_specs=in_specs, out_specs=out_specs, check_vma=False
    )
```

```python
import jax
import jax.numpy as jnp
from jax import lax
from jax.sharding import PartitionSpec as P

QKD = 192

import functools

from jax.experimental import pallas as pl
from jax.experimental.pallas import tpu as pltpu

MESH_ID = pl.DeviceIdType.MESH
ORDERS = ((2, 0, 1), (0, 1, 2), (1, 2, 0))


def _gather_kernel(
    sizes, col_cuts, slots, block_ref, weight_ref, result_ref, out_ref, own_sem, send_sems, recv_sems
):
    side = lax.axis_index("side")
    me = lax.axis_index("dev")
    count_y, count_z, count_x = sizes
    mine = (me // (count_z * count_x), (me // count_x) % count_z, me % count_x)

    def chip(coords):
        return (coords[0] * count_z + coords[1]) * count_x + coords[2]

    def shifted(base, axis, offset):
        coords = list(base)
        coords[axis] = (coords[axis] + offset) % sizes[axis]
        return tuple(coords)

    barrier = pltpu.get_barrier_semaphore()
    peers = 0
    for axis in range(3):
        for offset in range(1, sizes[axis]):
            pl.semaphore_signal(
                barrier, 1, device_id=(side, chip(shifted(mine, axis, offset))), device_id_type=MESH_ID
            )
            peers += 1
    pl.semaphore_wait(barrier, peers)

    own = pltpu.make_async_copy(block_ref, out_ref.at[me], own_sem)
    own.start()
    streams = len(col_cuts) - 1
    sent = []

    def sem_at(stream, phase, index):
        return (stream * 3 + phase) * slots + index

    def remote(stream, phase, index, block_coords, target, from_input=False):
        cols = pl.ds(col_cuts[stream], col_cuts[stream + 1] - col_cuts[stream])
        at = sem_at(stream, phase, index)
        if from_input:
            src = block_ref.at[:, cols]
        else:
            src = out_ref.at[chip(block_coords), :, cols]
        return pltpu.make_async_remote_copy(
            src_ref=src,
            dst_ref=out_ref.at[chip(block_coords), :, cols],
            send_sem=send_sems.at[at],
            recv_sem=recv_sems.at[at],
            device_id=(side, chip(target)),
            device_id_type=MESH_ID,
        )

    def wait_in(stream, phase, index, block_coords):
        remote(stream, phase, index, block_coords, mine).wait_recv()

    def phase_one_copy(stream, e0, from_input=False):
        a0, a1, _ = ORDERS[stream]
        n1 = sizes[a1]
        for step in range(1, n1):
            index = e0 * (n1 - 1) + (n1 - step) - 1
            yield remote(stream, 1, index, shifted(mine, a0, e0), shifted(mine, a1, step), from_input)

    def phase_two_copy(stream, e0, e1, from_input=False):
        a0, a1, a2 = ORDERS[stream]
        n1, n2 = sizes[a1], sizes[a2]
        block = shifted(shifted(mine, a0, e0), a1, e1)
        for step in range(1, n2):
            index = (e0 * n1 + e1) * (n2 - 1) + (n2 - step) - 1
            yield remote(stream, 2, index, block, shifted(mine, a2, step), from_input)

    def start_all(copies):
        for copy in copies:
            copy.start()
            sent.append(copy)

    for stream in range(streams):
        a0 = ORDERS[stream][0]
        n0 = sizes[a0]
        for step in range(1, n0):
            copy = remote(stream, 0, n0 - step - 1, mine, shifted(mine, a0, step), True)
            copy.start()
            sent.append(copy)
        start_all(phase_one_copy(stream, 0, True))
        start_all(phase_two_copy(stream, 0, 0, True))
    own.wait()
    for stream in range(streams):
        a0 = ORDERS[stream][0]
        for d0 in range(1, sizes[a0]):
            wait_in(stream, 0, d0 - 1, shifted(mine, a0, d0))
            start_all(phase_one_copy(stream, d0))
            start_all(phase_two_copy(stream, d0, 0))
    for stream in range(streams):
        a0, a1, _ = ORDERS[stream]
        n0, n1 = sizes[a0], sizes[a1]

        def forward(flat, carry, stream=stream, a0=a0, a1=a1, n1=n1):
            e0 = flat // (n1 - 1)
            d1 = flat % (n1 - 1) + 1
            wait_in(stream, 1, flat, shifted(shifted(mine, a0, e0), a1, d1))
            for copy in phase_two_copy(stream, e0, d1):
                copy.start()
            return carry

        lax.fori_loop(0, n0 * (n1 - 1), forward, 0)
    for stream in range(streams):
        a0, a1, a2 = ORDERS[stream]
        n0, n1, n2 = sizes[a0], sizes[a1], sizes[a2]

        def wait_plane(flat, carry, stream=stream, a0=a0, a1=a1, a2=a2, n1=n1, n2=n2):
            block = shifted(shifted(mine, a0, flat // n1), a1, flat % n1)
            for d2 in range(1, n2):
                wait_in(stream, 2, flat * (n2 - 1) + d2 - 1, shifted(block, a2, d2))
            return carry

        lax.fori_loop(0, n0 * n1, wait_plane, 0)
    for copy in sent:
        copy.wait_send()
    for stream in range(streams):
        a0, a1, _ = ORDERS[stream]
        n0, n1 = sizes[a0], sizes[a1]

        def drain(flat, carry, stream=stream, n1=n1):
            for copy in phase_two_copy(stream, flat // (n1 - 1), flat % (n1 - 1) + 1):
                copy.wait_send()
            return carry

        lax.fori_loop(0, n0 * (n1 - 1), drain, 0)

    chips, rows, width = out_ref.shape
    group = max(1, 128 // rows)

    def project(index, carry):
        held = out_ref[pl.ds(index * group, group)].reshape(group * rows, width)
        result_ref[pl.ds(index * group * rows, group * rows), :] = jnp.dot(
            held, weight_ref[...], preferred_element_type=jnp.float32
        )
        return carry

    lax.fori_loop(0, chips // group, project, 0)


def gather_and_project(block, weight, chips):
    side_len = round(chips ** (1.0 / 3.0))
    sizes = (side_len, side_len, side_len)
    rows, cols = block.shape
    tiles = cols // 128
    cuts = [0, (tiles + 2) // 3 * 128, (2 * tiles + 2) // 3 * 128, cols]
    slots = side_len * side_len * (side_len - 1)
    return pl.pallas_call(
        functools.partial(_gather_kernel, sizes, cuts, slots),
        out_shape=jax.ShapeDtypeStruct((chips * rows, weight.shape[1]), jnp.float32),
        in_specs=[pl.BlockSpec(memory_space=pltpu.VMEM), pl.BlockSpec(memory_space=pltpu.VMEM)],
        out_specs=pl.BlockSpec(memory_space=pltpu.VMEM),
        scratch_shapes=[
            pltpu.VMEM((chips, rows, cols), block.dtype),
            pltpu.SemaphoreType.DMA(()),
            pltpu.SemaphoreType.DMA((9 * slots,)),
            pltpu.SemaphoreType.DMA((9 * slots,)),
        ],
        compiler_params=pltpu.CompilerParams(
            collective_id=0, has_side_effects=True, vmem_limit_bytes=48 * 1024 * 1024
        ),
    )(block, weight)

def on_device(
    queries,
    latent_cache,
    lengths,
    value_lift,
    output_map,
    residual,
    norm_gain,
    expert_ids,
    gate_values,
    expert_in,
    expert_down,
):
    request_count = queries.shape[0]
    latent_width = value_lift.shape[1]
    half_heads = value_lift.shape[0]
    value_width = value_lift.shape[2]
    half_slots = latent_cache.shape[1]
    model_width = residual.shape[1]
    side_index = lax.axis_index("side")
    swap = [(0, 1), (1, 0)]
    score_scale = QKD ** (-0.5)
    scores = (
        jnp.einsum("rhc,rpc->rhp", queries, latent_cache, preferred_element_type=jnp.float32)
        * score_scale
    )
    positions = side_index * half_slots + jnp.arange(half_slots, dtype=jnp.int32)
    usable = (positions[None, :] < lengths[:, None])[:, None, :]
    masked = jnp.where(usable, scores, -1e30)
    swap = [(0, 1), (1, 0)]
    local_top = jnp.max(masked, axis=2)
    row_top = jnp.maximum(local_top, lax.ppermute(local_top, "side", swap))
    raised = jnp.where(usable, jnp.exp(masked - row_top[:, :, None]), 0.0)
    local_total = jnp.sum(raised, axis=2)
    probabilities = raised.astype(jnp.bfloat16)
    local_latent = jnp.einsum(
        "rhp,rpc->rhc",
        probabilities,
        latent_cache[:, :, :latent_width],
        preferred_element_type=jnp.float32,
    )
    other_index = 1 - side_index
    own_latent = lax.dynamic_slice_in_dim(local_latent, side_index * half_heads, half_heads, 1)
    own_total = lax.dynamic_slice_in_dim(local_total, side_index * half_heads, half_heads, 1)
    sent_latent = lax.dynamic_slice_in_dim(local_latent, other_index * half_heads, half_heads, 1)
    sent_total = lax.dynamic_slice_in_dim(local_total, other_index * half_heads, half_heads, 1)
    got_latent, got_total = lax.ppermute((sent_latent, sent_total), "side", swap)
    row_total = own_total + got_total
    latent_sum = own_latent + got_latent
    own_heads = (latent_sum / row_total[:, :, None]).astype(jnp.bfloat16)
    head_values = jnp.einsum(
        "rhc,hcv->rhv", own_heads, value_lift, preferred_element_type=jnp.float32
    )
    head_values = head_values.astype(jnp.bfloat16).reshape(request_count, half_heads * value_width)
    held_in, held_down, head_values = lax.optimization_barrier((expert_in, expert_down, head_values))
    partner_in, partner_down = lax.ppermute((held_in, held_down), "side", swap)
    partial_columns = gather_and_project(head_values, output_map, lax.axis_size("dev"))
    partial_columns, partner_in, partner_down = lax.optimization_barrier(
        (partial_columns, partner_in, partner_down)
    )
    half_requests = partial_columns.shape[0] // 2
    kept_columns = lax.dynamic_slice_in_dim(partial_columns, side_index * half_requests, half_requests, 0)
    sent_columns = lax.dynamic_slice_in_dim(partial_columns, other_index * half_requests, half_requests, 0)
    got_columns = lax.ppermute(sent_columns.astype(jnp.bfloat16), "side", swap)
    summed_columns = kept_columns + got_columns.astype(jnp.float32)
    attention = lax.all_to_all(summed_columns, "dev", split_axis=0, concat_axis=1, tiled=True)
    gate_up_local = expert_in.reshape(model_width, -1)
    gate_up_partner = partner_in.reshape(model_width, -1)
    hidden = (residual.astype(jnp.float32) + attention).astype(jnp.bfloat16)
    hidden_wide = hidden.astype(jnp.float32)
    normed = hidden_wide * lax.rsqrt(
        jnp.mean(hidden_wide * hidden_wide, axis=1, keepdims=True) + 1e-06
    )
    normed = (normed * norm_gain.astype(jnp.float32)[None, :]).astype(jnp.bfloat16)
    token_count = expert_ids.shape[0]
    route_count = expert_ids.shape[1]
    experts = lax.axis_size("dev") // 2
    capacity = max(4, token_count * route_count // experts)
    flat_ids = expert_ids.reshape(-1)
    expert_hits = (flat_ids[:, None] == jnp.arange(experts, dtype=jnp.int32)[None, :]).astype(
        jnp.int32
    )
    before = jnp.cumsum(expert_hits, axis=0) - expert_hits
    slot_index = jnp.sum(before * expert_hits, axis=1).reshape(token_count, route_count)
    slot_code = expert_ids * capacity + slot_index
    slot_table = jnp.arange(experts * capacity, dtype=jnp.int32)
    slot_match = slot_code[None, :, :] == slot_table[:, None, None]
    dispatch_matrix = jnp.any(slot_match, axis=2).astype(jnp.bfloat16)
    combine_matrix = jnp.sum(jnp.where(slot_match, gate_values[None, :, :], 0.0), axis=2).T
    dispatch_cube = dispatch_matrix.reshape(experts, capacity, token_count)
    outgoing = jnp.einsum(
        "sct,td->csd", dispatch_cube, normed, preferred_element_type=jnp.float32
    ).astype(jnp.bfloat16)
    quarter_width = expert_in.shape[3]
    down_local = expert_down[0]
    chips = lax.axis_size("dev")
    spread = jnp.broadcast_to(outgoing[:, :, None], (capacity, experts, chips // experts, model_width))
    spread = spread.reshape(capacity, chips, model_width)
    arrivals = lax.all_to_all(spread, "dev", split_axis=1, concat_axis=1, tiled=True)
    flat_rows = arrivals.reshape(capacity * chips, model_width)

    def expert_part(gate_up_weights, down_weights):
        gate_up = jnp.dot(flat_rows, gate_up_weights, preferred_element_type=jnp.float32)
        activated = (
            jax.nn.silu(gate_up[:, :quarter_width]) * gate_up[:, quarter_width:]
        ).astype(jnp.bfloat16)
        return jnp.dot(activated, down_weights, preferred_element_type=jnp.float32)

    summed = (
        expert_part(gate_up_local, down_local) + expert_part(gate_up_partner, partner_down[0])
    ).astype(jnp.bfloat16).reshape(capacity, chips, model_width)
    returned = lax.all_to_all(summed, "dev", split_axis=1, concat_axis=1, tiled=True)
    halves = chips // experts
    combine_cube = jnp.broadcast_to(
        combine_matrix.reshape(token_count, 1, experts, 1, capacity),
        (token_count, capacity, experts, halves, capacity),
    )
    slot_eye = jnp.eye(capacity, dtype=jnp.float32)[None, :, None, None, :]
    combine_full = jnp.sum(combine_cube * slot_eye, axis=4).reshape(token_count, capacity, chips)
    routed_sum = jnp.einsum(
        "tcs,csd->td",
        combine_full.astype(jnp.bfloat16),
        returned,
        preferred_element_type=jnp.float32,
    )
    return (hidden.astype(jnp.float32) + routed_sum).astype(jnp.bfloat16)


def solution(mesh):
    in_specs = (
        P("dev", None, None),
        P("dev", "side", None),
        P("dev"),
        P("side", None, None),
        P("side", "dev"),
        P(("side", "dev"), None),
        P(),
        P(("side", "dev"), None),
        P(("side", "dev"), None),
        P("dev", None, None, "side"),
        P("dev", "side", None),
    )
    out_specs = P(("side", "dev"), None)
    return jax.shard_map(
        on_device, mesh=mesh, in_specs=in_specs, out_specs=out_specs, check_vma=False
    )
```

```python
import jax
import jax.numpy as jnp
from jax import lax
from jax.sharding import PartitionSpec as P

QKD = 192

import functools

from jax.experimental import pallas as pl
from jax.experimental.pallas import tpu as pltpu

MESH_ID = pl.DeviceIdType.MESH
ORDERS = ((2, 0, 1), (0, 1, 2), (1, 2, 0))


def _gather_kernel(
    sizes, col_cuts, slots, block_ref, weight_ref, result_ref, out_ref, own_sem, send_sems, recv_sems
):
    side = lax.axis_index("side")
    me = lax.axis_index("dev")
    count_y, count_z, count_x = sizes
    mine = (me // (count_z * count_x), (me // count_x) % count_z, me % count_x)

    def chip(coords):
        return (coords[0] * count_z + coords[1]) * count_x + coords[2]

    def shifted(base, axis, offset):
        coords = list(base)
        coords[axis] = (coords[axis] + offset) % sizes[axis]
        return tuple(coords)

    barrier = pltpu.get_barrier_semaphore()
    peers = 0
    for axis in range(3):
        for offset in range(1, sizes[axis]):
            pl.semaphore_signal(
                barrier, 1, device_id=(side, chip(shifted(mine, axis, offset))), device_id_type=MESH_ID
            )
            peers += 1
    pl.semaphore_wait(barrier, peers)

    own = pltpu.make_async_copy(block_ref, out_ref.at[me], own_sem)
    own.start()
    streams = len(col_cuts) - 1
    sent = []

    def sem_at(stream, phase, index):
        return (stream * 3 + phase) * slots + index

    def remote(stream, phase, index, block_coords, target, from_input=False):
        cols = pl.ds(col_cuts[stream], col_cuts[stream + 1] - col_cuts[stream])
        at = sem_at(stream, phase, index)
        if from_input:
            src = block_ref.at[:, cols]
        else:
            src = out_ref.at[chip(block_coords), :, cols]
        return pltpu.make_async_remote_copy(
            src_ref=src,
            dst_ref=out_ref.at[chip(block_coords), :, cols],
            send_sem=send_sems.at[at],
            recv_sem=recv_sems.at[at],
            device_id=(side, chip(target)),
            device_id_type=MESH_ID,
        )

    def wait_in(stream, phase, index, block_coords):
        remote(stream, phase, index, block_coords, mine).wait_recv()

    def phase_one_copy(stream, e0, from_input=False):
        a0, a1, _ = ORDERS[stream]
        n1 = sizes[a1]
        for step in range(1, n1):
            index = e0 * (n1 - 1) + (n1 - step) - 1
            yield remote(stream, 1, index, shifted(mine, a0, e0), shifted(mine, a1, step), from_input)

    def phase_two_copy(stream, e0, e1, from_input=False):
        a0, a1, a2 = ORDERS[stream]
        n1, n2 = sizes[a1], sizes[a2]
        block = shifted(shifted(mine, a0, e0), a1, e1)
        for step in range(1, n2):
            index = (e0 * n1 + e1) * (n2 - 1) + (n2 - step) - 1
            yield remote(stream, 2, index, block, shifted(mine, a2, step), from_input)

    def start_all(copies):
        for copy in copies:
            copy.start()
            sent.append(copy)

    for stream in range(streams):
        a0 = ORDERS[stream][0]
        n0 = sizes[a0]
        for step in range(1, n0):
            copy = remote(stream, 0, n0 - step - 1, mine, shifted(mine, a0, step), True)
            copy.start()
            sent.append(copy)
        start_all(phase_one_copy(stream, 0, True))
        start_all(phase_two_copy(stream, 0, 0, True))
    own.wait()
    for stream in range(streams):
        a0 = ORDERS[stream][0]
        for d0 in range(1, sizes[a0]):
            wait_in(stream, 0, d0 - 1, shifted(mine, a0, d0))
            start_all(phase_one_copy(stream, d0))
            start_all(phase_two_copy(stream, d0, 0))
    for stream in range(streams):
        a0, a1, _ = ORDERS[stream]
        n0, n1 = sizes[a0], sizes[a1]

        def forward(flat, carry, stream=stream, a0=a0, a1=a1, n1=n1):
            e0 = flat // (n1 - 1)
            d1 = flat % (n1 - 1) + 1
            wait_in(stream, 1, flat, shifted(shifted(mine, a0, e0), a1, d1))
            for copy in phase_two_copy(stream, e0, d1):
                copy.start()
            return carry

        lax.fori_loop(0, n0 * (n1 - 1), forward, 0)
    for stream in range(streams):
        a0, a1, a2 = ORDERS[stream]
        n0, n1, n2 = sizes[a0], sizes[a1], sizes[a2]

        def wait_plane(flat, carry, stream=stream, a0=a0, a1=a1, a2=a2, n1=n1, n2=n2):
            block = shifted(shifted(mine, a0, flat // n1), a1, flat % n1)
            for d2 in range(1, n2):
                wait_in(stream, 2, flat * (n2 - 1) + d2 - 1, shifted(block, a2, d2))
            return carry

        lax.fori_loop(0, n0 * n1, wait_plane, 0)
    for copy in sent:
        copy.wait_send()
    for stream in range(streams):
        a0, a1, _ = ORDERS[stream]
        n0, n1 = sizes[a0], sizes[a1]

        def drain(flat, carry, stream=stream, n1=n1):
            for copy in phase_two_copy(stream, flat // (n1 - 1), flat % (n1 - 1) + 1):
                copy.wait_send()
            return carry

        lax.fori_loop(0, n0 * (n1 - 1), drain, 0)

    chips, rows, width = out_ref.shape
    group = max(1, 128 // rows)

    def project(index, carry):
        held = out_ref[pl.ds(index * group, group)].reshape(group * rows, width)
        result_ref[pl.ds(index * group * rows, group * rows), :] = jnp.dot(
            held, weight_ref[...], preferred_element_type=jnp.float32
        )
        return carry

    lax.fori_loop(0, chips // group, project, 0)


def gather_and_project(block, weight, chips):
    side_len = round(chips ** (1.0 / 3.0))
    sizes = (side_len, side_len, side_len)
    rows, cols = block.shape
    tiles = cols // 128
    cuts = [0, (tiles + 2) // 3 * 128, (2 * tiles + 2) // 3 * 128, cols]
    slots = side_len * side_len * (side_len - 1)
    return pl.pallas_call(
        functools.partial(_gather_kernel, sizes, cuts, slots),
        out_shape=jax.ShapeDtypeStruct((chips * rows, weight.shape[1]), jnp.float32),
        in_specs=[pl.BlockSpec(memory_space=pltpu.VMEM), pl.BlockSpec(memory_space=pltpu.VMEM)],
        out_specs=pl.BlockSpec(memory_space=pltpu.VMEM),
        scratch_shapes=[
            pltpu.VMEM((chips, rows, cols), block.dtype),
            pltpu.SemaphoreType.DMA(()),
            pltpu.SemaphoreType.DMA((9 * slots,)),
            pltpu.SemaphoreType.DMA((9 * slots,)),
        ],
        compiler_params=pltpu.CompilerParams(
            collective_id=0, has_side_effects=True, vmem_limit_bytes=48 * 1024 * 1024
        ),
    )(block, weight)

def on_device(
    queries,
    latent_cache,
    lengths,
    value_lift,
    output_map,
    residual,
    norm_gain,
    expert_ids,
    gate_values,
    expert_in,
    expert_down,
):
    request_count = queries.shape[0]
    latent_width = value_lift.shape[1]
    half_heads = value_lift.shape[0]
    value_width = value_lift.shape[2]
    half_slots = latent_cache.shape[1]
    model_width = residual.shape[1]
    side_index = lax.axis_index("side")
    swap = [(0, 1), (1, 0)]
    score_scale = QKD ** (-0.5)
    scores = (
        jnp.einsum("rhc,rpc->rhp", queries, latent_cache, preferred_element_type=jnp.float32)
        * score_scale
    )
    positions = side_index * half_slots + jnp.arange(half_slots, dtype=jnp.int32)
    usable = (positions[None, :] < lengths[:, None])[:, None, :]
    masked = jnp.where(usable, scores, -1e30)
    swap = [(0, 1), (1, 0)]
    local_top = jnp.max(masked, axis=2)
    row_top = jnp.maximum(local_top, lax.ppermute(local_top, "side", swap))
    raised = jnp.where(usable, jnp.exp(masked - row_top[:, :, None]), 0.0)
    local_total = jnp.sum(raised, axis=2)
    probabilities = raised.astype(jnp.bfloat16)
    local_latent = jnp.einsum(
        "rhp,rpc->rhc",
        probabilities,
        latent_cache[:, :, :latent_width],
        preferred_element_type=jnp.float32,
    )
    other_index = 1 - side_index
    own_latent = lax.dynamic_slice_in_dim(local_latent, side_index * half_heads, half_heads, 1)
    own_total = lax.dynamic_slice_in_dim(local_total, side_index * half_heads, half_heads, 1)
    sent_latent = lax.dynamic_slice_in_dim(local_latent, other_index * half_heads, half_heads, 1)
    sent_total = lax.dynamic_slice_in_dim(local_total, other_index * half_heads, half_heads, 1)
    got_latent, got_total = lax.ppermute((sent_latent, sent_total), "side", swap)
    row_total = own_total + got_total
    latent_sum = own_latent + got_latent
    own_heads = (latent_sum / row_total[:, :, None]).astype(jnp.bfloat16)
    head_values = jnp.einsum(
        "rhc,hcv->rhv", own_heads, value_lift, preferred_element_type=jnp.float32
    )
    head_values = head_values.astype(jnp.bfloat16).reshape(request_count, half_heads * value_width)
    held_in, held_down, head_values = lax.optimization_barrier((expert_in, expert_down, head_values))
    partner_in, partner_down = lax.ppermute((held_in, held_down), "side", swap)
    partial_columns = gather_and_project(head_values, output_map, lax.axis_size("dev"))
    partial_columns, partner_in, partner_down = lax.optimization_barrier(
        (partial_columns, partner_in, partner_down)
    )
    half_requests = partial_columns.shape[0] // 2
    kept_columns = lax.dynamic_slice_in_dim(partial_columns, side_index * half_requests, half_requests, 0)
    sent_columns = lax.dynamic_slice_in_dim(partial_columns, other_index * half_requests, half_requests, 0)
    got_columns = lax.ppermute(sent_columns.astype(jnp.bfloat16), "side", swap)
    summed_columns = kept_columns + got_columns.astype(jnp.float32)
    attention = lax.all_to_all(
        summed_columns.astype(jnp.bfloat16), "dev", split_axis=0, concat_axis=1, tiled=True
    ).astype(jnp.float32)
    gate_up_local = expert_in.reshape(model_width, -1)
    gate_up_partner = partner_in.reshape(model_width, -1)
    hidden = (residual.astype(jnp.float32) + attention).astype(jnp.bfloat16)
    hidden_wide = hidden.astype(jnp.float32)
    normed = hidden_wide * lax.rsqrt(
        jnp.mean(hidden_wide * hidden_wide, axis=1, keepdims=True) + 1e-06
    )
    normed = (normed * norm_gain.astype(jnp.float32)[None, :]).astype(jnp.bfloat16)
    token_count = expert_ids.shape[0]
    route_count = expert_ids.shape[1]
    experts = lax.axis_size("dev") // 2
    capacity = max(4, token_count * route_count // experts)
    flat_ids = expert_ids.reshape(-1)
    expert_hits = (flat_ids[:, None] == jnp.arange(experts, dtype=jnp.int32)[None, :]).astype(
        jnp.int32
    )
    before = jnp.cumsum(expert_hits, axis=0) - expert_hits
    slot_index = jnp.sum(before * expert_hits, axis=1).reshape(token_count, route_count)
    slot_code = expert_ids * capacity + slot_index
    slot_table = jnp.arange(experts * capacity, dtype=jnp.int32)
    slot_match = slot_code[None, :, :] == slot_table[:, None, None]
    dispatch_matrix = jnp.any(slot_match, axis=2).astype(jnp.bfloat16)
    combine_matrix = jnp.sum(jnp.where(slot_match, gate_values[None, :, :], 0.0), axis=2).T
    dispatch_cube = dispatch_matrix.reshape(experts, capacity, token_count)
    outgoing = jnp.einsum(
        "sct,td->csd", dispatch_cube, normed, preferred_element_type=jnp.float32
    ).astype(jnp.bfloat16)
    quarter_width = expert_in.shape[3]
    down_local = expert_down[0]
    chips = lax.axis_size("dev")
    spread = jnp.broadcast_to(outgoing[:, :, None], (capacity, experts, chips // experts, model_width))
    spread = spread.reshape(capacity, chips, model_width)
    arrivals = lax.all_to_all(spread, "dev", split_axis=1, concat_axis=1, tiled=True)
    flat_rows = arrivals.reshape(capacity * chips, model_width)

    def expert_part(gate_up_weights, down_weights):
        gate_up = jnp.dot(flat_rows, gate_up_weights, preferred_element_type=jnp.float32)
        activated = (
            jax.nn.silu(gate_up[:, :quarter_width]) * gate_up[:, quarter_width:]
        ).astype(jnp.bfloat16)
        return jnp.dot(activated, down_weights, preferred_element_type=jnp.float32)

    summed = (
        expert_part(gate_up_local, down_local) + expert_part(gate_up_partner, partner_down[0])
    ).astype(jnp.bfloat16).reshape(capacity, chips, model_width)
    returned = lax.all_to_all(summed, "dev", split_axis=1, concat_axis=1, tiled=True)
    halves = chips // experts
    combine_cube = jnp.broadcast_to(
        combine_matrix.reshape(token_count, 1, experts, 1, capacity),
        (token_count, capacity, experts, halves, capacity),
    )
    slot_eye = jnp.eye(capacity, dtype=jnp.float32)[None, :, None, None, :]
    combine_full = jnp.sum(combine_cube * slot_eye, axis=4).reshape(token_count, capacity, chips)
    routed_sum = jnp.einsum(
        "tcs,csd->td",
        combine_full.astype(jnp.bfloat16),
        returned,
        preferred_element_type=jnp.float32,
    )
    return (hidden.astype(jnp.float32) + routed_sum).astype(jnp.bfloat16)


def solution(mesh):
    in_specs = (
        P("dev", None, None),
        P("dev", "side", None),
        P("dev"),
        P("side", None, None),
        P("side", "dev"),
        P(("side", "dev"), None),
        P(),
        P(("side", "dev"), None),
        P(("side", "dev"), None),
        P("dev", None, None, "side"),
        P("dev", "side", None),
    )
    out_specs = P(("side", "dev"), None)
    return jax.shard_map(
        on_device, mesh=mesh, in_specs=in_specs, out_specs=out_specs, check_vma=False
    )
```

```python
import jax
import jax.numpy as jnp
from jax import lax
from jax.sharding import PartitionSpec as P

QKD = 192

import functools

from jax.experimental import pallas as pl
from jax.experimental.pallas import tpu as pltpu

MESH_ID = pl.DeviceIdType.MESH
ORDERS = ((2, 0, 1), (0, 1, 2), (1, 2, 0))


def _gather_kernel(
    sizes, col_cuts, slots, block_ref, weight_ref, result_ref, out_ref, own_sem, send_sems, recv_sems
):
    side = lax.axis_index("side")
    me = lax.axis_index("dev")
    count_y, count_z, count_x = sizes
    mine = (me // (count_z * count_x), (me // count_x) % count_z, me % count_x)

    def chip(coords):
        return (coords[0] * count_z + coords[1]) * count_x + coords[2]

    def shifted(base, axis, offset):
        coords = list(base)
        coords[axis] = (coords[axis] + offset) % sizes[axis]
        return tuple(coords)

    barrier = pltpu.get_barrier_semaphore()
    peers = 0
    for axis in range(3):
        for offset in range(1, sizes[axis]):
            pl.semaphore_signal(
                barrier, 1, device_id=(side, chip(shifted(mine, axis, offset))), device_id_type=MESH_ID
            )
            peers += 1
    pl.semaphore_wait(barrier, peers)

    own = pltpu.make_async_copy(block_ref, out_ref.at[me], own_sem)
    own.start()
    streams = len(col_cuts) - 1
    sent = []

    def sem_at(stream, phase, index):
        return (stream * 3 + phase) * slots + index

    def remote(stream, phase, index, block_coords, target, from_input=False):
        cols = pl.ds(col_cuts[stream], col_cuts[stream + 1] - col_cuts[stream])
        at = sem_at(stream, phase, index)
        if from_input:
            src = block_ref.at[:, cols]
        else:
            src = out_ref.at[chip(block_coords), :, cols]
        return pltpu.make_async_remote_copy(
            src_ref=src,
            dst_ref=out_ref.at[chip(block_coords), :, cols],
            send_sem=send_sems.at[at],
            recv_sem=recv_sems.at[at],
            device_id=(side, chip(target)),
            device_id_type=MESH_ID,
        )

    def wait_in(stream, phase, index, block_coords):
        remote(stream, phase, index, block_coords, mine).wait_recv()

    def phase_one_copy(stream, e0, from_input=False):
        a0, a1, _ = ORDERS[stream]
        n1 = sizes[a1]
        for step in range(1, n1):
            index = e0 * (n1 - 1) + (n1 - step) - 1
            yield remote(stream, 1, index, shifted(mine, a0, e0), shifted(mine, a1, step), from_input)

    def phase_two_copy(stream, e0, e1, from_input=False):
        a0, a1, a2 = ORDERS[stream]
        n1, n2 = sizes[a1], sizes[a2]
        block = shifted(shifted(mine, a0, e0), a1, e1)
        for step in range(1, n2):
            index = (e0 * n1 + e1) * (n2 - 1) + (n2 - step) - 1
            yield remote(stream, 2, index, block, shifted(mine, a2, step), from_input)

    def start_all(copies):
        for copy in copies:
            copy.start()
            sent.append(copy)

    for stream in range(streams):
        a0 = ORDERS[stream][0]
        n0 = sizes[a0]
        for step in range(1, n0):
            copy = remote(stream, 0, n0 - step - 1, mine, shifted(mine, a0, step), True)
            copy.start()
            sent.append(copy)
        start_all(phase_one_copy(stream, 0, True))
        start_all(phase_two_copy(stream, 0, 0, True))
    own.wait()
    for stream in range(streams):
        a0 = ORDERS[stream][0]
        for d0 in range(1, sizes[a0]):
            wait_in(stream, 0, d0 - 1, shifted(mine, a0, d0))
            start_all(phase_one_copy(stream, d0))
            start_all(phase_two_copy(stream, d0, 0))
    for stream in range(streams):
        a0, a1, _ = ORDERS[stream]
        n0, n1 = sizes[a0], sizes[a1]

        def forward(flat, carry, stream=stream, a0=a0, a1=a1, n1=n1):
            e0 = flat // (n1 - 1)
            d1 = flat % (n1 - 1) + 1
            wait_in(stream, 1, flat, shifted(shifted(mine, a0, e0), a1, d1))
            for copy in phase_two_copy(stream, e0, d1):
                copy.start()
            return carry

        lax.fori_loop(0, n0 * (n1 - 1), forward, 0)
    for stream in range(streams):
        a0, a1, a2 = ORDERS[stream]
        n0, n1, n2 = sizes[a0], sizes[a1], sizes[a2]

        def wait_plane(flat, carry, stream=stream, a0=a0, a1=a1, a2=a2, n1=n1, n2=n2):
            block = shifted(shifted(mine, a0, flat // n1), a1, flat % n1)
            for d2 in range(1, n2):
                wait_in(stream, 2, flat * (n2 - 1) + d2 - 1, shifted(block, a2, d2))
            return carry

        lax.fori_loop(0, n0 * n1, wait_plane, 0)
    for copy in sent:
        copy.wait_send()
    for stream in range(streams):
        a0, a1, _ = ORDERS[stream]
        n0, n1 = sizes[a0], sizes[a1]

        def drain(flat, carry, stream=stream, n1=n1):
            for copy in phase_two_copy(stream, flat // (n1 - 1), flat % (n1 - 1) + 1):
                copy.wait_send()
            return carry

        lax.fori_loop(0, n0 * (n1 - 1), drain, 0)

    chips, rows, width = out_ref.shape
    group = max(1, 128 // rows)

    def project(index, carry):
        held = out_ref[pl.ds(index * group, group)].reshape(group * rows, width)
        result_ref[pl.ds(index * group * rows, group * rows), :] = jnp.dot(
            held, weight_ref[...], preferred_element_type=jnp.float32
        )
        return carry

    lax.fori_loop(0, chips // group, project, 0)


def gather_and_project(block, weight, chips):
    side_len = round(chips ** (1.0 / 3.0))
    sizes = (side_len, side_len, side_len)
    rows, cols = block.shape
    tiles = cols // 128
    cuts = [0, (tiles + 2) // 3 * 128, (2 * tiles + 2) // 3 * 128, cols]
    slots = side_len * side_len * (side_len - 1)
    return pl.pallas_call(
        functools.partial(_gather_kernel, sizes, cuts, slots),
        out_shape=jax.ShapeDtypeStruct((chips * rows, weight.shape[1]), jnp.float32),
        in_specs=[pl.BlockSpec(memory_space=pltpu.VMEM), pl.BlockSpec(memory_space=pltpu.VMEM)],
        out_specs=pl.BlockSpec(memory_space=pltpu.VMEM),
        scratch_shapes=[
            pltpu.VMEM((chips, rows, cols), block.dtype),
            pltpu.SemaphoreType.DMA(()),
            pltpu.SemaphoreType.DMA((9 * slots,)),
            pltpu.SemaphoreType.DMA((9 * slots,)),
        ],
        compiler_params=pltpu.CompilerParams(
            collective_id=0, has_side_effects=True, vmem_limit_bytes=48 * 1024 * 1024
        ),
    )(block, weight)

def on_device(
    queries,
    latent_cache,
    lengths,
    value_lift,
    output_map,
    residual,
    norm_gain,
    expert_ids,
    gate_values,
    expert_in,
    expert_down,
):
    request_count = queries.shape[0]
    latent_width = value_lift.shape[1]
    half_heads = value_lift.shape[0]
    value_width = value_lift.shape[2]
    half_slots = latent_cache.shape[1]
    model_width = residual.shape[1]
    side_index = lax.axis_index("side")
    swap = [(0, 1), (1, 0)]
    score_scale = QKD ** (-0.5)
    scores = (
        jnp.einsum("rhc,rpc->rhp", queries, latent_cache, preferred_element_type=jnp.float32)
        * score_scale
    )
    positions = side_index * half_slots + jnp.arange(half_slots, dtype=jnp.int32)
    usable = (positions[None, :] < lengths[:, None])[:, None, :]
    masked = jnp.where(usable, scores, -1e30)
    swap = [(0, 1), (1, 0)]
    local_top = jnp.max(masked, axis=2)
    row_top = jnp.maximum(local_top, lax.ppermute(local_top, "side", swap))
    raised = jnp.where(usable, jnp.exp(masked - row_top[:, :, None]), 0.0)
    local_total = jnp.sum(raised, axis=2)
    probabilities = raised.astype(jnp.bfloat16)
    local_latent = jnp.einsum(
        "rhp,rpc->rhc",
        probabilities,
        latent_cache[:, :, :latent_width],
        preferred_element_type=jnp.float32,
    )
    other_index = 1 - side_index
    own_latent = lax.dynamic_slice_in_dim(local_latent, side_index * half_heads, half_heads, 1)
    own_total = lax.dynamic_slice_in_dim(local_total, side_index * half_heads, half_heads, 1)
    sent_latent = lax.dynamic_slice_in_dim(local_latent, other_index * half_heads, half_heads, 1)
    sent_total = lax.dynamic_slice_in_dim(local_total, other_index * half_heads, half_heads, 1)
    got_latent, got_total = lax.ppermute((sent_latent, sent_total), "side", swap)
    row_total = own_total + got_total
    latent_sum = own_latent + got_latent
    own_heads = (latent_sum / row_total[:, :, None]).astype(jnp.bfloat16)
    head_values = jnp.einsum(
        "rhc,hcv->rhv", own_heads, value_lift, preferred_element_type=jnp.float32
    )
    head_values = head_values.astype(jnp.bfloat16).reshape(request_count, half_heads * value_width)
    held_in, held_down, head_values = lax.optimization_barrier((expert_in, expert_down, head_values))
    partner_in, partner_down = lax.ppermute((held_in, held_down), "side", swap)
    partial_columns = gather_and_project(head_values, output_map, lax.axis_size("dev"))
    partial_columns, partner_in, partner_down = lax.optimization_barrier(
        (partial_columns, partner_in, partner_down)
    )
    half_requests = partial_columns.shape[0] // 2
    kept_columns = lax.dynamic_slice_in_dim(partial_columns, side_index * half_requests, half_requests, 0)
    sent_columns = lax.dynamic_slice_in_dim(partial_columns, other_index * half_requests, half_requests, 0)
    got_columns = lax.ppermute(sent_columns.astype(jnp.bfloat16), "side", swap)
    summed_columns = kept_columns + got_columns.astype(jnp.float32)
    attention = lax.all_to_all(
        summed_columns.astype(jnp.bfloat16), "dev", split_axis=0, concat_axis=1, tiled=True
    ).astype(jnp.float32)
    gate_up_local = expert_in.reshape(model_width, -1)
    gate_up_partner = partner_in.reshape(model_width, -1)
    hidden = (residual.astype(jnp.float32) + attention).astype(jnp.bfloat16)
    hidden_wide = hidden.astype(jnp.float32)
    normed = hidden_wide * lax.rsqrt(
        jnp.mean(hidden_wide * hidden_wide, axis=1, keepdims=True) + 1e-06
    )
    normed = (normed * norm_gain.astype(jnp.float32)[None, :]).astype(jnp.bfloat16)
    token_count = expert_ids.shape[0]
    route_count = expert_ids.shape[1]
    experts = lax.axis_size("dev") // 2
    capacity = max(4, token_count * route_count // experts)
    flat_ids = expert_ids.reshape(-1)
    expert_hits = (flat_ids[:, None] == jnp.arange(experts, dtype=jnp.int32)[None, :]).astype(
        jnp.int32
    )
    before = jnp.cumsum(expert_hits, axis=0) - expert_hits
    slot_index = jnp.sum(before * expert_hits, axis=1).reshape(token_count, route_count)
    slot_code = expert_ids * capacity + slot_index
    slot_table = jnp.arange(experts * capacity, dtype=jnp.int32)
    slot_match = slot_code[None, :, :] == slot_table[:, None, None]
    dispatch_matrix = jnp.any(slot_match, axis=2).astype(jnp.bfloat16)
    combine_matrix = jnp.sum(jnp.where(slot_match, gate_values[None, :, :], 0.0), axis=2).T
    quarter_width = expert_in.shape[3]
    down_local = expert_down[0]
    chips = lax.axis_size("dev")
    dispatch_cube = jnp.broadcast_to(
        dispatch_matrix.reshape(experts, 1, capacity, token_count),
        (experts, chips // experts, capacity, token_count),
    ).reshape(chips, capacity, token_count)
    spread = jnp.einsum(
        "sct,td->csd", dispatch_cube, normed, preferred_element_type=jnp.float32
    ).astype(jnp.bfloat16)
    arrivals = lax.all_to_all(spread, "dev", split_axis=1, concat_axis=1, tiled=True)
    flat_rows = arrivals.reshape(capacity * chips, model_width)

    def expert_part(gate_up_weights, down_weights):
        gate_up = jnp.dot(flat_rows, gate_up_weights, preferred_element_type=jnp.float32)
        activated = (
            jax.nn.silu(gate_up[:, :quarter_width]) * gate_up[:, quarter_width:]
        ).astype(jnp.bfloat16)
        return jnp.dot(activated, down_weights, preferred_element_type=jnp.float32)

    summed = (
        expert_part(gate_up_local, down_local) + expert_part(gate_up_partner, partner_down[0])
    ).astype(jnp.bfloat16).reshape(capacity, chips, model_width)
    returned = lax.all_to_all(summed, "dev", split_axis=1, concat_axis=1, tiled=True)
    halves = chips // experts
    combine_cube = jnp.broadcast_to(
        combine_matrix.reshape(token_count, 1, experts, 1, capacity),
        (token_count, capacity, experts, halves, capacity),
    )
    slot_eye = jnp.eye(capacity, dtype=jnp.float32)[None, :, None, None, :]
    combine_full = jnp.sum(combine_cube * slot_eye, axis=4).reshape(token_count, capacity, chips)
    routed_sum = jnp.einsum(
        "tcs,csd->td",
        combine_full.astype(jnp.bfloat16),
        returned,
        preferred_element_type=jnp.float32,
    )
    return (hidden.astype(jnp.float32) + routed_sum).astype(jnp.bfloat16)


def solution(mesh):
    in_specs = (
        P("dev", None, None),
        P("dev", "side", None),
        P("dev"),
        P("side", None, None),
        P("side", "dev"),
        P(("side", "dev"), None),
        P(),
        P(("side", "dev"), None),
        P(("side", "dev"), None),
        P("dev", None, None, "side"),
        P("dev", "side", None),
    )
    out_specs = P(("side", "dev"), None)
    return jax.shard_map(
        on_device, mesh=mesh, in_specs=in_specs, out_specs=out_specs, check_vma=False
    )
```

```python
import jax
import jax.numpy as jnp
from jax import lax
from jax.sharding import PartitionSpec as P

QKD = 192

import functools

from jax.experimental import pallas as pl
from jax.experimental.pallas import tpu as pltpu

MESH_ID = pl.DeviceIdType.MESH
ORDERS = ((2, 0, 1), (0, 1, 2), (1, 2, 0))


def _gather_kernel(
    sizes, col_cuts, slots, block_ref, weight_ref, result_ref, out_ref, own_sem, send_sems, recv_sems
):
    side = lax.axis_index("side")
    me = lax.axis_index("dev")
    count_y, count_z, count_x = sizes
    mine = (me // (count_z * count_x), (me // count_x) % count_z, me % count_x)

    def chip(coords):
        return (coords[0] * count_z + coords[1]) * count_x + coords[2]

    def shifted(base, axis, offset):
        coords = list(base)
        coords[axis] = (coords[axis] + offset) % sizes[axis]
        return tuple(coords)

    barrier = pltpu.get_barrier_semaphore()
    peers = 0
    for axis in range(3):
        for offset in range(1, sizes[axis]):
            pl.semaphore_signal(
                barrier, 1, device_id=(side, chip(shifted(mine, axis, offset))), device_id_type=MESH_ID
            )
            peers += 1
    pl.semaphore_wait(barrier, peers)

    own = pltpu.make_async_copy(block_ref, out_ref.at[me], own_sem)
    own.start()
    streams = len(col_cuts) - 1
    sent = []

    def sem_at(stream, phase, index):
        return (stream * 3 + phase) * slots + index

    def remote(stream, phase, index, block_coords, target, from_input=False):
        cols = pl.ds(col_cuts[stream], col_cuts[stream + 1] - col_cuts[stream])
        at = sem_at(stream, phase, index)
        if from_input:
            src = block_ref.at[:, cols]
        else:
            src = out_ref.at[chip(block_coords), :, cols]
        return pltpu.make_async_remote_copy(
            src_ref=src,
            dst_ref=out_ref.at[chip(block_coords), :, cols],
            send_sem=send_sems.at[at],
            recv_sem=recv_sems.at[at],
            device_id=(side, chip(target)),
            device_id_type=MESH_ID,
        )

    def wait_in(stream, phase, index, block_coords):
        remote(stream, phase, index, block_coords, mine).wait_recv()

    def phase_one_copy(stream, e0, from_input=False):
        a0, a1, _ = ORDERS[stream]
        n1 = sizes[a1]
        for step in range(1, n1):
            index = e0 * (n1 - 1) + (n1 - step) - 1
            yield remote(stream, 1, index, shifted(mine, a0, e0), shifted(mine, a1, step), from_input)

    def phase_two_copy(stream, e0, e1, from_input=False):
        a0, a1, a2 = ORDERS[stream]
        n1, n2 = sizes[a1], sizes[a2]
        block = shifted(shifted(mine, a0, e0), a1, e1)
        for step in range(1, n2):
            index = (e0 * n1 + e1) * (n2 - 1) + (n2 - step) - 1
            yield remote(stream, 2, index, block, shifted(mine, a2, step), from_input)

    def start_all(copies):
        for copy in copies:
            copy.start()
            sent.append(copy)

    for stream in range(streams):
        a0 = ORDERS[stream][0]
        n0 = sizes[a0]
        for step in range(1, n0):
            copy = remote(stream, 0, n0 - step - 1, mine, shifted(mine, a0, step), True)
            copy.start()
            sent.append(copy)
        start_all(phase_one_copy(stream, 0, True))
        start_all(phase_two_copy(stream, 0, 0, True))
    own.wait()
    for stream in range(streams):
        a0 = ORDERS[stream][0]
        for d0 in range(1, sizes[a0]):
            wait_in(stream, 0, d0 - 1, shifted(mine, a0, d0))
            start_all(phase_one_copy(stream, d0))
            start_all(phase_two_copy(stream, d0, 0))
    for stream in range(streams):
        a0, a1, _ = ORDERS[stream]
        n0, n1 = sizes[a0], sizes[a1]

        def forward(flat, carry, stream=stream, a0=a0, a1=a1, n1=n1):
            e0 = flat // (n1 - 1)
            d1 = flat % (n1 - 1) + 1
            wait_in(stream, 1, flat, shifted(shifted(mine, a0, e0), a1, d1))
            for copy in phase_two_copy(stream, e0, d1):
                copy.start()
            return carry

        lax.fori_loop(0, n0 * (n1 - 1), forward, 0)
    for stream in range(streams):
        a0, a1, a2 = ORDERS[stream]
        n0, n1, n2 = sizes[a0], sizes[a1], sizes[a2]

        def wait_plane(flat, carry, stream=stream, a0=a0, a1=a1, a2=a2, n1=n1, n2=n2):
            block = shifted(shifted(mine, a0, flat // n1), a1, flat % n1)
            for d2 in range(1, n2):
                wait_in(stream, 2, flat * (n2 - 1) + d2 - 1, shifted(block, a2, d2))
            return carry

        lax.fori_loop(0, n0 * n1, wait_plane, 0)
    for copy in sent:
        copy.wait_send()
    for stream in range(streams):
        a0, a1, _ = ORDERS[stream]
        n0, n1 = sizes[a0], sizes[a1]

        def drain(flat, carry, stream=stream, n1=n1):
            for copy in phase_two_copy(stream, flat // (n1 - 1), flat % (n1 - 1) + 1):
                copy.wait_send()
            return carry

        lax.fori_loop(0, n0 * (n1 - 1), drain, 0)

    chips, rows, width = out_ref.shape
    group = max(1, 128 // rows)

    def project(index, carry):
        held = out_ref[pl.ds(index * group, group)].reshape(group * rows, width)
        result_ref[pl.ds(index * group * rows, group * rows), :] = jnp.dot(
            held, weight_ref[...], preferred_element_type=jnp.float32
        )
        return carry

    lax.fori_loop(0, chips // group, project, 0)


def gather_and_project(block, weight, chips):
    side_len = round(chips ** (1.0 / 3.0))
    sizes = (side_len, side_len, side_len)
    rows, cols = block.shape
    tiles = cols // 128
    cuts = [0, (tiles + 2) // 3 * 128, (2 * tiles + 2) // 3 * 128, cols]
    slots = side_len * side_len * (side_len - 1)
    return pl.pallas_call(
        functools.partial(_gather_kernel, sizes, cuts, slots),
        out_shape=jax.ShapeDtypeStruct((chips * rows, weight.shape[1]), jnp.float32),
        in_specs=[pl.BlockSpec(memory_space=pltpu.VMEM), pl.BlockSpec(memory_space=pltpu.VMEM)],
        out_specs=pl.BlockSpec(memory_space=pltpu.VMEM),
        scratch_shapes=[
            pltpu.VMEM((chips, rows, cols), block.dtype),
            pltpu.SemaphoreType.DMA(()),
            pltpu.SemaphoreType.DMA((9 * slots,)),
            pltpu.SemaphoreType.DMA((9 * slots,)),
        ],
        compiler_params=pltpu.CompilerParams(
            collective_id=0, has_side_effects=True, vmem_limit_bytes=48 * 1024 * 1024
        ),
    )(block, weight)

def on_device(
    queries,
    latent_cache,
    lengths,
    value_lift,
    output_map,
    residual,
    norm_gain,
    expert_ids,
    gate_values,
    expert_in,
    expert_down,
):
    request_count = queries.shape[0]
    latent_width = value_lift.shape[1]
    half_heads = value_lift.shape[0]
    value_width = value_lift.shape[2]
    half_slots = latent_cache.shape[1]
    model_width = residual.shape[1]
    side_index = lax.axis_index("side")
    swap = [(0, 1), (1, 0)]
    score_scale = QKD ** (-0.5)
    scores = (
        jnp.einsum("rhc,rpc->rhp", queries, latent_cache, preferred_element_type=jnp.float32)
        * score_scale
    )
    positions = side_index * half_slots + jnp.arange(half_slots, dtype=jnp.int32)
    usable = (positions[None, :] < lengths[:, None])[:, None, :]
    masked = jnp.where(usable, scores, -1e30)
    swap = [(0, 1), (1, 0)]
    local_top = jnp.max(masked, axis=2)
    raised = jnp.where(usable, jnp.exp(masked - local_top[:, :, None]), 0.0)
    local_total = jnp.sum(raised, axis=2)
    probabilities = raised.astype(jnp.bfloat16)
    local_latent = jnp.einsum(
        "rhp,rpc->rhc",
        probabilities,
        latent_cache[:, :, :latent_width],
        preferred_element_type=jnp.float32,
    )
    other_index = 1 - side_index
    own_latent = lax.dynamic_slice_in_dim(local_latent, side_index * half_heads, half_heads, 1)
    own_total = lax.dynamic_slice_in_dim(local_total, side_index * half_heads, half_heads, 1)
    sent_latent = lax.dynamic_slice_in_dim(local_latent, other_index * half_heads, half_heads, 1)
    sent_total = lax.dynamic_slice_in_dim(local_total, other_index * half_heads, half_heads, 1)
    own_top = lax.dynamic_slice_in_dim(local_top, side_index * half_heads, half_heads, 1)
    sent_top = lax.dynamic_slice_in_dim(local_top, other_index * half_heads, half_heads, 1)
    got_latent, got_total, got_top = lax.ppermute(
        (sent_latent, sent_total, sent_top), "side", swap
    )
    row_top = jnp.maximum(own_top, got_top)
    own_weight = jnp.exp(own_top - row_top)
    got_weight = jnp.exp(got_top - row_top)
    row_total = own_weight * own_total + got_weight * got_total
    latent_sum = own_weight[:, :, None] * own_latent + got_weight[:, :, None] * got_latent
    own_heads = (latent_sum / row_total[:, :, None]).astype(jnp.bfloat16)
    head_values = jnp.einsum(
        "rhc,hcv->rhv", own_heads, value_lift, preferred_element_type=jnp.float32
    )
    head_values = head_values.astype(jnp.bfloat16).reshape(request_count, half_heads * value_width)
    held_in, held_down, head_values = lax.optimization_barrier((expert_in, expert_down, head_values))
    partner_in, partner_down = lax.ppermute((held_in, held_down), "side", swap)
    partial_columns = gather_and_project(head_values, output_map, lax.axis_size("dev"))
    partial_columns, partner_in, partner_down = lax.optimization_barrier(
        (partial_columns, partner_in, partner_down)
    )
    half_requests = partial_columns.shape[0] // 2
    kept_columns = lax.dynamic_slice_in_dim(partial_columns, side_index * half_requests, half_requests, 0)
    sent_columns = lax.dynamic_slice_in_dim(partial_columns, other_index * half_requests, half_requests, 0)
    got_columns = lax.ppermute(sent_columns.astype(jnp.bfloat16), "side", swap)
    summed_columns = kept_columns + got_columns.astype(jnp.float32)
    attention = lax.all_to_all(
        summed_columns.astype(jnp.bfloat16), "dev", split_axis=0, concat_axis=1, tiled=True
    ).astype(jnp.float32)
    gate_up_local = expert_in.reshape(model_width, -1)
    gate_up_partner = partner_in.reshape(model_width, -1)
    hidden = (residual.astype(jnp.float32) + attention).astype(jnp.bfloat16)
    hidden_wide = hidden.astype(jnp.float32)
    normed = hidden_wide * lax.rsqrt(
        jnp.mean(hidden_wide * hidden_wide, axis=1, keepdims=True) + 1e-06
    )
    normed = (normed * norm_gain.astype(jnp.float32)[None, :]).astype(jnp.bfloat16)
    token_count = expert_ids.shape[0]
    route_count = expert_ids.shape[1]
    experts = lax.axis_size("dev") // 2
    capacity = max(4, token_count * route_count // experts)
    flat_ids = expert_ids.reshape(-1)
    expert_hits = (flat_ids[:, None] == jnp.arange(experts, dtype=jnp.int32)[None, :]).astype(
        jnp.int32
    )
    before = jnp.cumsum(expert_hits, axis=0) - expert_hits
    slot_index = jnp.sum(before * expert_hits, axis=1).reshape(token_count, route_count)
    slot_code = expert_ids * capacity + slot_index
    slot_table = jnp.arange(experts * capacity, dtype=jnp.int32)
    slot_match = slot_code[None, :, :] == slot_table[:, None, None]
    dispatch_matrix = jnp.any(slot_match, axis=2).astype(jnp.bfloat16)
    combine_matrix = jnp.sum(jnp.where(slot_match, gate_values[None, :, :], 0.0), axis=2).T
    dispatch_cube = dispatch_matrix.reshape(experts, capacity, token_count)
    outgoing = jnp.einsum(
        "sct,td->csd", dispatch_cube, normed, preferred_element_type=jnp.float32
    ).astype(jnp.bfloat16)
    quarter_width = expert_in.shape[3]
    down_local = expert_down[0]
    chips = lax.axis_size("dev")
    spread = jnp.broadcast_to(outgoing[:, :, None], (capacity, experts, chips // experts, model_width))
    spread = spread.reshape(capacity, chips, model_width)
    arrivals = lax.all_to_all(spread, "dev", split_axis=1, concat_axis=1, tiled=True)
    flat_rows = arrivals.reshape(capacity * chips, model_width)

    def expert_part(gate_up_weights, down_weights):
        gate_up = jnp.dot(flat_rows, gate_up_weights, preferred_element_type=jnp.float32)
        activated = (
            jax.nn.silu(gate_up[:, :quarter_width]) * gate_up[:, quarter_width:]
        ).astype(jnp.bfloat16)
        return jnp.dot(activated, down_weights, preferred_element_type=jnp.float32)

    summed = (
        expert_part(gate_up_local, down_local) + expert_part(gate_up_partner, partner_down[0])
    ).astype(jnp.bfloat16).reshape(capacity, chips, model_width)
    returned = lax.all_to_all(summed, "dev", split_axis=1, concat_axis=1, tiled=True)
    halves = chips // experts
    combine_cube = jnp.broadcast_to(
        combine_matrix.reshape(token_count, 1, experts, 1, capacity),
        (token_count, capacity, experts, halves, capacity),
    )
    slot_eye = jnp.eye(capacity, dtype=jnp.float32)[None, :, None, None, :]
    combine_full = jnp.sum(combine_cube * slot_eye, axis=4).reshape(token_count, capacity, chips)
    routed_sum = jnp.einsum(
        "tcs,csd->td",
        combine_full.astype(jnp.bfloat16),
        returned,
        preferred_element_type=jnp.float32,
    )
    return (hidden.astype(jnp.float32) + routed_sum).astype(jnp.bfloat16)


def solution(mesh):
    in_specs = (
        P("dev", None, None),
        P("dev", "side", None),
        P("dev"),
        P("side", None, None),
        P("side", "dev"),
        P(("side", "dev"), None),
        P(),
        P(("side", "dev"), None),
        P(("side", "dev"), None),
        P("dev", None, None, "side"),
        P("dev", "side", None),
    )
    out_specs = P(("side", "dev"), None)
    return jax.shard_map(
        on_device, mesh=mesh, in_specs=in_specs, out_specs=out_specs, check_vma=False
    )
```

```python
import jax
import jax.numpy as jnp
from jax import lax
from jax.sharding import PartitionSpec as P

QKD = 192

import functools

from jax.experimental import pallas as pl
from jax.experimental.pallas import tpu as pltpu

MESH_ID = pl.DeviceIdType.MESH
ORDERS = ((2, 0, 1), (0, 1, 2), (1, 2, 0))


def _gather_kernel(
    sizes, col_cuts, slots, block_ref, weight_ref, result_ref, out_ref, own_sem, send_sems, recv_sems
):
    side = lax.axis_index("side")
    me = lax.axis_index("dev")
    count_y, count_z, count_x = sizes
    mine = (me // (count_z * count_x), (me // count_x) % count_z, me % count_x)

    def chip(coords):
        return (coords[0] * count_z + coords[1]) * count_x + coords[2]

    def shifted(base, axis, offset):
        coords = list(base)
        coords[axis] = (coords[axis] + offset) % sizes[axis]
        return tuple(coords)

    barrier = pltpu.get_barrier_semaphore()
    peers = 0
    for axis in range(3):
        for offset in range(1, sizes[axis]):
            pl.semaphore_signal(
                barrier, 1, device_id=(side, chip(shifted(mine, axis, offset))), device_id_type=MESH_ID
            )
            peers += 1
    pl.semaphore_wait(barrier, peers)

    own = pltpu.make_async_copy(block_ref, out_ref.at[me], own_sem)
    own.start()
    streams = len(col_cuts) - 1
    sent = []

    def sem_at(stream, phase, index):
        return (stream * 3 + phase) * slots + index

    def remote(stream, phase, index, block_coords, target, from_input=False):
        cols = pl.ds(col_cuts[stream], col_cuts[stream + 1] - col_cuts[stream])
        at = sem_at(stream, phase, index)
        if from_input:
            src = block_ref.at[:, cols]
        else:
            src = out_ref.at[chip(block_coords), :, cols]
        return pltpu.make_async_remote_copy(
            src_ref=src,
            dst_ref=out_ref.at[chip(block_coords), :, cols],
            send_sem=send_sems.at[at],
            recv_sem=recv_sems.at[at],
            device_id=(side, chip(target)),
            device_id_type=MESH_ID,
        )

    def wait_in(stream, phase, index, block_coords):
        remote(stream, phase, index, block_coords, mine).wait_recv()

    def phase_one_copy(stream, e0, from_input=False):
        a0, a1, _ = ORDERS[stream]
        n1 = sizes[a1]
        for step in range(1, n1):
            index = e0 * (n1 - 1) + (n1 - step) - 1
            yield remote(stream, 1, index, shifted(mine, a0, e0), shifted(mine, a1, step), from_input)

    def phase_two_copy(stream, e0, e1, from_input=False):
        a0, a1, a2 = ORDERS[stream]
        n1, n2 = sizes[a1], sizes[a2]
        block = shifted(shifted(mine, a0, e0), a1, e1)
        for step in range(1, n2):
            index = (e0 * n1 + e1) * (n2 - 1) + (n2 - step) - 1
            yield remote(stream, 2, index, block, shifted(mine, a2, step), from_input)

    def start_all(copies):
        for copy in copies:
            copy.start()
            sent.append(copy)

    for stream in range(streams):
        a0 = ORDERS[stream][0]
        n0 = sizes[a0]
        for step in range(1, n0):
            copy = remote(stream, 0, n0 - step - 1, mine, shifted(mine, a0, step), True)
            copy.start()
            sent.append(copy)
        start_all(phase_one_copy(stream, 0, True))
        start_all(phase_two_copy(stream, 0, 0, True))
    own.wait()
    for stream in range(streams):
        a0 = ORDERS[stream][0]
        for d0 in range(1, sizes[a0]):
            wait_in(stream, 0, d0 - 1, shifted(mine, a0, d0))
            start_all(phase_one_copy(stream, d0))
            start_all(phase_two_copy(stream, d0, 0))
    for stream in range(streams):
        a0, a1, _ = ORDERS[stream]
        n0, n1 = sizes[a0], sizes[a1]

        def forward(flat, carry, stream=stream, a0=a0, a1=a1, n1=n1):
            e0 = flat // (n1 - 1)
            d1 = flat % (n1 - 1) + 1
            wait_in(stream, 1, flat, shifted(shifted(mine, a0, e0), a1, d1))
            for copy in phase_two_copy(stream, e0, d1):
                copy.start()
            return carry

        lax.fori_loop(0, n0 * (n1 - 1), forward, 0)
    for stream in range(streams):
        a0, a1, a2 = ORDERS[stream]
        n0, n1, n2 = sizes[a0], sizes[a1], sizes[a2]

        def wait_plane(flat, carry, stream=stream, a0=a0, a1=a1, a2=a2, n1=n1, n2=n2):
            block = shifted(shifted(mine, a0, flat // n1), a1, flat % n1)
            for d2 in range(1, n2):
                wait_in(stream, 2, flat * (n2 - 1) + d2 - 1, shifted(block, a2, d2))
            return carry

        lax.fori_loop(0, n0 * n1, wait_plane, 0)
    for copy in sent:
        copy.wait_send()
    for stream in range(streams):
        a0, a1, _ = ORDERS[stream]
        n0, n1 = sizes[a0], sizes[a1]

        def drain(flat, carry, stream=stream, n1=n1):
            for copy in phase_two_copy(stream, flat // (n1 - 1), flat % (n1 - 1) + 1):
                copy.wait_send()
            return carry

        lax.fori_loop(0, n0 * (n1 - 1), drain, 0)

    chips, rows, width = out_ref.shape
    group = max(1, 128 // rows)

    def project(index, carry):
        held = out_ref[pl.ds(index * group, group)].reshape(group * rows, width)
        result_ref[pl.ds(index * group * rows, group * rows), :] = jnp.dot(
            held, weight_ref[...], preferred_element_type=jnp.float32
        )
        return carry

    lax.fori_loop(0, chips // group, project, 0)


def gather_and_project(block, weight, chips):
    side_len = round(chips ** (1.0 / 3.0))
    sizes = (side_len, side_len, side_len)
    rows, cols = block.shape
    tiles = cols // 128
    cuts = [0, (tiles + 2) // 3 * 128, (2 * tiles + 2) // 3 * 128, cols]
    slots = side_len * side_len * (side_len - 1)
    return pl.pallas_call(
        functools.partial(_gather_kernel, sizes, cuts, slots),
        out_shape=jax.ShapeDtypeStruct((chips * rows, weight.shape[1]), jnp.float32),
        in_specs=[pl.BlockSpec(memory_space=pltpu.VMEM), pl.BlockSpec(memory_space=pltpu.VMEM)],
        out_specs=pl.BlockSpec(memory_space=pltpu.VMEM),
        scratch_shapes=[
            pltpu.VMEM((chips, rows, cols), block.dtype),
            pltpu.SemaphoreType.DMA(()),
            pltpu.SemaphoreType.DMA((9 * slots,)),
            pltpu.SemaphoreType.DMA((9 * slots,)),
        ],
        compiler_params=pltpu.CompilerParams(
            collective_id=0, has_side_effects=True, vmem_limit_bytes=48 * 1024 * 1024
        ),
    )(block, weight)

def on_device(
    queries,
    latent_cache,
    lengths,
    value_lift,
    output_map,
    residual,
    norm_gain,
    expert_ids,
    gate_values,
    expert_in,
    expert_down,
):
    request_count = queries.shape[0]
    latent_width = value_lift.shape[1]
    half_heads = value_lift.shape[0]
    value_width = value_lift.shape[2]
    half_slots = latent_cache.shape[1]
    model_width = residual.shape[1]
    side_index = lax.axis_index("side")
    swap = [(0, 1), (1, 0)]
    score_scale = QKD ** (-0.5)
    scores = (
        jnp.einsum("rhc,rpc->rhp", queries, latent_cache, preferred_element_type=jnp.float32)
        * score_scale
    )
    positions = side_index * half_slots + jnp.arange(half_slots, dtype=jnp.int32)
    usable = (positions[None, :] < lengths[:, None])[:, None, :]
    masked = jnp.where(usable, scores, -1e30)
    swap = [(0, 1), (1, 0)]
    local_top = jnp.max(masked, axis=2)
    raised = jnp.where(usable, jnp.exp(masked - local_top[:, :, None]), 0.0)
    local_total = jnp.sum(raised, axis=2)
    probabilities = raised.astype(jnp.bfloat16)
    local_latent = jnp.einsum(
        "rhp,rpc->rhc",
        probabilities,
        latent_cache[:, :, :latent_width],
        preferred_element_type=jnp.float32,
    )
    other_index = 1 - side_index
    own_latent = lax.dynamic_slice_in_dim(local_latent, side_index * half_heads, half_heads, 1)
    own_total = lax.dynamic_slice_in_dim(local_total, side_index * half_heads, half_heads, 1)
    sent_latent = lax.dynamic_slice_in_dim(local_latent, other_index * half_heads, half_heads, 1)
    sent_total = lax.dynamic_slice_in_dim(local_total, other_index * half_heads, half_heads, 1)
    own_top = lax.dynamic_slice_in_dim(local_top, side_index * half_heads, half_heads, 1)
    sent_top = lax.dynamic_slice_in_dim(local_top, other_index * half_heads, half_heads, 1)
    got_latent, got_total, got_top = lax.ppermute(
        (sent_latent.astype(jnp.bfloat16), sent_total, sent_top), "side", swap
    )
    got_latent = got_latent.astype(jnp.float32)
    row_top = jnp.maximum(own_top, got_top)
    own_weight = jnp.exp(own_top - row_top)
    got_weight = jnp.exp(got_top - row_top)
    row_total = own_weight * own_total + got_weight * got_total
    latent_sum = own_weight[:, :, None] * own_latent + got_weight[:, :, None] * got_latent
    own_heads = (latent_sum / row_total[:, :, None]).astype(jnp.bfloat16)
    head_values = jnp.einsum(
        "rhc,hcv->rhv", own_heads, value_lift, preferred_element_type=jnp.float32
    )
    head_values = head_values.astype(jnp.bfloat16).reshape(request_count, half_heads * value_width)
    held_in, held_down, head_values = lax.optimization_barrier((expert_in, expert_down, head_values))
    partner_in, partner_down = lax.ppermute((held_in, held_down), "side", swap)
    partial_columns = gather_and_project(head_values, output_map, lax.axis_size("dev"))
    partial_columns, partner_in, partner_down = lax.optimization_barrier(
        (partial_columns, partner_in, partner_down)
    )
    half_requests = partial_columns.shape[0] // 2
    kept_columns = lax.dynamic_slice_in_dim(partial_columns, side_index * half_requests, half_requests, 0)
    sent_columns = lax.dynamic_slice_in_dim(partial_columns, other_index * half_requests, half_requests, 0)
    got_columns = lax.ppermute(sent_columns.astype(jnp.bfloat16), "side", swap)
    summed_columns = kept_columns + got_columns.astype(jnp.float32)
    attention = lax.all_to_all(
        summed_columns.astype(jnp.bfloat16), "dev", split_axis=0, concat_axis=1, tiled=True
    ).astype(jnp.float32)
    gate_up_local = expert_in.reshape(model_width, -1)
    gate_up_partner = partner_in.reshape(model_width, -1)
    hidden = (residual.astype(jnp.float32) + attention).astype(jnp.bfloat16)
    hidden_wide = hidden.astype(jnp.float32)
    normed = hidden_wide * lax.rsqrt(
        jnp.mean(hidden_wide * hidden_wide, axis=1, keepdims=True) + 1e-06
    )
    normed = (normed * norm_gain.astype(jnp.float32)[None, :]).astype(jnp.bfloat16)
    token_count = expert_ids.shape[0]
    route_count = expert_ids.shape[1]
    experts = lax.axis_size("dev") // 2
    capacity = max(4, token_count * route_count // experts)
    flat_ids = expert_ids.reshape(-1)
    expert_hits = (flat_ids[:, None] == jnp.arange(experts, dtype=jnp.int32)[None, :]).astype(
        jnp.int32
    )
    before = jnp.cumsum(expert_hits, axis=0) - expert_hits
    slot_index = jnp.sum(before * expert_hits, axis=1).reshape(token_count, route_count)
    slot_code = expert_ids * capacity + slot_index
    slot_table = jnp.arange(experts * capacity, dtype=jnp.int32)
    slot_match = slot_code[None, :, :] == slot_table[:, None, None]
    dispatch_matrix = jnp.any(slot_match, axis=2).astype(jnp.bfloat16)
    combine_matrix = jnp.sum(jnp.where(slot_match, gate_values[None, :, :], 0.0), axis=2).T
    dispatch_cube = dispatch_matrix.reshape(experts, capacity, token_count)
    outgoing = jnp.einsum(
        "sct,td->csd", dispatch_cube, normed, preferred_element_type=jnp.float32
    ).astype(jnp.bfloat16)
    quarter_width = expert_in.shape[3]
    down_local = expert_down[0]
    chips = lax.axis_size("dev")
    spread = jnp.broadcast_to(outgoing[:, :, None], (capacity, experts, chips // experts, model_width))
    spread = spread.reshape(capacity, chips, model_width)
    arrivals = lax.all_to_all(spread, "dev", split_axis=1, concat_axis=1, tiled=True)
    flat_rows = arrivals.reshape(capacity * chips, model_width)

    def expert_part(gate_up_weights, down_weights):
        gate_up = jnp.dot(flat_rows, gate_up_weights, preferred_element_type=jnp.float32)
        activated = (
            jax.nn.silu(gate_up[:, :quarter_width]) * gate_up[:, quarter_width:]
        ).astype(jnp.bfloat16)
        return jnp.dot(activated, down_weights, preferred_element_type=jnp.float32)

    summed = (
        expert_part(gate_up_local, down_local) + expert_part(gate_up_partner, partner_down[0])
    ).astype(jnp.bfloat16).reshape(capacity, chips, model_width)
    returned = lax.all_to_all(summed, "dev", split_axis=1, concat_axis=1, tiled=True)
    halves = chips // experts
    combine_cube = jnp.broadcast_to(
        combine_matrix.reshape(token_count, 1, experts, 1, capacity),
        (token_count, capacity, experts, halves, capacity),
    )
    slot_eye = jnp.eye(capacity, dtype=jnp.float32)[None, :, None, None, :]
    combine_full = jnp.sum(combine_cube * slot_eye, axis=4).reshape(token_count, capacity, chips)
    routed_sum = jnp.einsum(
        "tcs,csd->td",
        combine_full.astype(jnp.bfloat16),
        returned,
        preferred_element_type=jnp.float32,
    )
    return (hidden.astype(jnp.float32) + routed_sum).astype(jnp.bfloat16)


def solution(mesh):
    in_specs = (
        P("dev", None, None),
        P("dev", "side", None),
        P("dev"),
        P("side", None, None),
        P("side", "dev"),
        P(("side", "dev"), None),
        P(),
        P(("side", "dev"), None),
        P(("side", "dev"), None),
        P("dev", None, None, "side"),
        P("dev", "side", None),
    )
    out_specs = P(("side", "dev"), None)
    return jax.shard_map(
        on_device, mesh=mesh, in_specs=in_specs, out_specs=out_specs, check_vma=False
    )
```
